32 devices in a mesh: gx: 4 (over z), gy: 8 (over y, x, core).
Axes of the slice: x: 2, y: 2, z: 4, core: 2. Of those that a mesh axis runs over, the one named last changes fastest.
Arguments:
- start_block: float32 [4, 8, 128, 16, 128], P('gx', 'gy'), may hold values from -6 to 6
- slot_tiles: float32 [8, 128, 128], replicated, may hold values from -0.1875 to 0.1875
- edge_weights: float32 [4, 8, 128, 8], P('gx', 'gy'), may hold values from 0.3 to 3
- block_columns: int32 [4, 8, 128, 8], P('gx', 'gy'), may hold values from 0 to 159
- halo_sends: int32 [4, 8, 4, 8], P('gx', 'gy'), may hold values from 0 to 127
- split_side: int32 [4, 8, 128], P('gx', 'gy'), may hold values from 0 to 1, as said below
Outputs:
- moved_basis: float32 [4, 8, 128, 16, 128], P('gx', 'gy')
- moved_weights: float32 [4, 8, 128, 8], P('gx', 'gy')
- moved_columns: int32 [4, 8, 128, 8], P('gx', 'gy')
- rayleigh: float32 [16, 16], replicated
The draws below stay inside these ranges and needn't reach their ends.
Inputs may be any that keep to these rules, and one draw needn't show every extreme that they name: `split_side`: over each pair of partners exactly 128 block rows have each side; some subdomain gives all 128 of its block rows to its partner.
All inputs are finite; a program needn't handle non-finite values.
Results may differ from the reference program's by a relative error of at most 0.0003.
Values sent between devices are 32-bit elements; how exact they have to be, the bound alone decides.
No kernel may reach another device: no remote copies, remote signals or barrier semaphores. Data moves between devices by JAX's collectives and lax.ppermute only.
A program may use at most 64 MiB of HBM per device.

```python
import math
import jax
import jax.numpy as jnp
from jax import lax

COLS = 16
BS = 128
K = 8
NB = 128
HB = 8
STEPS = 3
GX = 4
GY = 8
N_GX = 4
N_GY = 8


def draw_split_side(key, part):
    half_axis = N_GY // 2
    key_moved, key_row, key_col, key_perm = jax.random.split(jax.random.fold_in(key, 7), 4)
    moved = jax.random.randint(key_moved, (N_GX, half_axis), 0, NB + 1)
    row_pick = jax.random.randint(key_row, (), 0, N_GX)
    col_pick = jax.random.randint(key_col, (), 0, half_axis)
    moved = moved.at[row_pick, col_pick].set(NB)
    moved_all = jnp.concatenate([moved, moved], 1)
    keys = jax.random.split(key_perm, N_GX * N_GY)
    perms = jax.vmap(lambda single: jax.random.permutation(single, NB))(keys).reshape(N_GX, N_GY, NB)
    goes = (perms < moved_all[:, :, None]).astype(jnp.int32)
    upper = (jnp.arange(N_GY) >= half_axis).astype(jnp.int32)[None, :, None]
    return jnp.where(upper == 1, 1 - goes, goes).astype(jnp.int32)


def plant(values, stream_key, low, high):
    index_at = [jax.random.randint(jax.random.fold_in(stream_key, axis), (), 0, length) for axis, length in enumerate(values.shape)]
    widest = values.shape.index(max(values.shape))
    neighbour = index_at[:widest] + [(index_at[widest] + 1) % values.shape[widest]] + index_at[widest + 1:]
    return values.at[tuple(index_at)].set(low).at[tuple(neighbour)].set(high)


def levels(own_key, extent, cuts, low, largest):
    def one(position, shards_of):
        steps = jax.random.uniform(jax.random.fold_in(jax.random.fold_in(own_key, 6), position), (shards_of,), jnp.float32, low / len(cuts), largest / len(cuts))
        return jnp.repeat(jnp.exp(steps), extent[position] // shards_of).reshape((-1,) + (1,) * (len(extent) - position - 1))

    level = one(*cuts[0])
    for cut in cuts[1:]:
        level = level * one(*cut)
    return level


def centred(key, shape, deviation, bound, cuts=(), kind=jnp.bfloat16):
    values = jax.random.normal(key, shape, jnp.float32) * deviation
    if len(cuts) > 0:
        values = levels(key, shape, cuts, -0.22, 0.18) * values
    return jnp.clip(values, min=-bound, max=bound).astype(kind)


def setup_inputs(seed: int = 0) -> dict:
    arg_keys = jax.random.split(jax.random.key(seed), 7)
    start_block = centred(arg_keys[0], (GX, GY, NB, COLS, BS), 1.0, 6.0, ((0, 4), (1, 8)), jnp.float32)
    slot_tiles = centred(arg_keys[1], (K, BS, BS), (K * BS) ** -0.5, 0.1875, (), jnp.float32)
    edge_weights = jnp.clip(jnp.exp(math.log(3.0) - 2.3025851 * jax.random.uniform(arg_keys[2], (GX, GY, NB, K), jnp.float32) ** levels(arg_keys[2], (GX, GY, NB, K), ((0, 4), (1, 8)), -0.2, 0.2)), 0.3, 3.0)
    block_columns = plant(jax.random.randint(arg_keys[3], (GX, GY, NB, K), 0, NB + 4 * HB), jax.random.fold_in(arg_keys[3], 1), 0, (NB + 4 * HB) - 1).astype(jnp.int32)
    halo_sends = plant(jax.random.randint(arg_keys[4], (GX, GY, 4, HB), 0, NB), jax.random.fold_in(arg_keys[4], 1), 0, NB - 1).astype(jnp.int32)
    split_side = draw_split_side(jax.random.fold_in(arg_keys[6], 71), 0)
    return {"start_block": start_block, "slot_tiles": slot_tiles, "edge_weights": edge_weights, "block_columns": block_columns, "halo_sends": halo_sends, "split_side": split_side}


def factor(gram):
    lower = jnp.linalg.cholesky(gram)
    ident = jnp.eye(gram.shape[0], dtype=gram.dtype)
    return jax.scipy.linalg.solve_triangular(lower, ident, lower=True).T

def local_product(full_dev, cols_dev, weight_dev, slot_tiles):
    picked = full_dev[cols_dev] * weight_dev[:, :, None, None]
    return jnp.einsum('bkcs,kst->bct', picked, slot_tiles, precision=lax.Precision.HIGHEST)

def apply_operator(block, slot_tiles, edge_weights, block_columns, halo_sends):
    sent = jax.vmap(jax.vmap(lambda v, s: v[s]))(block, halo_sends)
    zero_row = jnp.zeros_like(sent[:1, :, 0])
    zero_col = jnp.zeros_like(sent[:, :1, 0])
    from_low = jnp.concatenate([zero_row, sent[:-1, :, 1]], 0)
    from_high = jnp.concatenate([sent[1:, :, 0], zero_row], 0)
    from_left = jnp.concatenate([zero_col, sent[:, :-1, 3]], 1)
    from_right = jnp.concatenate([sent[:, 1:, 2], zero_col], 1)
    full = jnp.concatenate([block, from_low, from_high, from_left, from_right], 2)
    shape_full = full.shape
    flat_full = full.reshape((-1,) + shape_full[2:])
    flat_cols = block_columns.reshape((-1,) + block_columns.shape[2:])
    flat_weight = edge_weights.reshape((-1,) + edge_weights.shape[2:])
    result = lax.map(lambda item: local_product(item[0], item[1], item[2], slot_tiles), (flat_full, flat_cols, flat_weight))
    return result.reshape(block.shape)

def compose(own_items, recv_items, own_side, recv_side, my_side):
    capacity = own_side.shape[0]
    keep_own = (own_side == my_side).astype(jnp.int32)
    keep_recv = (recv_side == my_side).astype(jnp.int32)
    kept_count = jnp.sum(keep_own)
    pos_own = jnp.where(keep_own == 1, jnp.cumsum(keep_own) - 1, capacity).astype(jnp.int32)
    pos_recv = jnp.where(keep_recv == 1, kept_count + jnp.cumsum(keep_recv) - 1, capacity).astype(jnp.int32)
    outputs = []
    for own_rows, recv_rows in zip(own_items, recv_items):
        placed = jnp.zeros_like(own_rows).at[pos_own].set(own_rows, mode='drop')
        placed = placed.at[pos_recv].set(recv_rows, mode='drop')
        outputs.append(placed)
    return tuple(outputs)

def reference(start_block, slot_tiles, edge_weights, block_columns, halo_sends, split_side):
    basis = start_block
    cross = jnp.zeros((COLS, COLS), jnp.float32)
    for step in range(STEPS):
        image = apply_operator(basis, slot_tiles, edge_weights, block_columns, halo_sends)
        gram = jnp.einsum('ijbcs,ijbds->cd', image, image, precision=lax.Precision.HIGHEST)
        cross = jnp.einsum('ijbcs,ijbds->cd', basis, image, precision=lax.Precision.HIGHEST)
        scale = factor(gram)
        basis = jnp.einsum('ijbcs,cd->ijbds', image, scale, precision=lax.Precision.HIGHEST)
    half_axis = N_GY // 2
    my_side = jnp.broadcast_to((jnp.arange(N_GY) >= half_axis).astype(jnp.int32)[None, :], (N_GX, N_GY))

    def partner(arr):
        return jnp.concatenate([arr[:, half_axis:], arr[:, :half_axis]], 1)
    own_items = (basis, edge_weights, block_columns)
    recv_items = (partner(basis), partner(edge_weights), partner(block_columns))
    moved = jax.vmap(jax.vmap(compose))(own_items, recv_items, split_side, partner(split_side), my_side)
    return (moved[0], moved[1], moved[2], cross)
```

```python
import functools

import jax
import jax.numpy as jnp
from jax import lax
from jax.experimental import pallas as pl
from jax.experimental.pallas import tpu as pltpu
from jax.sharding import PartitionSpec as P

F32 = jnp.float32
BF16 = jnp.bfloat16
AXES = ("gx", "gy")
CHUNKS = 4
VMEM = pl.BlockSpec(memory_space=pltpu.VMEM)
SMEM = pl.BlockSpec(memory_space=pltpu.SMEM)
ANY = pl.BlockSpec(memory_space=pl.ANY)
VMEM_LIMIT = 40 << 20


def split(x):
    high = x.astype(BF16)
    return high, (x - high.astype(F32)).astype(BF16)


def lane_group(rows, cols):
    return lax.broadcasted_iota(jnp.int32, (rows, 128), 1) // cols


def spread(x, cols):
    width = 64
    while width >= cols:
        x = x + pltpu.roll(x, width, 1)
        width //= 2
    return x


def unpack(packed, cols):
    half = 128 // cols
    sub = lax.broadcasted_iota(jnp.int32, (half, 128), 0)
    own = lane_group(half, cols) == sub
    parts = []
    for start in range(0, cols, half):
        row = packed[:, start * cols : start * cols + 128]
        parts.append(spread(jnp.where(own, jnp.broadcast_to(row, (half, 128)), 0.0), cols))
    return jnp.concatenate(parts, 0)


def pack(tiled, cols):
    half = 128 // cols
    sub = lax.broadcasted_iota(jnp.int32, (half, 128), 0)
    own = lane_group(half, cols) == sub
    rows = []
    for start in range(0, cols, half):
        part = jnp.where(own, tiled[start : start + half], 0.0)
        rows.append(jnp.sum(part, 0, keepdims=True))
    return jnp.concatenate(rows, 1)


def identity(cols):
    lane = lax.broadcasted_iota(jnp.int32, (cols, 128), 1) % cols
    return (lane == lax.broadcasted_iota(jnp.int32, (cols, 128), 0)).astype(F32)


def eliminate(gram, right):
    cols = gram.shape[0]
    row = lax.broadcasted_iota(jnp.int32, (cols, 128), 0)
    for j in range(cols):
        inv = lax.rsqrt(gram[j : j + 1, j : j + 1])
        factor = gram[:, j : j + 1] * inv
        gram_row = gram[j : j + 1, :] * inv
        right_row = right[j : j + 1, :] * inv
        below = row > j
        gram = jnp.where(below, gram - factor * gram_row, gram)
        right = jnp.where(
            below, right - factor * right_row, jnp.where(row == j, right_row, right)
        )
    return right


def scaler(small):
    cols = small.shape[0]
    group = lane_group(cols, cols)
    diag = jnp.concatenate(
        [jnp.where(group == g, small, 0.0) for g in range(128 // cols)], 0
    )
    high, low = split(diag)
    return jnp.concatenate(
        [jnp.concatenate([high, high], 1), jnp.concatenate([low, low], 1)], 0
    )


def apply_scaler(left, x):
    high, low = split(x)
    both = jnp.dot(left, jnp.concatenate([high, low], 0), preferred_element_type=F32)
    return both[:128] + both[128:]


def stacked(groups):
    pairs = [split(x) for x in groups]
    return jnp.concatenate(
        [
            jnp.concatenate([p[0] for p in pairs], 1),
            jnp.concatenate([p[1] for p in pairs], 1),
        ],
        0,
    )


def inner(a, b, cols):
    full = lax.dot_general(a, b, (((1,), (1,)), ((), ())), preferred_element_type=F32)
    half = full[:128] + full[128:]
    square = half[:, :128] + half[:, 128:]
    group = lane_group(cols, cols)
    total = jnp.zeros((cols, 128), F32)
    for g in range(128 // cols):
        total = total + jnp.where(group == g, square[g * cols : (g + 1) * cols], 0.0)
    return spread(total, cols)


def read_group(ref, g, per):
    x = ref[g * per : (g + 1) * per]
    return x.reshape(128, 128)


def first_sends_kernel(sends, block, *rest):
    outs, sems = rest[:4], rest[4]
    count = outs[0].shape[0]
    copies = []
    for d in range(4):
        for h in range(count):
            copies.append(
                pltpu.make_async_copy(
                    block.at[sends[d, h]], outs[d].at[h], sems.at[d, h]
                )
            )
    for copy in copies:
        copy.start()
    for copy in copies:
        copy.wait()


def tiles_kernel(tiles, high_out, low_out):
    for pair in range(tiles.shape[0] // 2):
        for j in range(2):
            high, low = split(tiles[2 * pair + j])
            for half in range(2):
                rows = slice(128 * half, 128 * half + 128)
                high_out[pair, rows, 128 * j : 128 * j + 128] = high
                low_out[pair, rows, 128 * j : 128 * j + 128] = low


def products(z, x, tiles_high, tiles_low, blocks, cols):
    step = 32
    pairs = tiles_high.shape[0]

    @pl.loop(0, blocks // step)
    def _(i):
        first = pl.multiple_of(i * step, step)
        left = x[pl.ds(pl.multiple_of(i * step * cols, step * cols), step * cols), :]
        for pair in range(pairs):
            out = jnp.dot(left, tiles_high[pair], preferred_element_type=F32)
            out = out + jnp.dot(left, tiles_low[pair], preferred_element_type=F32)
            for j in range(2):
                z[2 * pair + j, pl.ds(first, step)] = out[:, 128 * j : 128 * j + 128].reshape(
                    step, cols, 128
                )


def load_blocks(x, block, halos, flags):
    count, cols, cells = block.shape

    def put(start, values):
        high, low = split(values)
        x[start : start + values.shape[0], :cells] = high
        x[start : start + values.shape[0], cells:] = low

    put(0, block[...].reshape(count * cols, cells))
    start = count * cols
    for d, halo in enumerate(halos):
        rows = halo.shape[0] * cols
        values = jnp.where(flags[d] != 0, halo[...].reshape(rows, cells), 0.0)
        put(start, values)
        start += rows


def combine(z, weights, columns, b, slots):
    total = weights[b * slots] * z[0, columns[b * slots]]
    for k in range(1, slots):
        total = total + weights[b * slots + k] * z[k, columns[b * slots + k]]
    return total


def step_kernel(scaled, flags, columns, weights, sends, block, h0, h1, h2, h3, th, tl, *rest):
    if scaled:
        sums, rest = rest[0], rest[1:]
    image, s0, s1, s2, s3, packed, x, z = rest
    count, cols, cells = block.shape
    slots = z.shape[0]
    load_blocks(x, block, (h0, h1, h2, h3), flags)
    products(z, x, th, tl, z.shape[1], cols)

    @pl.loop(0, count, unroll=4)
    def _(b):
        image[b] = combine(z, weights, columns, b, slots)

    per = 128 // cols
    groups = [read_group(image, g, per) for g in range(count // per)]
    if scaled:
        total = jnp.sum(sums[...], 0, keepdims=True)
        left = scaler(eliminate(unpack(total, cols), identity(cols)))
        groups = [apply_scaler(left, g) for g in groups]
        for g, value in enumerate(groups):
            image[g * per : (g + 1) * per] = value.reshape(per, cols, cells)
    both = stacked(groups)
    gram = pack(inner(both, both, cols), cols)
    packed[...] = jnp.broadcast_to(gram, packed.shape)
    for d, out in enumerate((s0, s1, s2, s3)):
        for h in range(out.shape[0]):
            out[h] = image[sends[d, h]]


def last_kernel(flags, columns, weights, order, block, h0, h1, h2, h3, th, tl, *rest):
    image, chunks, x, z = rest[0], rest[1:-2], rest[-2], rest[-1]
    count, cols, cells = block.shape
    slots = z.shape[0]
    load_blocks(x, block, (h0, h1, h2, h3), flags)
    products(z, x, th, tl, z.shape[1], cols)
    size = count // len(chunks)
    for i, chunk in enumerate(chunks):

        @pl.loop(0, size, unroll=4)
        def _(r):
            b = order[i * size + r]
            value = combine(z, weights, columns, b, slots)
            image[b] = value
            chunk[r] = value


def sums_kernel(sums, previous, image, packed, inverse):
    count, cols, cells = image.shape
    per = 128 // cols
    total = jnp.sum(sums[...], 0, keepdims=True)
    inv = eliminate(unpack(total, cols), identity(cols))
    inverse[...] = inv
    left = scaler(inv)
    now = stacked([apply_scaler(left, read_group(image, g, per)) for g in range(count // per)])
    before = stacked(
        [apply_scaler(left, read_group(previous, g, per)) for g in range(count // per)]
    )
    gram = pack(inner(now, now, cols), cols)
    cross = pack(inner(before, now, cols), cols)
    packed[...] = jnp.broadcast_to(jnp.concatenate([gram, cross], 1), packed.shape)


def final_kernel(given, sums, inverse, *rest):
    half = (len(rest) - 3) // 2
    mine, theirs = rest[:half], rest[half : 2 * half]
    out, rayleigh, rows = rest[2 * half :]
    size, cols, cells = mine[0].shape
    for i in range(half):
        rows[i * size : (i + 1) * size] = mine[i][...]
        rows[(half + i) * size : (half + i + 1) * size] = theirs[i][...]
    total = jnp.sum(sums[...], 0, keepdims=True)
    wide = cols * cols
    inv = eliminate(unpack(total[:, :wide], cols), inverse[...])
    rayleigh[...] = unpack(total[:, wide:], cols)[:, :cols]
    left = scaler(inv)
    per = 128 // cols
    for g in range(out.shape[0] // per):
        value = rows[pl.ds(given[0] + g * per, per)].reshape(128, cells)
        out[g * per : (g + 1) * per] = apply_scaler(left, value).reshape(per, cols, cells)


def call(kernel, out_shape, in_specs, out_specs, scratch=(), flops=0, moved=0):
    return pl.pallas_call(
        kernel,
        out_shape=out_shape,
        in_specs=in_specs,
        out_specs=out_specs,
        scratch_shapes=list(scratch),
        compiler_params=pltpu.CompilerParams(vmem_limit_bytes=VMEM_LIMIT),
        cost_estimate=pl.CostEstimate(flops=flops, transcendentals=0, bytes_accessed=moved),
    )


def ring(x, axis, shift):
    size = lax.axis_size(axis)
    return lax.ppermute(x, axis, [(i, (i + shift) % size) for i in range(size)])


def halo(sent):
    return (
        ring(sent[1], "gx", 1),
        ring(sent[0], "gx", -1),
        ring(sent[3], "gy", 1),
        ring(sent[2], "gy", -1),
    )


def everywhere(rows):
    return lax.all_to_all(rows, AXES, 0, 0, tiled=True)


def shape(*dims, dtype=F32):
    return jax.ShapeDtypeStruct(dims, dtype)


def per_device(start_block, slot_tiles, edge_weights, block_columns, halo_sends, split_side):
    block = start_block[0, 0]
    weights, columns, sends, sides = (
        edge_weights[0, 0],
        block_columns[0, 0],
        halo_sends[0, 0],
        split_side[0, 0],
    )
    count, cols, cells = block.shape
    slots, width = slot_tiles.shape[0], sends.shape[1]
    size_x, size_y = lax.axis_size("gx"), lax.axis_size("gy")
    devices = size_x * size_y
    place_x, place_y = lax.axis_index("gx"), lax.axis_index("gy")
    flags = jnp.stack(
        [place_x > 0, place_x < size_x - 1, place_y > 0, place_y < size_y - 1]
    ).astype(jnp.int32)
    flat_weights = weights.reshape(count * slots)
    flat_columns = columns.reshape(count * slots)

    my_side = (place_y >= size_y // 2).astype(jnp.int32)
    keep = (sides == my_side).astype(jnp.int32)
    given = count - jnp.sum(keep)
    place = jnp.where(keep == 1, given + jnp.cumsum(keep) - 1, jnp.cumsum(1 - keep) - 1)
    order = jnp.zeros((count,), jnp.int32).at[place].set(
        jnp.arange(count, dtype=jnp.int32), unique_indices=True
    )

    piece = shape(width, cols, cells)
    sent = call(
        first_sends_kernel,
        [piece] * 4,
        [SMEM, ANY],
        [VMEM] * 4,
        [pltpu.SemaphoreType.DMA((4, width))],
    )(sends, block)
    wide = 2 * cells
    tiles = call(
        tiles_kernel, [shape(slots // 2, wide, wide, dtype=BF16)] * 2, [VMEM], [VMEM] * 2
    )(slot_tiles)

    blocks = count + 4 * width
    scratch = [
        pltpu.VMEM((blocks * cols, wide), BF16),
        pltpu.VMEM((slots, blocks, cols, cells), F32),
    ]

    def step(block, near, sums):
        extra = () if sums is None else (sums,)
        out = call(
            functools.partial(step_kernel, sums is not None),
            [shape(count, cols, cells)] + [piece] * 4 + [shape(devices, cols * cols)],
            [SMEM] * 4 + [VMEM] * (7 + len(extra)),
            [VMEM] * 6,
            scratch,
        )(flags, flat_columns, flat_weights, sends, block, *near, *tiles, *extra)
        return out[0], out[1:5], out[5]

    image, sent, packed = step(block, halo(sent), None)
    near = halo(sent)
    image, sent, packed = step(image, near, everywhere(packed))
    previous = image
    near = halo(sent)
    size = count // CHUNKS
    image, *mine = call(
        last_kernel,
        [shape(count, cols, cells)] + [shape(size, cols, cells)] * CHUNKS,
        [SMEM] * 4 + [VMEM] * 7,
        [VMEM] * (1 + CHUNKS),
        scratch,
    )(flags, flat_columns, flat_weights, order, image, *near, *tiles)

    swap = [(j, j ^ (size_y // 2)) for j in range(size_y)]
    theirs = [lax.ppermute(x, "gy", swap) for x in mine]
    packed, image = lax.optimization_barrier((packed, image))
    packed, inverse = call(
        sums_kernel,
        [shape(devices, 2 * cols * cols), shape(cols, cells)],
        [VMEM] * 3,
        [VMEM] * 2,
    )(everywhere(packed), previous, image)
    sums = everywhere(packed)

    meta = jnp.concatenate([weights, columns.astype(F32)], 1)[order]
    both = jnp.concatenate([meta, lax.ppermute(meta, "gy", swap)], 0)
    moved = lax.dynamic_slice(both, (given, 0), (count, 2 * slots))
    moved_weights = moved[:, :slots]
    moved_columns = moved[:, slots:].astype(jnp.int32)

    moved_basis, rayleigh = call(
        final_kernel,
        [shape(count, cols, cells), shape(cols, cols)],
        [SMEM] + [VMEM] * (2 + 2 * CHUNKS),
        [VMEM] * 2,
        [pltpu.VMEM((2 * count, cols, cells), F32)],
    )(given.reshape(1), sums, inverse, *mine, *theirs)
    return (
        moved_basis[None, None],
        moved_weights[None, None],
        moved_columns[None, None],
        rayleigh,
    )


def solution(mesh):
    return jax.shard_map(
        per_device,
        mesh=mesh,
        in_specs=(
            P("gx", "gy", None, None, None),
            P(),
            P("gx", "gy", None, None),
            P("gx", "gy", None, None),
            P("gx", "gy", None, None),
            P("gx", "gy", None),
        ),
        out_specs=(
            P("gx", "gy", None, None, None),
            P("gx", "gy", None, None),
            P("gx", "gy", None, None),
            P(),
        ),
        check_vma=False,
    )
```

```python
import functools

import jax
import jax.numpy as jnp
from jax import lax
from jax.experimental import pallas as pl
from jax.experimental.pallas import tpu as pltpu
from jax.sharding import PartitionSpec as P

F32 = jnp.float32
BF16 = jnp.bfloat16
AXES = ("gx", "gy")
CHUNKS = 4
VMEM = pl.BlockSpec(memory_space=pltpu.VMEM)
SMEM = pl.BlockSpec(memory_space=pltpu.SMEM)
ANY = pl.BlockSpec(memory_space=pl.ANY)
HBM = pl.BlockSpec(memory_space=pltpu.HBM)


def split(x):
    high = x.astype(BF16)
    return high, (x - high.astype(F32)).astype(BF16)


def lane_group(rows, cols):
    return lax.broadcasted_iota(jnp.int32, (rows, 128), 1) // cols


def spread(x, cols):
    width = 64
    while width >= cols:
        x = x + pltpu.roll(x, width, 1)
        width //= 2
    return x


def unpack(packed, cols):
    half = 128 // cols
    sub = lax.broadcasted_iota(jnp.int32, (half, 128), 0)
    own = lane_group(half, cols) == sub
    parts = []
    for start in range(0, cols, half):
        row = packed[:, start * cols : start * cols + 128]
        parts.append(spread(jnp.where(own, jnp.broadcast_to(row, (half, 128)), 0.0), cols))
    return jnp.concatenate(parts, 0)


def pack(tiled, cols):
    half = 128 // cols
    sub = lax.broadcasted_iota(jnp.int32, (half, 128), 0)
    own = lane_group(half, cols) == sub
    rows = []
    for start in range(0, cols, half):
        part = jnp.where(own, tiled[start : start + half], 0.0)
        rows.append(jnp.sum(part, 0, keepdims=True))
    return jnp.concatenate(rows, 1)


def identity(cols):
    lane = lax.broadcasted_iota(jnp.int32, (cols, 128), 1) % cols
    return (lane == lax.broadcasted_iota(jnp.int32, (cols, 128), 0)).astype(F32)


def eliminate(gram, right):
    cols = gram.shape[0]
    row = lax.broadcasted_iota(jnp.int32, (cols, 128), 0)
    for j in range(cols):
        inv = lax.rsqrt(gram[j : j + 1, j : j + 1])
        factor = gram[:, j : j + 1] * inv
        gram_row = gram[j : j + 1, :] * inv
        right_row = right[j : j + 1, :] * inv
        below = row > j
        gram = jnp.where(below, gram - factor * gram_row, gram)
        right = jnp.where(
            below, right - factor * right_row, jnp.where(row == j, right_row, right)
        )
    return right


def scaler(small):
    cols = small.shape[0]
    group = lane_group(cols, cols)
    diag = jnp.concatenate(
        [jnp.where(group == g, small, 0.0) for g in range(128 // cols)], 0
    )
    high, low = split(diag)
    return jnp.concatenate(
        [jnp.concatenate([high, high], 1), jnp.concatenate([low, low], 1)], 0
    )


def apply_scaler(left, x):
    high, low = split(x)
    both = jnp.dot(left, jnp.concatenate([high, low], 0), preferred_element_type=F32)
    return both[:128] + both[128:]


def stacked(groups):
    pairs = [split(x) for x in groups]
    return jnp.concatenate(
        [
            jnp.concatenate([p[0] for p in pairs], 1),
            jnp.concatenate([p[1] for p in pairs], 1),
        ],
        0,
    )


def inner(a, b, cols):
    full = lax.dot_general(a, b, (((1,), (1,)), ((), ())), preferred_element_type=F32)
    half = full[:128] + full[128:]
    square = half[:, :128] + half[:, 128:]
    group = lane_group(cols, cols)
    total = jnp.zeros((cols, 128), F32)
    for g in range(128 // cols):
        total = total + jnp.where(group == g, square[g * cols : (g + 1) * cols], 0.0)
    return spread(total, cols)


def read_group(ref, g, per):
    x = ref[g * per : (g + 1) * per]
    return x.reshape(128, 128)


def first_sends_kernel(plan, sends, block, *rest):
    outs, sems = rest[:-1], rest[-1]
    copies = []
    for n, out in enumerate(outs):
        for h in range(out.shape[0]):
            copies.append(
                pltpu.make_async_copy(block.at[sends[plan[n], h]], out.at[h], sems.at[n, h])
            )
    for copy in copies:
        copy.start()
    for copy in copies:
        copy.wait()


def tiles_kernel(tiles, high_out, low_out):
    for pair in range(tiles.shape[0] // 2):
        for j in range(2):
            high, low = split(tiles[2 * pair + j])
            for half in range(2):
                rows = slice(128 * half, 128 * half + 128)
                high_out[pair, rows, 128 * j : 128 * j + 128] = high
                low_out[pair, rows, 128 * j : 128 * j + 128] = low


def lanes_product(a, b):
    return lax.dot_general(
        a.astype(BF16), b.astype(BF16), (((1,), (1,)), ((), ())), preferred_element_type=F32
    )


def order_kernel(side, sides, weights, columns, order, meta):
    count, slots = sides.shape[1], weights.shape[0]
    row = lax.broadcasted_iota(jnp.int32, (count, count), 0)
    col = lax.broadcasted_iota(jnp.int32, (count, count), 1)
    keep = jnp.broadcast_to((sides[...] == side[0]).astype(F32), (8, count))
    kept = lanes_product(keep, (col <= row).astype(F32))
    given = count - jnp.sum(keep, 1, keepdims=True)
    lane = lax.broadcasted_iota(jnp.int32, (8, count), 1).astype(F32)
    place = jnp.where(keep > 0.5, given + kept - 1.0, lane - kept)
    pick = (place[:1].astype(jnp.int32) == row).astype(F32)
    moved = lanes_product(lane, pick)
    order[...] = jnp.where(
        lax.broadcasted_iota(jnp.int32, (8, count), 0) == 0, moved, given
    ).astype(jnp.int32)
    values = weights[...]
    total = jnp.zeros((slots, count), F32)
    for _ in range(3):
        part = values.astype(BF16)
        total = total + lanes_product(part, pick)
        values = values - part.astype(F32)
    meta[:slots] = total
    meta[slots:] = lanes_product(columns[...].astype(F32), pick)


def products(z, x, tiles_high, tiles_low, cols):
    step = 32

    @pl.loop(0, z.shape[1] // step)
    def _(i):
        first = pl.multiple_of(i * step, step)
        left = x[pl.ds(pl.multiple_of(i * step * cols, step * cols), step * cols), :]
        for pair in range(tiles_high.shape[0]):
            out = jnp.dot(left, tiles_high[pair], preferred_element_type=F32)
            out = out + jnp.dot(left, tiles_low[pair], preferred_element_type=F32)
            for j in range(2):
                z[2 * pair + j, pl.ds(first, step)] = out[:, 128 * j : 128 * j + 128].reshape(
                    step, cols, 128
                )


def load_blocks(x, block, halos, plan, left):
    count, cols, cells = block.shape

    def put(rows, values):
        high, low = split(values)
        x[rows, :cells] = high
        x[rows, cells:] = low

    put(slice(0, count * cols), block[...].reshape(count * cols, cells))
    for n, halo in enumerate(halos):
        rows = halo.shape[0] * cols
        values = jnp.where(plan[len(halos) + n] != 0, halo[...].reshape(rows, cells), 0.0)
        if left is not None:
            values = apply_scaler(left, values)
        start = pl.multiple_of((count + plan[n] * halo.shape[0]) * cols, rows)
        put(pl.ds(start, rows), values)


def combine(z, weights, columns, b, count):
    total = weights[b] * z[0, columns[b]]
    for k in range(1, z.shape[0]):
        total = total + weights[k * count + b] * z[k, columns[k * count + b]]
    return total


def operator_kernel(plan, columns, weights, sends, block, h0, h1, h2, h3, th, tl, *rest):
    image, sent, x, z = rest[0], rest[1:-2], rest[-2], rest[-1]
    count, cols, _ = block.shape
    load_blocks(x, block, (h0, h1, h2, h3), plan, None)
    products(z, x, th, tl, cols)

    @pl.loop(0, count, unroll=4)
    def _(b):
        image[b] = combine(z, weights, columns, b, count)

    for n, out in enumerate(sent):
        for h in range(out.shape[0]):
            out[h] = image[sends[plan[n], h]]


def last_kernel(plan, columns, weights, order, block, h0, h1, h2, h3, th, tl, inv, meta, *rest):
    image, chunks, x, z = rest[0], rest[1:-2], rest[-2], rest[-1]
    count, cols, _ = block.shape
    load_blocks(x, block, (h0, h1, h2, h3), plan, scaler(inv[...]))
    products(z, x, th, tl, cols)
    size = count // len(chunks)
    for i, chunk in enumerate(chunks):

        @pl.loop(0, size, unroll=4)
        def _(r):
            b = order[i * size + r]
            value = combine(z, weights, columns, b, count)
            image[b] = value
            chunk[r] = value

    chunks[0][size] = meta[...]


def row_sum(sums):
    total = sums[0]
    for d in range(1, sums.shape[0]):
        total = total + sums[d]
    return total


def put_rows(packed, row):
    for d in range(packed.shape[0]):
        packed[d] = row


def groups_of(ref):
    count, cols, _ = ref.shape
    per = 128 // cols
    return [ref[g * per : (g + 1) * per].reshape(128, 128) for g in range(count // per)]


def gram_kernel(image, packed):
    cols = image.shape[1]
    both = stacked(groups_of(image))
    put_rows(packed, pack(inner(both, both, cols), cols))


def scale_kernel(sums, image, out, inverse, packed):
    _, cols, cells = image.shape
    per = 128 // cols
    inv = eliminate(unpack(row_sum(sums), cols), identity(cols))
    inverse[...] = inv
    left = scaler(inv)
    groups = [apply_scaler(left, g) for g in groups_of(image)]
    for g, value in enumerate(groups):
        out[g * per : (g + 1) * per] = value.reshape(per, cols, cells)
    both = stacked(groups)
    put_rows(packed, pack(inner(both, both, cols), cols))


def sums_kernel(sums, previous, image, packed, inverse):
    cols = image.shape[1]
    inv = eliminate(unpack(row_sum(sums), cols), identity(cols))
    inverse[...] = inv
    left = scaler(inv)
    now = stacked([apply_scaler(left, g) for g in groups_of(image)])
    before = stacked([apply_scaler(left, g) for g in groups_of(previous)])
    gram = pack(inner(now, now, cols), cols)
    cross = pack(inner(before, now, cols), cols)
    put_rows(packed, jnp.concatenate([gram, cross], 1))


def factor_kernel(order, sums, inverse, mine, theirs, total_inverse, rayleigh, weights, columns):
    cols = inverse.shape[0]
    count = weights.shape[1]
    slots = weights.shape[0]
    wide = cols * cols
    total = row_sum(sums)
    total_inverse[...] = eliminate(unpack(total[:, :wide], cols), inverse[...])
    rayleigh[...] = unpack(total[:, wide:], cols)[:, :cols]
    last = mine.shape[0] - 1
    both = jnp.concatenate([mine[last], theirs[last]], 1)
    moved = pltpu.roll(both, 2 * count - order[count], 1)[:, :count]
    weights[...] = moved[:slots]
    columns[...] = moved[slots:].astype(jnp.int32)


def final_kernel(first, order, inverse, image, *rest):
    theirs, out, rows = rest[:-2], rest[-2], rest[-1]
    if first:
        theirs = theirs[:-1]
    count, cols, cells = image.shape
    size, per = out.shape[0], 128 // cols
    part = first + pl.program_id(0)

    @pl.when(pl.program_id(0) == 0)
    def _():
        for i, chunk in enumerate(theirs):
            rows[count + i * size : count + (i + 1) * size] = chunk[:size]

        @pl.loop(0, count, unroll=4)
        def _(r):
            rows[r] = image[order[r]]

    left = scaler(inverse[...])
    start = order[count] + part * size
    for g in range(size // per):
        value = rows[pl.ds(start + g * per, per)].reshape(128, cells)
        out[g * per : (g + 1) * per] = apply_scaler(left, value).reshape(per, cols, cells)


def call(kernel, out_shape, in_specs, out_specs, scratch=(), limit=16, flops=0, moved=0, **more):
    return pl.pallas_call(
        kernel,
        out_shape=out_shape,
        in_specs=in_specs,
        out_specs=out_specs,
        scratch_shapes=list(scratch),
        compiler_params=pltpu.CompilerParams(vmem_limit_bytes=limit << 20),
        cost_estimate=pl.CostEstimate(flops=flops, transcendentals=0, bytes_accessed=moved),
        **more,
    )


def pairs(x, axis, odd):
    size = lax.axis_size(axis)
    swap = []
    for low in range(odd, size, 2):
        high = (low + 1) % size
        swap += [(low, high), (high, low)]
    return lax.ppermute(x, axis, swap)


def halo(sent):
    return (
        pairs(sent[0], "gx", 0),
        pairs(sent[1], "gx", 1),
        pairs(sent[2], "gy", 0),
        pairs(sent[3], "gy", 1),
    )


def everywhere(rows):
    return lax.all_to_all(rows, AXES, 0, 0, tiled=True)


def shape(*dims, dtype=F32):
    return jax.ShapeDtypeStruct(dims, dtype)


def exchange_plan(size_x, size_y):
    numbers, counts = [], []
    for base, axis, size in ((0, "gx", size_x), (2, "gy", size_y)):
        place = lax.axis_index(axis)
        odd = place % 2
        edge = jnp.where(odd == 1, place < size - 1, place > 0).astype(jnp.int32)
        numbers += [base + 1 - odd, base + odd]
        counts += [jnp.int32(1), edge]
    return jnp.stack(numbers + counts).astype(jnp.int32)


def per_device(start_block, slot_tiles, edge_weights, block_columns, halo_sends, split_side):
    block = start_block[0, 0]
    sends = halo_sends[0, 0]
    weights, columns = edge_weights[0, 0].T, block_columns[0, 0].T
    count, cols, cells = block.shape
    slots, width = slot_tiles.shape[0], sends.shape[1]
    size_x, size_y = lax.axis_size("gx"), lax.axis_size("gy")
    devices = size_x * size_y
    plan = exchange_plan(size_x, size_y)
    flat_weights = weights.reshape(slots * count)
    flat_columns = columns.reshape(slots * count)

    piece = shape(width, cols, cells)
    whole = shape(count, cols, cells)
    square = shape(cols, cells)
    sent = call(
        first_sends_kernel,
        [piece] * 4,
        [SMEM, SMEM, HBM],
        [VMEM] * 4,
        [pltpu.SemaphoreType.DMA((4, width))],
    )(plan, sends, block)
    near = halo(sent)

    wide = 2 * cells
    tiles = call(
        tiles_kernel, [shape(slots // 2, wide, wide, dtype=BF16)] * 2, [VMEM], [VMEM] * 2
    )(slot_tiles)
    my_side = (lax.axis_index("gy") >= size_y // 2).astype(jnp.int32)
    order, meta = call(
        order_kernel,
        [shape(8, count, dtype=jnp.int32), shape(2 * slots, count)],
        [SMEM] + [VMEM] * 3,
        [VMEM] * 2,
    )(my_side.reshape(1), split_side[0], weights, columns)
    order = order.reshape(8 * count)

    blocks = count + 4 * width
    scratch = [
        pltpu.VMEM((blocks * cols, wide), BF16),
        pltpu.VMEM((slots, blocks, cols, cells), F32),
    ]

    def operator(block, near):
        image, *sent = call(
            operator_kernel,
            [whole] + [piece] * 4,
            [SMEM] * 4 + [VMEM] * 7,
            [VMEM] * 5,
            scratch,
            limit=24,
        )(plan, flat_columns, flat_weights, sends, block, *near, *tiles)
        return image, sent

    gram_rows = shape(devices, 1, cols * cols)
    image, sent = operator(block, near)
    near = halo(sent)
    packed = call(gram_kernel, gram_rows, [VMEM], VMEM)(image)
    sums = everywhere(packed)
    image, sent = operator(image, near)
    near = halo(sent)
    previous, inverse, packed = call(
        scale_kernel, [whole, square, gram_rows], [VMEM] * 2, [VMEM] * 3
    )(sums, image)
    sums = everywhere(packed)

    size = count // CHUNKS
    image, *mine = call(
        last_kernel,
        [whole, shape(size + 1, cols, cells)] + [shape(size, cols, cells)] * (CHUNKS - 1),
        [SMEM] * 4 + [VMEM] * 9,
        [VMEM] * (1 + CHUNKS),
        scratch,
        limit=24,
    )(plan, flat_columns, flat_weights, order, previous, *near, *tiles, inverse, meta)
    swap = [(j, j ^ (size_y // 2)) for j in range(size_y)]
    theirs = [lax.ppermute(x, "gy", swap) for x in mine]

    packed, inverse = call(
        sums_kernel,
        [shape(devices, 1, 2 * cols * cols), square],
        [VMEM] * 3,
        [VMEM] * 2,
    )(sums, previous, image)
    sums = everywhere(packed)
    inverse, rayleigh, moved_weights, moved_columns = call(
        factor_kernel,
        [
            square,
            shape(cols, cols),
            shape(slots, count),
            shape(slots, count, dtype=jnp.int32),
        ],
        [SMEM] + [VMEM] * 4,
        [VMEM] * 4,
    )(order, sums, inverse, mine[0], theirs[0])

    def final(first, parts, theirs, *before):
        return call(
            functools.partial(final_kernel, first),
            whole,
            [SMEM] + [VMEM] * (2 + len(theirs)) + [ANY] * len(before),
            pl.BlockSpec((size, cols, cells), lambda i: (first + i, 0, 0)),
            [pltpu.VMEM((2 * count, cols, cells), F32)],
            grid=(parts,),
            input_output_aliases={3 + len(theirs): 0} if before else {},
        )(order, inverse, image, *theirs, *before)

    moved_basis = final(0, CHUNKS - 1, theirs[:-1])
    moved_basis = final(CHUNKS - 1, 1, theirs, moved_basis)
    return (
        moved_basis[None, None],
        moved_weights.T[None, None],
        moved_columns.T[None, None],
        rayleigh,
    )


def solution(mesh):
    return jax.shard_map(
        per_device,
        mesh=mesh,
        in_specs=(
            P("gx", "gy", None, None, None),
            P(),
            P("gx", "gy", None, None),
            P("gx", "gy", None, None),
            P("gx", "gy", None, None),
            P("gx", "gy", None),
        ),
        out_specs=(
            P("gx", "gy", None, None, None),
            P("gx", "gy", None, None),
            P("gx", "gy", None, None),
            P(),
        ),
        check_vma=False,
    )
```

```python
import functools

import jax
import jax.numpy as jnp
from jax import lax
from jax.experimental import pallas as pl
from jax.experimental.pallas import tpu as pltpu
from jax.sharding import PartitionSpec as P

F32 = jnp.float32
BF16 = jnp.bfloat16
AXES = ("gx", "gy")
CHUNKS = 4
VMEM = pl.BlockSpec(memory_space=pltpu.VMEM)
SMEM = pl.BlockSpec(memory_space=pltpu.SMEM)
ANY = pl.BlockSpec(memory_space=pl.ANY)
HBM = pl.BlockSpec(memory_space=pltpu.HBM)


def split(x):
    high = x.astype(BF16)
    return high, (x - high.astype(F32)).astype(BF16)


def lane_group(rows, cols):
    return lax.broadcasted_iota(jnp.int32, (rows, 128), 1) // cols


def spread(x, cols):
    width = 64
    while width >= cols:
        x = x + pltpu.roll(x, width, 1)
        width //= 2
    return x


def unpack(packed, cols):
    half = 128 // cols
    sub = lax.broadcasted_iota(jnp.int32, (half, 128), 0)
    own = lane_group(half, cols) == sub
    parts = []
    for start in range(0, cols, half):
        row = packed[:, start * cols : start * cols + 128]
        parts.append(spread(jnp.where(own, jnp.broadcast_to(row, (half, 128)), 0.0), cols))
    return jnp.concatenate(parts, 0)


def pack(tiled, cols):
    half = 128 // cols
    sub = lax.broadcasted_iota(jnp.int32, (half, 128), 0)
    own = lane_group(half, cols) == sub
    rows = []
    for start in range(0, cols, half):
        part = jnp.where(own, tiled[start : start + half], 0.0)
        rows.append(jnp.sum(part, 0, keepdims=True))
    return jnp.concatenate(rows, 1)


def identity(cols):
    lane = lax.broadcasted_iota(jnp.int32, (cols, 128), 1) % cols
    return (lane == lax.broadcasted_iota(jnp.int32, (cols, 128), 0)).astype(F32)


def eliminate(gram, right):
    cols = gram.shape[0]
    row = lax.broadcasted_iota(jnp.int32, (cols, 128), 0)
    for j in range(cols):
        inv = lax.rsqrt(gram[j : j + 1, j : j + 1])
        factor = gram[:, j : j + 1] * inv
        gram_row = gram[j : j + 1, :] * inv
        right_row = right[j : j + 1, :] * inv
        below = row > j
        gram = jnp.where(below, gram - factor * gram_row, gram)
        right = jnp.where(
            below, right - factor * right_row, jnp.where(row == j, right_row, right)
        )
    return right


def scaler(small):
    cols = small.shape[0]
    group = lane_group(cols, cols)
    diag = jnp.concatenate(
        [jnp.where(group == g, small, 0.0) for g in range(128 // cols)], 0
    )
    high, low = split(diag)
    return jnp.concatenate(
        [jnp.concatenate([high, high], 1), jnp.concatenate([low, low], 1)], 0
    )


def apply_scaler(left, x):
    high, low = split(x)
    both = jnp.dot(left, jnp.concatenate([high, low], 0), preferred_element_type=F32)
    return both[:128] + both[128:]


def stacked(groups):
    pairs = [split(x) for x in groups]
    return jnp.concatenate(
        [
            jnp.concatenate([p[0] for p in pairs], 1),
            jnp.concatenate([p[1] for p in pairs], 1),
        ],
        0,
    )


def inner(a, b, cols):
    full = lax.dot_general(a, b, (((1,), (1,)), ((), ())), preferred_element_type=F32)
    half = full[:128] + full[128:]
    square = half[:, :128] + half[:, 128:]
    group = lane_group(cols, cols)
    total = jnp.zeros((cols, 128), F32)
    for g in range(128 // cols):
        total = total + jnp.where(group == g, square[g * cols : (g + 1) * cols], 0.0)
    return spread(total, cols)


def read_group(ref, g, per):
    x = ref[g * per : (g + 1) * per]
    return x.reshape(128, 128)


def first_sends_kernel(plan, sends_hbm, block, *rest):
    outs, (sends, sems, sem) = rest[:-3], rest[-3:]
    copy = pltpu.make_async_copy(sends_hbm, sends, sem)
    copy.start()
    copy.wait()
    copies = []
    for n, out in enumerate(outs):
        for h in range(out.shape[0]):
            copies.append(
                pltpu.make_async_copy(block.at[sends[plan[n], h]], out.at[h], sems.at[n, h])
            )
    for copy in copies:
        copy.start()
    for copy in copies:
        copy.wait()


def tiles_kernel(tiles, high_out, low_out):
    for pair in range(tiles.shape[0] // 2):
        for j in range(2):
            high, low = split(tiles[2 * pair + j])
            for half in range(2):
                rows = slice(128 * half, 128 * half + 128)
                high_out[pair, rows, 128 * j : 128 * j + 128] = high
                low_out[pair, rows, 128 * j : 128 * j + 128] = low


def lanes_product(a, b):
    return lax.dot_general(
        a.astype(BF16), b.astype(BF16), (((1,), (1,)), ((), ())), preferred_element_type=F32
    )


def order_kernel(side, sides, weights, columns, order, meta):
    count, slots = sides.shape[1], weights.shape[0]
    row = lax.broadcasted_iota(jnp.int32, (count, count), 0)
    col = lax.broadcasted_iota(jnp.int32, (count, count), 1)
    keep = jnp.broadcast_to((sides[...] == side[0]).astype(F32), (8, count))
    kept = lanes_product(keep, (col <= row).astype(F32))
    given = count - jnp.sum(keep, 1, keepdims=True)
    lane = lax.broadcasted_iota(jnp.int32, (8, count), 1).astype(F32)
    place = jnp.where(keep > 0.5, given + kept - 1.0, lane - kept)
    pick = (place[:1].astype(jnp.int32) == row).astype(F32)
    moved = lanes_product(lane, pick)
    order[...] = jnp.where(
        lax.broadcasted_iota(jnp.int32, (8, count), 0) == 0, moved, given
    ).astype(jnp.int32)
    values = weights[...]
    total = jnp.zeros((slots, count), F32)
    for _ in range(3):
        part = values.astype(BF16)
        total = total + lanes_product(part, pick)
        values = values - part.astype(F32)
    meta[:slots] = total
    meta[slots:] = lanes_product(columns[...].astype(F32), pick)


def products(z, x, tiles_high, tiles_low, cols):
    step = 32

    @pl.loop(0, z.shape[1] // step)
    def _(i):
        first = pl.multiple_of(i * step, step)
        left = x[pl.ds(pl.multiple_of(i * step * cols, step * cols), step * cols), :]
        for pair in range(tiles_high.shape[0]):
            out = jnp.dot(left, tiles_high[pair], preferred_element_type=F32)
            out = out + jnp.dot(left, tiles_low[pair], preferred_element_type=F32)
            for j in range(2):
                z[2 * pair + j, pl.ds(first, step)] = out[:, 128 * j : 128 * j + 128].reshape(
                    step, cols, 128
                )


def load_blocks(x, block, halos, landed, sems, plan, left):
    count, cols, cells = block.shape
    copies = [
        pltpu.make_async_copy(halo, landed.at[n], sems.at[n]) for n, halo in enumerate(halos)
    ]
    for copy in copies:
        copy.start()

    def put(rows, values):
        high, low = split(values)
        x[rows, :cells] = high
        x[rows, cells:] = low

    put(slice(0, count * cols), block[...].reshape(count * cols, cells))
    for n, halo in enumerate(halos):
        rows = halo.shape[0] * cols
        copies[n].wait()
        values = jnp.where(plan[len(halos) + n] != 0, landed[n].reshape(rows, cells), 0.0)
        if left is not None:
            values = apply_scaler(left, values)
        start = pl.multiple_of((count + plan[n] * halo.shape[0]) * cols, rows)
        put(pl.ds(start, rows), values)


def combine(z, weights, columns, b, count):
    total = weights[b] * z[0, columns[b]]
    for k in range(1, z.shape[0]):
        total = total + weights[k * count + b] * z[k, columns[k * count + b]]
    return total


def operator_kernel(plan, columns, weights, sends, block, h0, h1, h2, h3, th, tl, *rest):
    image, sent, (x, z, landed, sems) = rest[0], rest[1:-4], rest[-4:]
    count, cols, _ = block.shape
    load_blocks(x, block, (h0, h1, h2, h3), landed, sems, plan, None)
    products(z, x, th, tl, cols)

    @pl.loop(0, count, unroll=4)
    def _(b):
        image[b] = combine(z, weights, columns, b, count)

    for n, out in enumerate(sent):
        for h in range(out.shape[0]):
            out[h] = image[sends[plan[n], h]]


def last_kernel(plan, columns, weights, order, block, h0, h1, h2, h3, th, tl, inv, meta, *rest):
    image, chunks, (x, z, landed, sems) = rest[0], rest[1:-4], rest[-4:]
    count, cols, _ = block.shape
    load_blocks(x, block, (h0, h1, h2, h3), landed, sems, plan, scaler(inv[...]))
    products(z, x, th, tl, cols)
    size = count // len(chunks)
    for i, chunk in enumerate(chunks):

        @pl.loop(0, size, unroll=4)
        def _(r):
            b = order[i * size + r]
            value = combine(z, weights, columns, b, count)
            image[b] = value
            chunk[r] = value

    chunks[0][size] = meta[...]


def row_sum(sums):
    total = sums[0]
    for d in range(1, sums.shape[0]):
        total = total + sums[d]
    return total


def put_rows(packed, row):
    for d in range(packed.shape[0]):
        packed[d] = row


def groups_of(ref):
    count, cols, _ = ref.shape
    per = 128 // cols
    return [ref[g * per : (g + 1) * per].reshape(128, 128) for g in range(count // per)]


def gram_kernel(image, packed):
    cols = image.shape[1]
    both = stacked(groups_of(image))
    put_rows(packed, pack(inner(both, both, cols), cols))


def scale_kernel(sums, image, out, inverse, packed):
    _, cols, cells = image.shape
    per = 128 // cols
    inv = eliminate(unpack(row_sum(sums), cols), identity(cols))
    inverse[...] = inv
    left = scaler(inv)
    groups = [apply_scaler(left, g) for g in groups_of(image)]
    for g, value in enumerate(groups):
        out[g * per : (g + 1) * per] = value.reshape(per, cols, cells)
    both = stacked(groups)
    put_rows(packed, pack(inner(both, both, cols), cols))


def sums_kernel(sums, previous, image, packed, inverse):
    cols = image.shape[1]
    inv = eliminate(unpack(row_sum(sums), cols), identity(cols))
    inverse[...] = inv
    left = scaler(inv)
    now = stacked([apply_scaler(left, g) for g in groups_of(image)])
    before = stacked([apply_scaler(left, g) for g in groups_of(previous)])
    gram = pack(inner(now, now, cols), cols)
    cross = pack(inner(before, now, cols), cols)
    put_rows(packed, jnp.concatenate([gram, cross], 1))


def factor_kernel(order, sums, inverse, mine, theirs, total_inverse, rayleigh, weights, columns):
    cols = inverse.shape[0]
    count = weights.shape[1]
    slots = weights.shape[0]
    wide = cols * cols
    total = row_sum(sums)
    total_inverse[...] = eliminate(unpack(total[:, :wide], cols), inverse[...])
    rayleigh[...] = unpack(total[:, wide:], cols)[:, :cols]
    last = mine.shape[0] - 1
    both = jnp.concatenate([mine[last], theirs[last]], 1)
    moved = pltpu.roll(both, 2 * count - order[count], 1)[:, :count]
    weights[...] = moved[:slots]
    columns[...] = moved[slots:].astype(jnp.int32)


def final_kernel(first, order, inverse, image, *rest):
    theirs, out, rows = rest[:-2], rest[-2], rest[-1]
    if first:
        theirs = theirs[:-1]
    count, cols, cells = image.shape
    size, per = out.shape[0], 128 // cols
    part = first + pl.program_id(0)

    @pl.when(pl.program_id(0) == 0)
    def _():
        for i, chunk in enumerate(theirs):
            rows[count + i * size : count + (i + 1) * size] = chunk[:size]

        @pl.loop(0, count, unroll=4)
        def _(r):
            rows[r] = image[order[r]]

    left = scaler(inverse[...])
    start = order[count] + part * size
    for g in range(size // per):
        value = rows[pl.ds(start + g * per, per)].reshape(128, cells)
        out[g * per : (g + 1) * per] = apply_scaler(left, value).reshape(per, cols, cells)


def call(kernel, out_shape, in_specs, out_specs, scratch=(), limit=24, cost=(0, 0), **more):
    return pl.pallas_call(
        kernel,
        out_shape=out_shape,
        in_specs=in_specs,
        out_specs=out_specs,
        scratch_shapes=list(scratch),
        compiler_params=pltpu.CompilerParams(vmem_limit_bytes=limit << 20),
        cost_estimate=pl.CostEstimate(flops=cost[0], transcendentals=0, bytes_accessed=cost[1]),
        **more,
    )


def pairs(x, axis, odd):
    size = lax.axis_size(axis)
    swap = []
    for low in range(odd, size, 2):
        high = (low + 1) % size
        swap += [(low, high), (high, low)]
    return lax.ppermute(x, axis, swap)


def in_hbm(x):
    return pltpu.with_memory_space_constraint(x, pltpu.HBM)


def halo(sent):
    near = (
        pairs(sent[0], "gx", 0),
        pairs(sent[1], "gx", 1),
        pairs(sent[2], "gy", 0),
        pairs(sent[3], "gy", 1),
    )
    return near


def everywhere(rows):
    return lax.all_to_all(rows, AXES, 0, 0, tiled=True)


def shape(*dims, dtype=F32):
    return jax.ShapeDtypeStruct(dims, dtype)


def exchange_plan(size_x, size_y):
    numbers, counts = [], []
    for base, axis, size in ((0, "gx", size_x), (2, "gy", size_y)):
        place = lax.axis_index(axis)
        odd = place % 2
        edge = jnp.where(odd == 1, place < size - 1, place > 0).astype(jnp.int32)
        numbers += [base + 1 - odd, base + odd]
        counts += [jnp.int32(1), edge]
    return jnp.stack(numbers + counts).astype(jnp.int32)


def per_device(start_block, slot_tiles, edge_weights, block_columns, halo_sends, split_side):
    block = start_block[0, 0]
    sends = halo_sends[0, 0]
    weights, columns = edge_weights[0, 0].T, block_columns[0, 0].T
    count, cols, cells = block.shape
    slots, width = slot_tiles.shape[0], sends.shape[1]
    size_x, size_y = lax.axis_size("gx"), lax.axis_size("gy")
    devices = size_x * size_y
    plan = exchange_plan(size_x, size_y)
    flat_weights = weights.reshape(slots * count)
    flat_columns = columns.reshape(slots * count)

    piece = shape(width, cols, cells)
    whole = shape(count, cols, cells)
    square = shape(cols, cells)
    sent = call(
        first_sends_kernel,
        [piece] * 4,
        [SMEM, HBM, HBM],
        [VMEM] * 4,
        [
            pltpu.SMEM(sends.shape, jnp.int32),
            pltpu.SemaphoreType.DMA((4, width)),
            pltpu.SemaphoreType.DMA,
        ],
    )(plan, in_hbm(sends), in_hbm(block))
    near = halo(sent)

    wide = 2 * cells
    tiles = call(
        tiles_kernel, [shape(slots // 2, wide, wide, dtype=BF16)] * 2, [VMEM], [VMEM] * 2
    )(slot_tiles)
    my_side = (lax.axis_index("gy") >= size_y // 2).astype(jnp.int32)
    order, meta = call(
        order_kernel,
        [shape(8, count, dtype=jnp.int32), shape(2 * slots, count)],
        [SMEM] + [VMEM] * 3,
        [VMEM] * 2,
    )(my_side.reshape(1), split_side[0], weights, columns)
    order = order.reshape(8 * count)

    blocks = count + 4 * width
    work = 8 * blocks * cols * cells * cells * slots, 0
    small = 8 * count * cells * cells * cols, 0
    scratch = [
        pltpu.VMEM((blocks * cols, wide), BF16),
        pltpu.VMEM((slots, blocks, cols, cells), F32),
        pltpu.VMEM((4, width, cols, cells), F32),
        pltpu.SemaphoreType.DMA((4,)),
    ]

    def operator(block, near):
        image, *sent = call(
            operator_kernel,
            [whole] + [piece] * 4,
            [SMEM] * 4 + [VMEM] + [ANY] * 4 + [VMEM] * 2,
            [VMEM] * 5,
            scratch,
            limit=24,
            cost=work,
        )(plan, flat_columns, flat_weights, sends, block, *near, *tiles)
        return image, sent

    gram_rows = shape(devices, 1, cols * cols)
    image, sent = operator(block, near)
    near = halo(sent)
    packed = call(gram_kernel, gram_rows, [VMEM], VMEM, cost=small)(image)
    image, packed = lax.optimization_barrier((image, packed))
    sums = everywhere(packed)
    image, sent = operator(image, near)
    near = halo(sent)
    previous, inverse, packed = call(
        scale_kernel, [whole, square, gram_rows], [VMEM] * 2, [VMEM] * 3, cost=small
    )(sums, image)
    sums = everywhere(packed)

    size = count // CHUNKS
    image, *mine = call(
        last_kernel,
        [whole, shape(size + 1, cols, cells)] + [shape(size, cols, cells)] * (CHUNKS - 1),
        [SMEM] * 4 + [VMEM] + [ANY] * 4 + [VMEM] * 4,
        [VMEM] * (1 + CHUNKS),
        scratch,
        limit=24,
        cost=work,
    )(plan, flat_columns, flat_weights, order, previous, *near, *tiles, inverse, meta)
    mine, sums = lax.optimization_barrier((mine, sums))
    swap = [(j, j ^ (size_y // 2)) for j in range(size_y)]
    theirs = [lax.ppermute(mine[0], "gy", swap)]
    packed, inverse = call(
        sums_kernel,
        [shape(devices, 1, 2 * cols * cols), square],
        [VMEM] * 3,
        [VMEM] * 2,
        cost=small,
    )(sums, previous, image)
    packed, *later = lax.optimization_barrier((packed, *mine[1:]))
    sums = everywhere(packed)
    theirs += [lax.ppermute(x, "gy", swap) for x in later]
    inverse, rayleigh, moved_weights, moved_columns = call(
        factor_kernel,
        [
            square,
            shape(cols, cols),
            shape(slots, count),
            shape(slots, count, dtype=jnp.int32),
        ],
        [SMEM] + [VMEM] * 4,
        [VMEM] * 4,
    )(order, sums, inverse, mine[0], theirs[0])

    def final(first, parts, theirs, *before):
        return call(
            functools.partial(final_kernel, first),
            whole,
            [SMEM] + [VMEM] * (2 + len(theirs)) + [ANY] * len(before),
            pl.BlockSpec((size, cols, cells), lambda i: (first + i, 0, 0)),
            [pltpu.VMEM((2 * count, cols, cells), F32)],
            grid=(parts,),
            input_output_aliases={3 + len(theirs): 0} if before else {},
        )(order, inverse, image, *theirs, *before)

    moved_basis = final(0, CHUNKS - 1, theirs[:-1])
    moved_basis = final(CHUNKS - 1, 1, theirs, moved_basis)
    return (
        moved_basis[None, None],
        moved_weights.T[None, None],
        moved_columns.T[None, None],
        rayleigh,
    )


def solution(mesh):
    return jax.shard_map(
        per_device,
        mesh=mesh,
        in_specs=(
            P("gx", "gy", None, None, None),
            P(),
            P("gx", "gy", None, None),
            P("gx", "gy", None, None),
            P("gx", "gy", None, None),
            P("gx", "gy", None),
        ),
        out_specs=(
            P("gx", "gy", None, None, None),
            P("gx", "gy", None, None),
            P("gx", "gy", None, None),
            P(),
        ),
        check_vma=False,
    )
```

```python
import functools

import jax
import jax.numpy as jnp
from jax import lax
from jax.experimental import pallas as pl
from jax.experimental.pallas import tpu as pltpu
from jax.sharding import PartitionSpec as P

F32 = jnp.float32
BF16 = jnp.bfloat16
AXES = ("gx", "gy")
CHUNKS = 4
VMEM = pl.BlockSpec(memory_space=pltpu.VMEM)
SMEM = pl.BlockSpec(memory_space=pltpu.SMEM)
ANY = pl.BlockSpec(memory_space=pl.ANY)
HBM = pl.BlockSpec(memory_space=pltpu.HBM)


def split(x):
    high = x.astype(BF16)
    return high, (x - high.astype(F32)).astype(BF16)


def lane_group(rows, cols):
    return lax.broadcasted_iota(jnp.int32, (rows, 128), 1) // cols


def spread(x, cols):
    width = 64
    while width >= cols:
        x = x + pltpu.roll(x, width, 1)
        width //= 2
    return x


def unpack(packed, cols):
    half = 128 // cols
    sub = lax.broadcasted_iota(jnp.int32, (half, 128), 0)
    own = lane_group(half, cols) == sub
    parts = []
    for start in range(0, cols, half):
        row = packed[:, start * cols : start * cols + 128]
        parts.append(spread(jnp.where(own, jnp.broadcast_to(row, (half, 128)), 0.0), cols))
    return jnp.concatenate(parts, 0)


def pack(tiled, cols):
    half = 128 // cols
    sub = lax.broadcasted_iota(jnp.int32, (half, 128), 0)
    own = lane_group(half, cols) == sub
    rows = []
    for start in range(0, cols, half):
        part = jnp.where(own, tiled[start : start + half], 0.0)
        rows.append(jnp.sum(part, 0, keepdims=True))
    return jnp.concatenate(rows, 1)


def identity(cols):
    lane = lax.broadcasted_iota(jnp.int32, (cols, 128), 1) % cols
    return (lane == lax.broadcasted_iota(jnp.int32, (cols, 128), 0)).astype(F32)


def eliminate(gram, right):
    cols = gram.shape[0]
    row = lax.broadcasted_iota(jnp.int32, (cols, 128), 0)
    for j in range(cols):
        inv = lax.rsqrt(gram[j : j + 1, j : j + 1])
        factor = gram[:, j : j + 1] * inv
        gram_row = gram[j : j + 1, :] * inv
        right_row = right[j : j + 1, :] * inv
        below = row > j
        gram = jnp.where(below, gram - factor * gram_row, gram)
        right = jnp.where(
            below, right - factor * right_row, jnp.where(row == j, right_row, right)
        )
    return right


def scaler(small):
    cols = small.shape[0]
    group = lane_group(cols, cols)
    diag = jnp.concatenate(
        [jnp.where(group == g, small, 0.0) for g in range(128 // cols)], 0
    )
    high, low = split(diag)
    return jnp.concatenate(
        [jnp.concatenate([high, high], 1), jnp.concatenate([low, low], 1)], 0
    )


def apply_scaler(left, x):
    high, low = split(x)
    both = jnp.dot(left, jnp.concatenate([high, low], 0), preferred_element_type=F32)
    return both[:128] + both[128:]


def stacked(groups):
    pairs = [split(x) for x in groups]
    return jnp.concatenate(
        [
            jnp.concatenate([p[0] for p in pairs], 1),
            jnp.concatenate([p[1] for p in pairs], 1),
        ],
        0,
    )


def inner(a, b, cols):
    full = lax.dot_general(a, b, (((1,), (1,)), ((), ())), preferred_element_type=F32)
    half = full[:128] + full[128:]
    square = half[:, :128] + half[:, 128:]
    group = lane_group(cols, cols)
    total = jnp.zeros((cols, 128), F32)
    for g in range(128 // cols):
        total = total + jnp.where(group == g, square[g * cols : (g + 1) * cols], 0.0)
    return spread(total, cols)


def read_group(ref, g, per):
    x = ref[g * per : (g + 1) * per]
    return x.reshape(128, 128)


def first_sends_kernel(plan, sends_hbm, block, *rest):
    outs, (sends, sems, sem) = rest[:-3], rest[-3:]
    copy = pltpu.make_async_copy(sends_hbm, sends, sem)
    copy.start()
    copy.wait()
    copies = []
    for n, out in enumerate(outs):
        for h in range(out.shape[0]):
            copies.append(
                pltpu.make_async_copy(block.at[sends[plan[n], h]], out.at[h], sems.at[n, h])
            )
    for copy in copies:
        copy.start()
    for copy in copies:
        copy.wait()


def tiles_kernel(tiles, high_out, low_out):
    for pair in range(tiles.shape[0] // 2):
        for j in range(2):
            high, low = split(tiles[2 * pair + j])
            high_out[pair, :, 128 * j : 128 * j + 128] = high
            low_out[pair, :, 128 * j : 128 * j + 128] = low


def lanes_product(a, b):
    return lax.dot_general(
        a.astype(BF16), b.astype(BF16), (((1,), (1,)), ((), ())), preferred_element_type=F32
    )


def order_kernel(side, sides, weights, columns, order, meta):
    count, slots = sides.shape[1], weights.shape[0]
    row = lax.broadcasted_iota(jnp.int32, (count, count), 0)
    col = lax.broadcasted_iota(jnp.int32, (count, count), 1)
    keep = jnp.broadcast_to((sides[...] == side[0]).astype(F32), (8, count))
    kept = lanes_product(keep, (col <= row).astype(F32))
    given = count - jnp.sum(keep, 1, keepdims=True)
    lane = lax.broadcasted_iota(jnp.int32, (8, count), 1).astype(F32)
    place = jnp.where(keep > 0.5, given + kept - 1.0, lane - kept)
    pick = (place[:1].astype(jnp.int32) == row).astype(F32)
    moved = lanes_product(lane, pick)
    order[...] = jnp.where(
        lax.broadcasted_iota(jnp.int32, (8, count), 0) == 0, moved, given
    ).astype(jnp.int32)
    values = weights[...]
    total = jnp.zeros((slots, count), F32)
    for _ in range(3):
        part = values.astype(BF16)
        total = total + lanes_product(part, pick)
        values = values - part.astype(F32)
    meta[:slots] = total
    meta[slots:] = lanes_product(columns[...].astype(F32), pick)


def products(z, x, tiles_high, tiles_low, cols):
    step = 32

    @pl.loop(0, z.shape[1] // step)
    def _(i):
        first = pl.multiple_of(i * step, step)
        left = x[pl.ds(pl.multiple_of(i * step * cols, step * cols), step * cols), :]
        for pair in range(tiles_high.shape[0]):
            high, low = tiles_high[pair], tiles_low[pair]
            out = jnp.dot(left, jnp.concatenate([high, high], 0), preferred_element_type=F32)
            out = out + jnp.dot(left, jnp.concatenate([low, low], 0), preferred_element_type=F32)
            for j in range(2):
                z[2 * pair + j, pl.ds(first, step)] = out[:, 128 * j : 128 * j + 128].reshape(
                    step, cols, 128
                )


def load_blocks(x, block, halos, landed, sems, plan, left):
    count, cols, cells = block.shape
    copies = [
        pltpu.make_async_copy(halo, landed.at[n], sems.at[n]) for n, halo in enumerate(halos)
    ]
    for copy in copies:
        copy.start()

    def put(rows, values):
        high, low = split(values)
        x[rows, :cells] = high
        x[rows, cells:] = low

    put(slice(0, count * cols), block[...].reshape(count * cols, cells))
    for n, halo in enumerate(halos):
        rows = halo.shape[0] * cols
        copies[n].wait()
        values = jnp.where(plan[len(halos) + n] != 0, landed[n].reshape(rows, cells), 0.0)
        if left is not None:
            values = apply_scaler(left, values)
        start = pl.multiple_of((count + plan[n] * halo.shape[0]) * cols, rows)
        put(pl.ds(start, rows), values)


def combine(z, weights, columns, b, count):
    total = weights[b] * z[0, columns[b]]
    for k in range(1, z.shape[0]):
        total = total + weights[k * count + b] * z[k, columns[k * count + b]]
    return total


def operator_kernel(plan, columns, weights, sends, block, h0, h1, h2, h3, th, tl, *rest):
    image, sent, (x, z, landed, sems) = rest[0], rest[1:-4], rest[-4:]
    count, cols, _ = block.shape
    load_blocks(x, block, (h0, h1, h2, h3), landed, sems, plan, None)
    products(z, x, th, tl, cols)

    @pl.loop(0, count, unroll=4)
    def _(b):
        image[b] = combine(z, weights, columns, b, count)

    for n, out in enumerate(sent):
        for h in range(out.shape[0]):
            out[h] = image[sends[plan[n], h]]


def last_kernel(plan, columns, weights, order, block, h0, h1, h2, h3, th, tl, inv, meta, *rest):
    image, chunks, (x, z, landed, sems, ordered, out_sems) = rest[0], rest[1:-6], rest[-6:]
    count, cols, _ = block.shape
    load_blocks(x, block, (h0, h1, h2, h3), landed, sems, plan, scaler(inv[...]))
    products(z, x, th, tl, cols)
    size = count // len(chunks)
    ordered[0, size] = meta[...]
    copies = []
    for i, chunk in enumerate(chunks):

        @pl.loop(0, size, unroll=4)
        def _(r):
            b = order[i * size + r]
            value = combine(z, weights, columns, b, count)
            image[b] = value
            ordered[i, r] = value

        copy = pltpu.make_async_copy(
            ordered.at[i, pl.ds(0, chunk.shape[0])], chunk, out_sems.at[i]
        )
        copy.start()
        copies.append(copy)
    for copy in copies:
        copy.wait()


def row_sum(sums):
    total = sums[0]
    for d in range(1, sums.shape[0]):
        total = total + sums[d]
    return total


def put_rows(packed, row):
    for d in range(packed.shape[0]):
        packed[d] = row


def groups_of(ref):
    count, cols, _ = ref.shape
    per = 128 // cols
    return [ref[g * per : (g + 1) * per].reshape(128, 128) for g in range(count // per)]


def gram_kernel(image, packed):
    cols = image.shape[1]
    both = stacked(groups_of(image))
    put_rows(packed, pack(inner(both, both, cols), cols))


def scale_kernel(sums, image, out, inverse, packed):
    _, cols, cells = image.shape
    per = 128 // cols
    inv = eliminate(unpack(row_sum(sums), cols), identity(cols))
    inverse[...] = inv
    left = scaler(inv)
    groups = [apply_scaler(left, g) for g in groups_of(image)]
    for g, value in enumerate(groups):
        out[g * per : (g + 1) * per] = value.reshape(per, cols, cells)
    both = stacked(groups)
    put_rows(packed, pack(inner(both, both, cols), cols))


def sums_kernel(sums, previous, image, packed, inverse):
    cols = image.shape[1]
    inv = eliminate(unpack(row_sum(sums), cols), identity(cols))
    inverse[...] = inv
    left = scaler(inv)
    now = stacked([apply_scaler(left, g) for g in groups_of(image)])
    before = stacked([apply_scaler(left, g) for g in groups_of(previous)])
    gram = pack(inner(now, now, cols), cols)
    cross = pack(inner(before, now, cols), cols)
    put_rows(packed, jnp.concatenate([gram, cross], 1))


def final_kernel(order, sums, inverse, image, meta, *rest):
    theirs, (out, rayleigh, weights, columns, rows, left) = rest[:-6], rest[-6:]
    count, cols, cells = image.shape
    size, per = out.shape[0], 128 // cols

    @pl.when(pl.program_id(0) == 0)
    def _():
        wide = cols * cols
        total = row_sum(sums)
        left[...] = scaler(eliminate(unpack(total[:, :wide], cols), inverse[...]))
        rayleigh[...] = unpack(total[:, wide:], cols)[:, :cols]
        both = jnp.concatenate([meta[...], theirs[0][size]], 1)
        moved = pltpu.roll(both, 2 * count - order[count], 1)[:, :count]
        slots = weights.shape[0]
        weights[...] = moved[:slots]
        columns[...] = moved[slots:].astype(jnp.int32)
        for i, chunk in enumerate(theirs):
            rows[count + i * size : count + (i + 1) * size] = chunk[:size]

        @pl.loop(0, count, unroll=8)
        def _(r):
            rows[r] = image[order[r]]

    start = order[count] + pl.program_id(0) * size
    for g in range(size // per):
        value = rows[pl.ds(start + g * per, per)].reshape(128, cells)
        out[g * per : (g + 1) * per] = apply_scaler(left[...], value).reshape(per, cols, cells)


def call(kernel, out_shape, in_specs, out_specs, scratch=(), limit=24, cost=(0, 0), **more):
    return pl.pallas_call(
        kernel,
        out_shape=out_shape,
        in_specs=in_specs,
        out_specs=out_specs,
        scratch_shapes=list(scratch),
        compiler_params=pltpu.CompilerParams(vmem_limit_bytes=limit << 20),
        cost_estimate=pl.CostEstimate(flops=cost[0], transcendentals=0, bytes_accessed=cost[1]),
        **more,
    )


def pairs(x, axis, odd):
    size = lax.axis_size(axis)
    swap = []
    for low in range(odd, size, 2):
        high = (low + 1) % size
        swap += [(low, high), (high, low)]
    return lax.ppermute(x, axis, swap)


def in_hbm(x):
    return pltpu.with_memory_space_constraint(x, pltpu.HBM)


def halo(sent):
    near = (
        pairs(sent[0], "gx", 0),
        pairs(sent[1], "gx", 1),
        pairs(sent[2], "gy", 0),
        pairs(sent[3], "gy", 1),
    )
    return near


def everywhere(rows):
    return lax.all_to_all(rows, AXES, 0, 0, tiled=True)


def shape(*dims, dtype=F32):
    return jax.ShapeDtypeStruct(dims, dtype)


def exchange_plan(size_x, size_y):
    numbers, counts = [], []
    for base, axis, size in ((0, "gx", size_x), (2, "gy", size_y)):
        place = lax.axis_index(axis)
        odd = place % 2
        edge = jnp.where(odd == 1, place < size - 1, place > 0).astype(jnp.int32)
        numbers += [base + 1 - odd, base + odd]
        counts += [jnp.int32(1), edge]
    return jnp.stack(numbers + counts).astype(jnp.int32)


def per_device(start_block, slot_tiles, edge_weights, block_columns, halo_sends, split_side):
    block = start_block[0, 0]
    sends = halo_sends[0, 0]
    weights, columns = edge_weights[0, 0].T, block_columns[0, 0].T
    count, cols, cells = block.shape
    slots, width = slot_tiles.shape[0], sends.shape[1]
    size_x, size_y = lax.axis_size("gx"), lax.axis_size("gy")
    devices = size_x * size_y
    plan = exchange_plan(size_x, size_y)
    flat_weights = weights.reshape(slots * count)
    flat_columns = columns.reshape(slots * count)

    piece = shape(width, cols, cells)
    whole = shape(count, cols, cells)
    square = shape(cols, cells)
    sent = call(
        first_sends_kernel,
        [piece] * 4,
        [SMEM, HBM, HBM],
        [VMEM] * 4,
        [
            pltpu.SMEM(sends.shape, jnp.int32),
            pltpu.SemaphoreType.DMA((4, width)),
            pltpu.SemaphoreType.DMA,
        ],
    )(plan, in_hbm(sends), in_hbm(block))
    near = halo(sent)

    wide = 2 * cells
    tiles = call(
        tiles_kernel, [shape(slots // 2, cells, wide, dtype=BF16)] * 2, [VMEM], [VMEM] * 2
    )(slot_tiles)
    my_side = (lax.axis_index("gy") >= size_y // 2).astype(jnp.int32)
    order, meta = call(
        order_kernel,
        [shape(8, count, dtype=jnp.int32), shape(2 * slots, count)],
        [SMEM] + [VMEM] * 3,
        [VMEM] * 2,
    )(my_side.reshape(1), split_side[0], weights, columns)
    order = order.reshape(8 * count)

    blocks = count + 4 * width
    work = 8 * blocks * cols * cells * cells * slots, 0
    small = 8 * count * cells * cells * cols, 0
    scratch = [
        pltpu.VMEM((blocks * cols, wide), BF16),
        pltpu.VMEM((slots, blocks, cols, cells), F32),
        pltpu.VMEM((4, width, cols, cells), F32),
        pltpu.SemaphoreType.DMA((4,)),
    ]

    def operator(block, near):
        image, *sent = call(
            operator_kernel,
            [whole] + [piece] * 4,
            [SMEM] * 4 + [VMEM] + [ANY] * 4 + [VMEM] * 2,
            [VMEM] * 5,
            scratch,
            limit=24,
            cost=work,
        )(plan, flat_columns, flat_weights, sends, block, *near, *tiles)
        return image, sent

    gram_rows = shape(devices, 1, cols * cols)
    image, sent = operator(block, near)
    near = halo(sent)
    packed = call(gram_kernel, gram_rows, [VMEM], VMEM, cost=small)(image)
    image, packed, *near = lax.optimization_barrier((image, packed, *near))
    sums = everywhere(packed)
    image, sent = operator(image, near)
    near = halo(sent)
    previous, inverse, packed = call(
        scale_kernel, [whole, square, gram_rows], [VMEM] * 2, [VMEM] * 3, cost=small
    )(sums, image)
    packed, *near = lax.optimization_barrier((packed, *near))
    sums = everywhere(packed)

    size = count // CHUNKS
    image, *mine = call(
        last_kernel,
        [whole]
        + [pltpu.HBM((size + (i == 0), cols, cells), F32) for i in range(CHUNKS)],
        [SMEM] * 4 + [VMEM] + [ANY] * 4 + [VMEM] * 4,
        [VMEM] + [HBM] * CHUNKS,
        scratch
        + [
            pltpu.VMEM((CHUNKS, size + 1, cols, cells), F32),
            pltpu.SemaphoreType.DMA((CHUNKS,)),
        ],
        limit=24,
        cost=work,
    )(plan, flat_columns, flat_weights, order, previous, *near, *tiles, inverse, meta)
    mine, sums = lax.optimization_barrier((mine, sums))
    swap = [(j, j ^ (size_y // 2)) for j in range(size_y)]
    theirs = [lax.ppermute(mine[0], "gy", swap)]
    packed, inverse = call(
        sums_kernel,
        [shape(devices, 1, 2 * cols * cols), square],
        [VMEM] * 3,
        [VMEM] * 2,
        cost=small,
    )(sums, previous, image)
    packed, *later = lax.optimization_barrier((packed, *mine[1:]))
    sums = everywhere(packed)
    theirs += [lax.ppermute(x, "gy", swap) for x in later]
    moved_basis, rayleigh, moved_weights, moved_columns = call(
        final_kernel,
        [
            whole,
            shape(cols, cols),
            shape(slots, count),
            shape(slots, count, dtype=jnp.int32),
        ],
        [SMEM] + [VMEM] * (4 + CHUNKS),
        [pl.BlockSpec((size, cols, cells), lambda i: (i, 0, 0))] + [VMEM] * 3,
        [pltpu.VMEM((2 * count, cols, cells), F32), pltpu.VMEM((wide, wide), BF16)],
        grid=(CHUNKS,),
    )(order, sums, inverse, image, meta, *theirs)
    return (
        moved_basis[None, None],
        moved_weights.T[None, None],
        moved_columns.T[None, None],
        rayleigh,
    )


def solution(mesh):
    return jax.shard_map(
        per_device,
        mesh=mesh,
        in_specs=(
            P("gx", "gy", None, None, None),
            P(),
            P("gx", "gy", None, None),
            P("gx", "gy", None, None),
            P("gx", "gy", None, None),
            P("gx", "gy", None),
        ),
        out_specs=(
            P("gx", "gy", None, None, None),
            P("gx", "gy", None, None),
            P("gx", "gy", None, None),
            P(),
        ),
        check_vma=False,
    )
```

```python
import functools

import jax
import jax.numpy as jnp
from jax import lax
from jax.experimental import pallas as pl
from jax.experimental.pallas import tpu as pltpu
from jax.sharding import PartitionSpec as P

F32 = jnp.float32
BF16 = jnp.bfloat16
AXES = ("gx", "gy")
CHUNKS = 4
VMEM = pl.BlockSpec(memory_space=pltpu.VMEM)
SMEM = pl.BlockSpec(memory_space=pltpu.SMEM)
ANY = pl.BlockSpec(memory_space=pl.ANY)
HBM = pl.BlockSpec(memory_space=pltpu.HBM)


def split(x):
    high = x.astype(BF16)
    return high, (x - high.astype(F32)).astype(BF16)


def lane_group(rows, cols):
    return lax.broadcasted_iota(jnp.int32, (rows, 128), 1) // cols


def spread(x, cols):
    width = 64
    while width >= cols:
        x = x + pltpu.roll(x, width, 1)
        width //= 2
    return x


def unpack(packed, cols):
    half = 128 // cols
    sub = lax.broadcasted_iota(jnp.int32, (half, 128), 0)
    own = lane_group(half, cols) == sub
    parts = []
    for start in range(0, cols, half):
        row = packed[:, start * cols : start * cols + 128]
        parts.append(spread(jnp.where(own, jnp.broadcast_to(row, (half, 128)), 0.0), cols))
    return jnp.concatenate(parts, 0)


def pack(tiled, cols):
    half = 128 // cols
    sub = lax.broadcasted_iota(jnp.int32, (half, 128), 0)
    own = lane_group(half, cols) == sub
    rows = []
    for start in range(0, cols, half):
        part = jnp.where(own, tiled[start : start + half], 0.0)
        rows.append(jnp.sum(part, 0, keepdims=True))
    return jnp.concatenate(rows, 1)


def identity(cols):
    lane = lax.broadcasted_iota(jnp.int32, (cols, 128), 1) % cols
    return (lane == lax.broadcasted_iota(jnp.int32, (cols, 128), 0)).astype(F32)


def eliminate(gram, right):
    cols = gram.shape[0]
    row = lax.broadcasted_iota(jnp.int32, (cols, 128), 0)
    for j in range(cols):
        inv = lax.rsqrt(gram[j : j + 1, j : j + 1])
        factor = gram[:, j : j + 1] * inv
        gram_row = gram[j : j + 1, :] * inv
        right_row = right[j : j + 1, :] * inv
        below = row > j
        gram = jnp.where(below, gram - factor * gram_row, gram)
        right = jnp.where(
            below, right - factor * right_row, jnp.where(row == j, right_row, right)
        )
    return right


def scaler(small):
    cols = small.shape[0]
    group = lane_group(cols, cols)
    diag = jnp.concatenate(
        [jnp.where(group == g, small, 0.0) for g in range(128 // cols)], 0
    )
    high, low = split(diag)
    return jnp.concatenate(
        [jnp.concatenate([high, high], 1), jnp.concatenate([low, low], 1)], 0
    )


def apply_scaler(left, x):
    high, low = split(x)
    both = jnp.dot(left, jnp.concatenate([high, low], 0), preferred_element_type=F32)
    return both[:128] + both[128:]


def stacked(groups):
    pairs = [split(x) for x in groups]
    return jnp.concatenate(
        [
            jnp.concatenate([p[0] for p in pairs], 1),
            jnp.concatenate([p[1] for p in pairs], 1),
        ],
        0,
    )


def inner(a, b, cols):
    full = lax.dot_general(a, b, (((1,), (1,)), ((), ())), preferred_element_type=F32)
    half = full[:128] + full[128:]
    square = half[:, :128] + half[:, 128:]
    group = lane_group(cols, cols)
    total = jnp.zeros((cols, 128), F32)
    for g in range(128 // cols):
        total = total + jnp.where(group == g, square[g * cols : (g + 1) * cols], 0.0)
    return spread(total, cols)


def read_group(ref, g, per):
    x = ref[g * per : (g + 1) * per]
    return x.reshape(128, 128)


def first_sends_kernel(plan, sends_hbm, block, *rest):
    outs, (sends, sems, sem) = rest[:-3], rest[-3:]
    copy = pltpu.make_async_copy(sends_hbm, sends, sem)
    copy.start()
    copy.wait()
    copies = []
    for n, out in enumerate(outs):
        for h in range(out.shape[0]):
            copies.append(
                pltpu.make_async_copy(block.at[sends[plan[n], h]], out.at[h], sems.at[n, h])
            )
    for copy in copies:
        copy.start()
    for copy in copies:
        copy.wait()


def tiles_kernel(tiles, both_out):
    cells = tiles.shape[1]
    for k in range(tiles.shape[0]):
        high, low = split(tiles[k])
        both_out[k * cells : (k + 1) * cells, :cells] = high
        both_out[k * cells : (k + 1) * cells, cells:] = low


def lanes_product(a, b):
    return lax.dot_general(
        a.astype(BF16), b.astype(BF16), (((1,), (1,)), ((), ())), preferred_element_type=F32
    )


def order_kernel(side, sides, weights, columns, order, meta):
    count, slots = sides.shape[1], weights.shape[0]
    row = lax.broadcasted_iota(jnp.int32, (count, count), 0)
    col = lax.broadcasted_iota(jnp.int32, (count, count), 1)
    keep = jnp.broadcast_to((sides[...] == side[0]).astype(F32), (8, count))
    kept = lanes_product(keep, (col <= row).astype(F32))
    given = count - jnp.sum(keep, 1, keepdims=True)
    lane = lax.broadcasted_iota(jnp.int32, (8, count), 1).astype(F32)
    place = jnp.where(keep > 0.5, given + kept - 1.0, lane - kept)
    pick = (place[:1].astype(jnp.int32) == row).astype(F32)
    moved = lanes_product(lane, pick)
    order[...] = jnp.where(
        lax.broadcasted_iota(jnp.int32, (8, count), 0) == 0, moved, given
    ).astype(jnp.int32)
    values = weights[...]
    total = jnp.zeros((slots, count), F32)
    for _ in range(3):
        part = values.astype(BF16)
        total = total + lanes_product(part, pick)
        values = values - part.astype(F32)
    meta[:slots] = total
    meta[slots:] = lanes_product(columns[...].astype(F32), pick)


def fill(full, count, halos, plan, left):
    _, cols, cells = full.shape
    for n, halo in enumerate(halos):
        width = halo.shape[0]
        values = jnp.where(plan[len(halos) + n] != 0, halo[...], 0.0)
        if left is not None:
            values = apply_scaler(left, values.reshape(width * cols, cells))
            values = values.reshape(width, cols, cells)
        full[pl.ds(count + plan[n] * width, width)] = values


def gather(high, low, full, columns, weights, rows, count):
    _, cols, cells = full.shape
    for r, b in enumerate(rows):
        for k in range(high.shape[1] // cells):
            at = k * count + b
            upper, lower = split(full[columns[at]] * weights[at])
            place = slice(r * cols, (r + 1) * cols), slice(k * cells, (k + 1) * cells)
            high[place] = upper
            low[place] = lower


def multiply(high, low, tiles):
    cells = tiles.shape[1] // 2
    both = jnp.dot(high[...], tiles[...], preferred_element_type=F32)
    rest = jnp.dot(low[...], tiles[:, :cells], preferred_element_type=F32)
    return both[:, :cells] + (both[:, cells:] + rest)


def operator_kernel(plan, columns, weights, sends_hbm, block, h0, h1, h2, h3, tiles, *rest):
    image, sent, scratch = rest[0], rest[1:5], rest[5:]
    full, high0, low0, high1, low1, sends, sem = scratch
    copy = pltpu.make_async_copy(sends_hbm, sends, sem)
    copy.start()
    count, cols, cells = block.shape
    step = high0.shape[0] // cols

    def load(high, low, first):
        gather(high, low, full, columns, weights, [first + r for r in range(step)], count)

    def put(first, high, low):
        image[pl.ds(first, step)] = multiply(high, low, tiles).reshape(step, cols, cells)

    full[:count] = block[...]
    fill(full, count, (h0, h1, h2, h3), plan, None)
    load(high0, low0, 0)

    @pl.loop(0, count // (2 * step))
    def _(i):
        first = pl.multiple_of(i * 2 * step, 2 * step)
        load(high1, low1, first + step)
        put(first, high0, low0)
        load(high0, low0, jnp.minimum(first + 2 * step, count - step))
        put(first + step, high1, low1)

    copy.wait()
    for n, out in enumerate(sent):
        for h in range(out.shape[0]):
            out[h] = image[sends[plan[n], h]]


def last_first_kernel(plan, columns, weights, order, own, h0, h1, h2, h3, tiles, inv, meta, *rest):
    chunk, full, high, low = rest
    _, cols, cells = full.shape
    count = full.shape[0] - 4 * h0.shape[0]
    step = high.shape[0] // cols
    fill(full, count, (h0, h1, h2, h3), plan, scaler(inv[...]))
    gather(high, low, full, columns, weights, [order[r] for r in range(step)], count)
    chunk[:step] = multiply(high, low, tiles).reshape(step, cols, cells)
    chunk[step] = meta[...]


def last_rest_kernel(columns, weights, order, full, tiles, *rest):
    chunks, slots = rest[:-4], (rest[-4:-2], rest[-2:])
    _, cols, cells = full.shape
    step = slots[0][0].shape[0] // cols
    parts = len(chunks)
    count = (parts + 1) * step

    def load(part):
        rows = [order[part * step + r] for r in range(step)]
        gather(*slots[part % 2], full, columns, weights, rows, count)

    load(1)
    for part in range(1, parts + 1):
        if part < parts:
            load(part + 1)
        value = multiply(*slots[part % 2], tiles)
        chunks[part - 1][...] = value.reshape(step, cols, cells)


def row_sum(sums):
    total = sums[0]
    for d in range(1, sums.shape[0]):
        total = total + sums[d]
    return total


def put_rows(packed, row):
    for d in range(packed.shape[0]):
        packed[d] = row


def groups_of(ref):
    count, cols, _ = ref.shape
    per = 128 // cols
    return [ref[g * per : (g + 1) * per].reshape(128, 128) for g in range(count // per)]


def gram_kernel(image, packed):
    cols = image.shape[1]
    both = stacked(groups_of(image))
    put_rows(packed, pack(inner(both, both, cols), cols))


def scale_kernel(sums, image, out, inverse, packed):
    _, cols, cells = image.shape
    per = 128 // cols
    inv = eliminate(unpack(row_sum(sums), cols), identity(cols))
    inverse[...] = inv
    left = scaler(inv)
    groups = [apply_scaler(left, g) for g in groups_of(image)]
    for g, value in enumerate(groups):
        out[g * per : (g + 1) * per] = value.reshape(per, cols, cells)
    both = stacked(groups)
    put_rows(packed, pack(inner(both, both, cols), cols))


def sums_kernel(order, sums, full, first, *rest):
    later, (packed, inverse) = rest[:-2], rest[-2:]
    _, cols, cells = full.shape
    per = 128 // cols
    inv = eliminate(unpack(row_sum(sums), cols), identity(cols))
    inverse[...] = inv
    left = scaler(inv)
    count = (first.shape[0] - 1) * (len(later) + 1)
    own = groups_of(first.at[: first.shape[0] - 1])
    for chunk in later:
        own = own + groups_of(chunk)
    previous = [
        jnp.concatenate([full[order[g * per + r]] for r in range(per)], 0)
        for g in range(count // per)
    ]
    now = stacked([apply_scaler(left, g) for g in own])
    before = stacked([apply_scaler(left, g) for g in previous])
    gram = pack(inner(now, now, cols), cols)
    cross = pack(inner(before, now, cols), cols)
    put_rows(packed, jnp.concatenate([gram, cross], 1))


def final_kernel(order, sums, inverse, *rest):
    chunks, (out, rayleigh, weights, columns, rows, left) = rest[:-6], rest[-6:]
    mine, theirs = chunks[: len(chunks) // 2], chunks[len(chunks) // 2 :]
    slots, count = weights.shape
    cols, cells = out.shape[1:]
    size, per = out.shape[0], 128 // cols

    @pl.when(pl.program_id(0) == 0)
    def _():
        wide = cols * cols
        total = row_sum(sums)
        left[...] = scaler(eliminate(unpack(total[:, :wide], cols), inverse[...]))
        rayleigh[...] = unpack(total[:, wide:], cols)[:, :cols]
        both = jnp.concatenate([mine[0][size], theirs[0][size]], 1)
        moved = pltpu.roll(both, 2 * count - order[count], 1)[:, :count]
        weights[...] = moved[:slots]
        columns[...] = moved[slots:].astype(jnp.int32)
        for i in range(len(mine)):
            rows[i * size : (i + 1) * size] = mine[i][:size]
            rows[count + i * size : count + (i + 1) * size] = theirs[i][:size]

    start = order[count] + pl.program_id(0) * size
    for g in range(size // per):
        value = rows[pl.ds(start + g * per, per)].reshape(128, cells)
        out[g * per : (g + 1) * per] = apply_scaler(left[...], value).reshape(per, cols, cells)


def call(kernel, out_shape, in_specs, out_specs, scratch=(), limit=24, cost=(0, 0), **more):
    return pl.pallas_call(
        kernel,
        out_shape=out_shape,
        in_specs=in_specs,
        out_specs=out_specs,
        scratch_shapes=list(scratch),
        compiler_params=pltpu.CompilerParams(vmem_limit_bytes=limit << 20),
        cost_estimate=pl.CostEstimate(flops=cost[0], transcendentals=0, bytes_accessed=cost[1]),
        **more,
    )


def pairs(x, axis, odd):
    size = lax.axis_size(axis)
    swap = []
    for low in range(odd, size, 2):
        high = (low + 1) % size
        swap += [(low, high), (high, low)]
    return lax.ppermute(x, axis, swap)


def in_hbm(x):
    return pltpu.with_memory_space_constraint(x, pltpu.HBM)


def halo(sent):
    near = (
        pairs(sent[0], "gx", 0),
        pairs(sent[1], "gx", 1),
        pairs(sent[2], "gy", 0),
        pairs(sent[3], "gy", 1),
    )
    return near


def everywhere(rows):
    return lax.all_to_all(rows, AXES, 0, 0, tiled=True)


def shape(*dims, dtype=F32):
    return jax.ShapeDtypeStruct(dims, dtype)


def exchange_plan(size_x, size_y):
    numbers, counts = [], []
    for base, axis, size in ((0, "gx", size_x), (2, "gy", size_y)):
        place = lax.axis_index(axis)
        odd = place % 2
        edge = jnp.where(odd == 1, place < size - 1, place > 0).astype(jnp.int32)
        numbers += [base + 1 - odd, base + odd]
        counts += [jnp.int32(1), edge]
    return jnp.stack(numbers + counts).astype(jnp.int32)


def per_device(start_block, slot_tiles, edge_weights, block_columns, halo_sends, split_side):
    block = start_block[0, 0]
    sends = halo_sends[0, 0]
    weights, columns = edge_weights[0, 0].T, block_columns[0, 0].T
    count, cols, cells = block.shape
    slots, width = slot_tiles.shape[0], sends.shape[1]
    size_x, size_y = lax.axis_size("gx"), lax.axis_size("gy")
    devices = size_x * size_y
    plan = exchange_plan(size_x, size_y)
    flat_weights = weights.reshape(slots * count)
    flat_columns = columns.reshape(slots * count)

    piece = shape(width, cols, cells)
    whole = shape(count, cols, cells)
    square = shape(cols, cells)
    sent = call(
        first_sends_kernel,
        [piece] * 4,
        [SMEM, HBM, HBM],
        [VMEM] * 4,
        [
            pltpu.SMEM(sends.shape, jnp.int32),
            pltpu.SemaphoreType.DMA((4, width)),
            pltpu.SemaphoreType.DMA,
        ],
    )(plan, in_hbm(sends), in_hbm(block))
    near = halo(sent)

    wide = 2 * cells
    tiles = call(tiles_kernel, shape(slots * cells, wide, dtype=BF16), [VMEM], VMEM)(slot_tiles)
    my_side = (lax.axis_index("gy") >= size_y // 2).astype(jnp.int32)
    order, meta = call(
        order_kernel,
        [shape(8, count, dtype=jnp.int32), shape(2 * slots, count)],
        [SMEM] + [VMEM] * 3,
        [VMEM] * 2,
    )(my_side.reshape(1), split_side[0], weights, columns)
    order = order.reshape(8 * count)
    near, order, meta = lax.optimization_barrier((near, order, meta))

    size = count // CHUNKS
    blocks = shape(count + 4 * width, cols, cells)
    half = pltpu.VMEM((size * cols, slots * cells), BF16)
    work = 6 * count * cols * cells * cells * slots, 0
    small = 8 * count * cells * cells * cols, 0

    def operator(block, near, **more):
        image, *sent = call(
            operator_kernel,
            [whole] + [piece] * 4,
            [SMEM] * 3 + [HBM] + [VMEM] * 6,
            [VMEM] * 5,
            [
                pltpu.VMEM(blocks.shape, F32),
                half,
                half,
                half,
                half,
                pltpu.SMEM(sends.shape, jnp.int32),
                pltpu.SemaphoreType.DMA,
            ],
            cost=work,
            **more,
        )(plan, flat_columns, flat_weights, in_hbm(sends), block, *near, tiles)
        return image, sent

    gram_rows = shape(devices, 1, cols * cols)
    image, sent = operator(block, near)
    near = halo(sent)
    packed = call(gram_kernel, gram_rows, [VMEM], VMEM, cost=small)(image)
    image, packed, *near = lax.optimization_barrier((image, packed, *near))
    sums = everywhere(packed)
    image, sent = operator(image, near, input_output_aliases={4: 0})
    near = halo(sent)
    full, inverse, packed = call(
        scale_kernel, [blocks, square, gram_rows], [VMEM] * 2, [VMEM] * 3, cost=small
    )(sums, image)
    packed, *near = lax.optimization_barrier((packed, *near))
    sums = everywhere(packed)

    first, full = call(
        last_first_kernel,
        [shape(size + 1, cols, cells), blocks],
        [SMEM] * 4 + [VMEM] * 8,
        [VMEM] * 2,
        [half] * 2,
        cost=(work[0] // CHUNKS, 0),
        input_output_aliases={4: 1},
    )(plan, flat_columns, flat_weights, order, full, *near, tiles, inverse, meta)
    swap = [(j, j ^ (size_y // 2)) for j in range(size_y)]
    their_first = lax.ppermute(first, "gy", swap)
    later = call(
        last_rest_kernel,
        [shape(size, cols, cells)] * (CHUNKS - 1),
        [SMEM] * 3 + [VMEM] * 2,
        [VMEM] * (CHUNKS - 1),
        [half] * 4,
        cost=(work[0] // CHUNKS * (CHUNKS - 1), 0),
    )(flat_columns, flat_weights, order, full, tiles)
    later, sums = lax.optimization_barrier((later, sums))
    their_later = [lax.ppermute(x, "gy", swap) for x in later]

    packed, inverse = call(
        sums_kernel,
        [shape(devices, 1, 2 * cols * cols), square],
        [SMEM] + [VMEM] * (2 + CHUNKS),
        [VMEM] * 2,
    )(order, sums, full, first, *later)
    sums = everywhere(packed)
    moved_basis, rayleigh, moved_weights, moved_columns = call(
        final_kernel,
        [
            whole,
            shape(cols, cols),
            shape(slots, count),
            shape(slots, count, dtype=jnp.int32),
        ],
        [SMEM] + [VMEM] * (2 + 2 * CHUNKS),
        [pl.BlockSpec((size, cols, cells), lambda i: (i, 0, 0))] + [VMEM] * 3,
        [pltpu.VMEM((2 * count, cols, cells), F32), pltpu.VMEM((wide, wide), BF16)],
        grid=(CHUNKS,),
    )(order, sums, inverse, first, *later, their_first, *their_later)
    return (
        moved_basis[None, None],
        moved_weights.T[None, None],
        moved_columns.T[None, None],
        rayleigh,
    )


def solution(mesh):
    return jax.shard_map(
        per_device,
        mesh=mesh,
        in_specs=(
            P("gx", "gy", None, None, None),
            P(),
            P("gx", "gy", None, None),
            P("gx", "gy", None, None),
            P("gx", "gy", None, None),
            P("gx", "gy", None),
        ),
        out_specs=(
            P("gx", "gy", None, None, None),
            P("gx", "gy", None, None),
            P("gx", "gy", None, None),
            P(),
        ),
        check_vma=False,
    )
```

```python
import functools

import jax
import jax.numpy as jnp
from jax import lax
from jax.experimental import pallas as pl
from jax.experimental.pallas import tpu as pltpu
from jax.sharding import PartitionSpec as P

F32 = jnp.float32
BF16 = jnp.bfloat16
AXES = ("gx", "gy")
CHUNKS = 4
VMEM = pl.BlockSpec(memory_space=pltpu.VMEM)
SMEM = pl.BlockSpec(memory_space=pltpu.SMEM)
ANY = pl.BlockSpec(memory_space=pl.ANY)
HBM = pl.BlockSpec(memory_space=pltpu.HBM)


def split(x):
    high = x.astype(BF16)
    return high, (x - high.astype(F32)).astype(BF16)


def lane_group(rows, cols):
    return lax.broadcasted_iota(jnp.int32, (rows, 128), 1) // cols


def spread(x, cols):
    width = 64
    while width >= cols:
        x = x + pltpu.roll(x, width, 1)
        width //= 2
    return x


def unpack(packed, cols):
    half = 128 // cols
    sub = lax.broadcasted_iota(jnp.int32, (half, 128), 0)
    own = lane_group(half, cols) == sub
    parts = []
    for start in range(0, cols, half):
        row = packed[:, start * cols : start * cols + 128]
        parts.append(spread(jnp.where(own, jnp.broadcast_to(row, (half, 128)), 0.0), cols))
    return jnp.concatenate(parts, 0)


def pack(tiled, cols):
    half = 128 // cols
    sub = lax.broadcasted_iota(jnp.int32, (half, 128), 0)
    own = lane_group(half, cols) == sub
    rows = []
    for start in range(0, cols, half):
        part = jnp.where(own, tiled[start : start + half], 0.0)
        rows.append(jnp.sum(part, 0, keepdims=True))
    return jnp.concatenate(rows, 1)


def identity(cols):
    lane = lax.broadcasted_iota(jnp.int32, (cols, 128), 1) % cols
    return (lane == lax.broadcasted_iota(jnp.int32, (cols, 128), 0)).astype(F32)


def eliminate(gram, right):
    size = gram.shape[0]
    row = lax.broadcasted_iota(jnp.int32, (size, 128), 0)
    columns = [jnp.broadcast_to(gram[:, j : j + 1], (size, 128)) for j in range(size)]
    pivots = []
    for j in range(size):
        pivots.append(columns[j][j : j + 1])
        factor = jnp.where(row > j, columns[j], 0.0) * (1.0 / pivots[j])
        for k in range(j + 1, size):
            columns[k] = columns[k] - factor * columns[k][j : j + 1]
        right = right - factor * right[j : j + 1]
    return right * lax.rsqrt(jnp.concatenate(pivots, 0))


def scaler(small):
    cols = small.shape[0]
    group = lane_group(cols, cols)
    diag = jnp.concatenate(
        [jnp.where(group == g, small, 0.0) for g in range(128 // cols)], 0
    )
    high, low = split(diag)
    return jnp.concatenate(
        [jnp.concatenate([high, high], 1), jnp.concatenate([low, low], 1)], 0
    )


def apply_scaler(left, x):
    high, low = split(x)
    both = jnp.dot(left, jnp.concatenate([high, low], 0), preferred_element_type=F32)
    return both[:128] + both[128:]


def stacked(groups):
    pairs = [split(x) for x in groups]
    return jnp.concatenate(
        [
            jnp.concatenate([p[0] for p in pairs], 1),
            jnp.concatenate([p[1] for p in pairs], 1),
        ],
        0,
    )


def inner(a, b, cols):
    full = lax.dot_general(a, b, (((1,), (1,)), ((), ())), preferred_element_type=F32)
    half = full[:128] + full[128:]
    square = half[:, :128] + half[:, 128:]
    group = lane_group(cols, cols)
    total = jnp.zeros((cols, 128), F32)
    for g in range(128 // cols):
        total = total + jnp.where(group == g, square[g * cols : (g + 1) * cols], 0.0)
    return spread(total, cols)


def read_group(ref, g, per):
    x = ref[g * per : (g + 1) * per]
    return x.reshape(128, 128)


def first_sends_kernel(plan, sends_hbm, block_hbm, tiles_hbm, block, tiles, *rest):
    outs, (sends, sems) = rest[:-2], rest[-2:]
    copies = [
        pltpu.make_async_copy(sends_hbm, sends, sems.at[0]),
        pltpu.make_async_copy(block_hbm, block, sems.at[1]),
        pltpu.make_async_copy(tiles_hbm, tiles, sems.at[2]),
    ]
    for copy in copies:
        copy.start()
    copies[0].wait()
    copies[1].wait()
    for n, out in enumerate(outs):
        for h in range(out.shape[0]):
            out[h] = block[sends[plan[n], h]]
    copies[2].wait()


def tiles_kernel(tiles, both_out):
    cells = tiles.shape[1]
    for k in range(tiles.shape[0]):
        high, low = split(tiles[k])
        both_out[k * cells : (k + 1) * cells, :cells] = high
        both_out[k * cells : (k + 1) * cells, cells:] = low


def lanes_product(a, b):
    return lax.dot_general(
        a.astype(BF16), b.astype(BF16), (((1,), (1,)), ((), ())), preferred_element_type=F32
    )


def order_kernel(side, sides, weights, columns, order, meta):
    count, slots = sides.shape[1], weights.shape[0]
    row = lax.broadcasted_iota(jnp.int32, (count, count), 0)
    col = lax.broadcasted_iota(jnp.int32, (count, count), 1)
    keep = jnp.broadcast_to((sides[...] == side[0]).astype(F32), (8, count))
    kept = lanes_product(keep, (col <= row).astype(F32))
    given = count - jnp.sum(keep, 1, keepdims=True)
    lane = lax.broadcasted_iota(jnp.int32, (8, count), 1).astype(F32)
    place = jnp.where(keep > 0.5, given + kept - 1.0, lane - kept)
    pick = (place[:1].astype(jnp.int32) == row).astype(F32)
    moved = lanes_product(lane, pick)
    order[...] = jnp.where(
        lax.broadcasted_iota(jnp.int32, (8, count), 0) == 0, moved, given
    ).astype(jnp.int32)
    values = weights[...]
    total = jnp.zeros((slots, count), F32)
    for _ in range(3):
        part = values.astype(BF16)
        total = total + lanes_product(part, pick)
        values = values - part.astype(F32)
    meta[:slots] = total
    meta[slots:] = lanes_product(columns[...].astype(F32), pick)


def fill(full, count, halos, plan, left):
    _, cols, cells = full.shape
    for n, halo in enumerate(halos):
        width = halo.shape[0]
        values = jnp.where(plan[len(halos) + n] != 0, halo[...], 0.0)
        if left is not None:
            values = apply_scaler(left, values.reshape(width * cols, cells))
            values = values.reshape(width, cols, cells)
        full[pl.ds(count + plan[n] * width, width)] = values


def gather(high, low, full, columns, weights, rows, count):
    _, cols, cells = full.shape
    for r, b in enumerate(rows):
        for k in range(high.shape[1] // cells):
            at = k * count + b
            upper, lower = split(full[columns[at]] * weights[at])
            place = slice(r * cols, (r + 1) * cols), slice(k * cells, (k + 1) * cells)
            high[place] = upper
            low[place] = lower


def multiply(high, low, tiles):
    cells = tiles.shape[1] // 2
    both = jnp.dot(high[...], tiles[...], preferred_element_type=F32)
    rest = jnp.dot(low[...], tiles[:, :cells], preferred_element_type=F32)
    return both[:, :cells] + (both[:, cells:] + rest)


def operator_kernel(plan, columns, weights, sends_hbm, block, h0, h1, h2, h3, tiles, *rest):
    image, sent, scratch = rest[0], rest[1:5], rest[5:]
    full, high0, low0, high1, low1, sends, sem = scratch
    copy = pltpu.make_async_copy(sends_hbm, sends, sem)
    copy.start()
    count, cols, cells = block.shape
    step = high0.shape[0] // cols

    def load(high, low, first):
        gather(high, low, full, columns, weights, [first + r for r in range(step)], count)

    def put(first, high, low):
        image[pl.ds(first, step)] = multiply(high, low, tiles).reshape(step, cols, cells)

    full[:count] = block[...]
    fill(full, count, (h0, h1, h2, h3), plan, None)
    load(high0, low0, 0)

    @pl.loop(0, count // (2 * step))
    def _(i):
        first = pl.multiple_of(i * 2 * step, 2 * step)
        load(high1, low1, first + step)
        put(first, high0, low0)
        load(high0, low0, jnp.minimum(first + 2 * step, count - step))
        put(first + step, high1, low1)

    copy.wait()
    for n, out in enumerate(sent):
        for h in range(out.shape[0]):
            out[h] = image[sends[plan[n], h]]


def last_first_kernel(plan, columns, weights, order, own, h0, h1, h2, h3, tiles, inv, meta, *rest):
    chunk, full, high, low = rest
    _, cols, cells = full.shape
    count = full.shape[0] - 4 * h0.shape[0]
    step = high.shape[0] // cols
    fill(full, count, (h0, h1, h2, h3), plan, scaler(inv[...]))
    gather(high, low, full, columns, weights, [order[r] for r in range(step)], count)
    chunk[:step] = multiply(high, low, tiles).reshape(step, cols, cells)
    chunk[step] = meta[...]


def last_rest_kernel(columns, weights, order, full, tiles, *rest):
    chunks, slots = rest[:-4], (rest[-4:-2], rest[-2:])
    _, cols, cells = full.shape
    step = slots[0][0].shape[0] // cols
    parts = len(chunks)
    count = (parts + 1) * step

    def load(part):
        rows = [order[part * step + r] for r in range(step)]
        gather(*slots[part % 2], full, columns, weights, rows, count)

    load(1)
    for part in range(1, parts + 1):
        if part < parts:
            load(part + 1)
        value = multiply(*slots[part % 2], tiles)
        chunks[part - 1][...] = value.reshape(step, cols, cells)


def row_sum(sums):
    total = sums[0]
    for d in range(1, sums.shape[0]):
        total = total + sums[d]
    return total


def put_rows(packed, row):
    for d in range(packed.shape[0]):
        packed[d] = row


def groups_of(ref):
    count, cols, _ = ref.shape
    per = 128 // cols
    return [ref[g * per : (g + 1) * per].reshape(128, 128) for g in range(count // per)]


def gram_kernel(image, packed):
    cols = image.shape[1]
    both = stacked(groups_of(image))
    put_rows(packed, pack(inner(both, both, cols), cols))


def scale_kernel(sums, image, out, inverse, packed):
    _, cols, cells = image.shape
    per = 128 // cols
    inv = eliminate(unpack(row_sum(sums), cols), identity(cols))
    inverse[...] = inv
    left = scaler(inv)
    groups = [apply_scaler(left, g) for g in groups_of(image)]
    for g, value in enumerate(groups):
        out[g * per : (g + 1) * per] = value.reshape(per, cols, cells)
    both = stacked(groups)
    put_rows(packed, pack(inner(both, both, cols), cols))


def sums_kernel(order, sums, full, first, *rest):
    later, (packed, inverse) = rest[:-2], rest[-2:]
    _, cols, cells = full.shape
    per = 128 // cols
    inv = eliminate(unpack(row_sum(sums), cols), identity(cols))
    inverse[...] = inv
    left = scaler(inv)
    count = (first.shape[0] - 1) * (len(later) + 1)
    own = groups_of(first.at[: first.shape[0] - 1])
    for chunk in later:
        own = own + groups_of(chunk)
    previous = [
        jnp.concatenate([full[order[g * per + r]] for r in range(per)], 0)
        for g in range(count // per)
    ]
    now = stacked([apply_scaler(left, g) for g in own])
    before = stacked([apply_scaler(left, g) for g in previous])
    gram = pack(inner(now, now, cols), cols)
    cross = pack(inner(before, now, cols), cols)
    put_rows(packed, jnp.concatenate([gram, cross], 1))


def final_kernel(order, sums, inverse, *rest):
    chunks, (out, rayleigh, weights, columns, rows, ready, sems) = rest[:-7], rest[-7:]
    mine, theirs = chunks[: len(chunks) // 2], chunks[len(chunks) // 2 :]
    slots, count = weights.shape
    cols, cells = out.shape[1:]
    size, per = count // len(mine), 128 // cols
    wide = cols * cols
    for i in range(len(mine)):
        rows[i * size : (i + 1) * size] = mine[i][:size]
        rows[count + i * size : count + (i + 1) * size] = theirs[i][:size]
    total = row_sum(sums)
    left = scaler(eliminate(unpack(total[:, :wide], cols), inverse[...]))
    copies = []
    for i in range(len(mine)):
        for g in range(i * size, (i + 1) * size, per):
            value = rows[pl.ds(order[count] + g, per)].reshape(128, cells)
            ready[g : g + per] = apply_scaler(left, value).reshape(per, cols, cells)
        part = pl.ds(i * size, size)
        copies.append(pltpu.make_async_copy(ready.at[part], out.at[part], sems.at[i]))
        copies[i].start()
    rayleigh[...] = unpack(total[:, wide:], cols)[:, :cols]
    both = jnp.concatenate([mine[0][size], theirs[0][size]], 1)
    moved = pltpu.roll(both, 2 * count - order[count], 1)[:, :count]
    weights[...] = moved[:slots]
    columns[...] = moved[slots:].astype(jnp.int32)
    for copy in copies:
        copy.wait()


def call(kernel, out_shape, in_specs, out_specs, scratch=(), limit=24, cost=(0, 0), **more):
    return pl.pallas_call(
        kernel,
        out_shape=out_shape,
        in_specs=in_specs,
        out_specs=out_specs,
        scratch_shapes=list(scratch),
        compiler_params=pltpu.CompilerParams(vmem_limit_bytes=limit << 20),
        cost_estimate=pl.CostEstimate(flops=cost[0], transcendentals=0, bytes_accessed=cost[1]),
        **more,
    )


def pairs(x, axis, odd):
    size = lax.axis_size(axis)
    swap = []
    for low in range(odd, size, 2):
        high = (low + 1) % size
        swap += [(low, high), (high, low)]
    return lax.ppermute(x, axis, swap)


def in_hbm(x):
    return pltpu.with_memory_space_constraint(x, pltpu.HBM)


def halo(sent):
    near = (
        pairs(sent[0], "gx", 0),
        pairs(sent[1], "gx", 1),
        pairs(sent[2], "gy", 0),
        pairs(sent[3], "gy", 1),
    )
    return near


def everywhere(rows):
    return lax.all_to_all(rows, AXES, 0, 0, tiled=True)


def shape(*dims, dtype=F32):
    return jax.ShapeDtypeStruct(dims, dtype)


def exchange_plan(size_x, size_y):
    numbers, counts = [], []
    for base, axis, size in ((0, "gx", size_x), (2, "gy", size_y)):
        place = lax.axis_index(axis)
        odd = place % 2
        edge = jnp.where(odd == 1, place < size - 1, place > 0).astype(jnp.int32)
        numbers += [base + 1 - odd, base + odd]
        counts += [jnp.int32(1), edge]
    return jnp.stack(numbers + counts).astype(jnp.int32)


def per_device(start_block, slot_tiles, edge_weights, block_columns, halo_sends, split_side):
    block = start_block[0, 0]
    sends = halo_sends[0, 0]
    weights, columns = edge_weights[0, 0].T, block_columns[0, 0].T
    count, cols, cells = block.shape
    slots, width = slot_tiles.shape[0], sends.shape[1]
    size_x, size_y = lax.axis_size("gx"), lax.axis_size("gy")
    devices = size_x * size_y
    plan = exchange_plan(size_x, size_y)
    flat_weights = weights.reshape(slots * count)
    flat_columns = columns.reshape(slots * count)

    piece = shape(width, cols, cells)
    whole = shape(count, cols, cells)
    square = shape(cols, cells)
    block, slot_tiles, *sent = call(
        first_sends_kernel,
        [whole, shape(*slot_tiles.shape)] + [piece] * 4,
        [SMEM] + [HBM] * 3,
        [VMEM] * 6,
        [pltpu.SMEM(sends.shape, jnp.int32), pltpu.SemaphoreType.DMA((3,))],
    )(plan, in_hbm(sends), in_hbm(block), in_hbm(slot_tiles))
    near = halo(sent)

    wide = 2 * cells
    tiles = call(tiles_kernel, shape(slots * cells, wide, dtype=BF16), [VMEM], VMEM)(slot_tiles)
    my_side = (lax.axis_index("gy") >= size_y // 2).astype(jnp.int32)
    order, meta = call(
        order_kernel,
        [shape(8, count, dtype=jnp.int32), shape(2 * slots, count)],
        [SMEM] + [VMEM] * 3,
        [VMEM] * 2,
    )(my_side.reshape(1), split_side[0], weights, columns)
    order = order.reshape(8 * count)
    near, order, meta = lax.optimization_barrier((near, order, meta))

    size = count // CHUNKS
    blocks = shape(count + 4 * width, cols, cells)
    half = pltpu.VMEM((size * cols, slots * cells), BF16)
    work = 6 * count * cols * cells * cells * slots, 0
    small = 8 * count * cells * cells * cols, 0

    def operator(block, near):
        image, *sent = call(
            operator_kernel,
            [whole] + [piece] * 4,
            [SMEM] * 3 + [HBM] + [VMEM] * 6,
            [VMEM] * 5,
            [
                pltpu.VMEM(blocks.shape, F32),
                half,
                half,
                half,
                half,
                pltpu.SMEM(sends.shape, jnp.int32),
                pltpu.SemaphoreType.DMA,
            ],
            cost=work,
            input_output_aliases={4: 0},
        )(plan, flat_columns, flat_weights, in_hbm(sends), block, *near, tiles)
        return image, sent

    gram_rows = shape(devices, 1, cols * cols)
    image, sent = operator(block, near)
    near = halo(sent)
    packed = call(gram_kernel, gram_rows, [VMEM], VMEM, cost=small)(image)
    image, packed, *near = lax.optimization_barrier((image, packed, *near))
    sums = everywhere(packed)
    image, sent = operator(image, near)
    near = halo(sent)
    full, inverse, packed = call(
        scale_kernel, [blocks, square, gram_rows], [VMEM] * 2, [VMEM] * 3, cost=small
    )(sums, image)
    packed, *near = lax.optimization_barrier((packed, *near))
    sums = everywhere(packed)

    first, full = call(
        last_first_kernel,
        [shape(size + 1, cols, cells), blocks],
        [SMEM] * 4 + [VMEM] * 8,
        [VMEM] * 2,
        [half] * 2,
        cost=(work[0] // CHUNKS, 0),
        input_output_aliases={4: 1},
    )(plan, flat_columns, flat_weights, order, full, *near, tiles, inverse, meta)
    swap = [(j, j ^ (size_y // 2)) for j in range(size_y)]
    their_first = lax.ppermute(first, "gy", swap)
    later = call(
        last_rest_kernel,
        [shape(size, cols, cells)] * (CHUNKS - 1),
        [SMEM] * 3 + [VMEM] * 2,
        [VMEM] * (CHUNKS - 1),
        [half] * 4,
        cost=(work[0] // CHUNKS * (CHUNKS - 1), 0),
    )(flat_columns, flat_weights, order, full, tiles)
    later, sums = lax.optimization_barrier((later, sums))
    their_later = [lax.ppermute(x, "gy", swap) for x in later]

    packed, inverse = call(
        sums_kernel,
        [shape(devices, 1, 2 * cols * cols), square],
        [SMEM] + [VMEM] * (2 + CHUNKS),
        [VMEM] * 2,
    )(order, sums, full, first, *later)
    sums = everywhere(packed)
    moved_basis, rayleigh, moved_weights, moved_columns = call(
        final_kernel,
        [
            whole,
            shape(cols, cols),
            shape(slots, count),
            shape(slots, count, dtype=jnp.int32),
        ],
        [SMEM] + [VMEM] * (2 + 2 * CHUNKS),
        [ANY] + [VMEM] * 3,
        [
            pltpu.VMEM((2 * count, cols, cells), F32),
            pltpu.VMEM((count, cols, cells), F32),
            pltpu.SemaphoreType.DMA((CHUNKS,)),
        ],
    )(order, sums, inverse, first, *later, their_first, *their_later)
    return (
        moved_basis[None, None],
        moved_weights.T[None, None],
        moved_columns.T[None, None],
        rayleigh,
    )


def solution(mesh):
    return jax.shard_map(
        per_device,
        mesh=mesh,
        in_specs=(
            P("gx", "gy", None, None, None),
            P(),
            P("gx", "gy", None, None),
            P("gx", "gy", None, None),
            P("gx", "gy", None, None),
            P("gx", "gy", None),
        ),
        out_specs=(
            P("gx", "gy", None, None, None),
            P("gx", "gy", None, None),
            P("gx", "gy", None, None),
            P(),
        ),
        check_vma=False,
    )
```

```python
import functools

import jax
import jax.numpy as jnp
from jax import lax
from jax.experimental import pallas as pl
from jax.experimental.pallas import tpu as pltpu
from jax.sharding import PartitionSpec as P

F32 = jnp.float32
BF16 = jnp.bfloat16
AXES = ("gx", "gy")
CHUNKS = 4
VMEM = pl.BlockSpec(memory_space=pltpu.VMEM)
SMEM = pl.BlockSpec(memory_space=pltpu.SMEM)
ANY = pl.BlockSpec(memory_space=pl.ANY)
HBM = pl.BlockSpec(memory_space=pltpu.HBM)


def split(x):
    high = x.astype(BF16)
    return high, (x - high.astype(F32)).astype(BF16)


def lane_group(rows, cols):
    return lax.broadcasted_iota(jnp.int32, (rows, 128), 1) // cols


def spread(x, cols):
    width = 64
    while width >= cols:
        x = x + pltpu.roll(x, width, 1)
        width //= 2
    return x


def unpack(packed, cols):
    half = 128 // cols
    sub = lax.broadcasted_iota(jnp.int32, (half, 128), 0)
    own = lane_group(half, cols) == sub
    parts = []
    for start in range(0, cols, half):
        row = packed[:, start * cols : start * cols + 128]
        parts.append(spread(jnp.where(own, jnp.broadcast_to(row, (half, 128)), 0.0), cols))
    return jnp.concatenate(parts, 0)


def pack(tiled, cols):
    half = 128 // cols
    sub = lax.broadcasted_iota(jnp.int32, (half, 128), 0)
    own = lane_group(half, cols) == sub
    rows = []
    for start in range(0, cols, half):
        part = jnp.where(own, tiled[start : start + half], 0.0)
        rows.append(jnp.sum(part, 0, keepdims=True))
    return jnp.concatenate(rows, 1)


def identity(cols):
    lane = lax.broadcasted_iota(jnp.int32, (cols, 128), 1) % cols
    return (lane == lax.broadcasted_iota(jnp.int32, (cols, 128), 0)).astype(F32)


def eliminate(gram, right):
    size = gram.shape[0]
    row = lax.broadcasted_iota(jnp.int32, (size, 128), 0)
    columns = [jnp.broadcast_to(gram[:, j : j + 1], (size, 128)) for j in range(size)]
    pivots = []
    for j in range(size):
        pivots.append(columns[j][j : j + 1])
        factor = jnp.where(row > j, columns[j], 0.0) * (1.0 / pivots[j])
        for k in range(j + 1, size):
            columns[k] = columns[k] - factor * columns[k][j : j + 1]
        right = right - factor * right[j : j + 1]
    return right * lax.rsqrt(jnp.concatenate(pivots, 0))


def scaler(small):
    cols = small.shape[0]
    group = lane_group(cols, cols)
    diag = jnp.concatenate(
        [jnp.where(group == g, small, 0.0) for g in range(128 // cols)], 0
    )
    high, low = split(diag)
    return jnp.concatenate(
        [jnp.concatenate([high, high], 1), jnp.concatenate([low, low], 1)], 0
    )


def apply_scaler(left, x):
    high, low = split(x)
    both = jnp.dot(left, jnp.concatenate([high, low], 0), preferred_element_type=F32)
    return both[:128] + both[128:]


def stacked(groups):
    pairs = [split(x) for x in groups]
    return jnp.concatenate(
        [
            jnp.concatenate([p[0] for p in pairs], 1),
            jnp.concatenate([p[1] for p in pairs], 1),
        ],
        0,
    )


def inner(a, b, cols):
    full = lax.dot_general(a, b, (((1,), (1,)), ((), ())), preferred_element_type=F32)
    half = full[:128] + full[128:]
    square = half[:, :128] + half[:, 128:]
    group = lane_group(cols, cols)
    total = jnp.zeros((cols, 128), F32)
    for g in range(128 // cols):
        total = total + jnp.where(group == g, square[g * cols : (g + 1) * cols], 0.0)
    return spread(total, cols)


def read_group(ref, g, per):
    x = ref[g * per : (g + 1) * per]
    return x.reshape(128, 128)


def first_sends_kernel(plan, sends_hbm, block_hbm, tiles_hbm, block, tiles, *rest):
    outs, (sends, sems) = rest[:-2], rest[-2:]
    copies = [
        pltpu.make_async_copy(sends_hbm, sends, sems.at[0]),
        pltpu.make_async_copy(block_hbm, block, sems.at[1]),
        pltpu.make_async_copy(tiles_hbm, tiles, sems.at[2]),
    ]
    for copy in copies:
        copy.start()
    copies[0].wait()
    copies[1].wait()
    for n, out in enumerate(outs):
        for h in range(out.shape[0]):
            out[h] = block[sends[plan[n], h]]
    copies[2].wait()


def tiles_kernel(tiles, both_out):
    cells = tiles.shape[1]
    for k in range(tiles.shape[0]):
        high, low = split(tiles[k])
        both_out[k * cells : (k + 1) * cells, :cells] = high
        both_out[k * cells : (k + 1) * cells, cells:] = low


def lanes_product(a, b):
    return lax.dot_general(
        a.astype(BF16), b.astype(BF16), (((1,), (1,)), ((), ())), preferred_element_type=F32
    )


def order_kernel(side, sides, weights, columns, order, meta):
    count, slots = sides.shape[1], weights.shape[0]
    row = lax.broadcasted_iota(jnp.int32, (count, count), 0)
    col = lax.broadcasted_iota(jnp.int32, (count, count), 1)
    keep = jnp.broadcast_to((sides[...] == side[0]).astype(F32), (8, count))
    kept = lanes_product(keep, (col <= row).astype(F32))
    given = count - jnp.sum(keep, 1, keepdims=True)
    lane = lax.broadcasted_iota(jnp.int32, (8, count), 1).astype(F32)
    place = jnp.where(keep > 0.5, given + kept - 1.0, lane - kept)
    pick = (place[:1].astype(jnp.int32) == row).astype(F32)
    moved = lanes_product(lane, pick)
    order[...] = jnp.where(
        lax.broadcasted_iota(jnp.int32, (8, count), 0) == 0, moved, given
    ).astype(jnp.int32)
    values = weights[...]
    total = jnp.zeros((slots, count), F32)
    for _ in range(3):
        part = values.astype(BF16)
        total = total + lanes_product(part, pick)
        values = values - part.astype(F32)
    meta[:slots] = total
    meta[slots:] = lanes_product(columns[...].astype(F32), pick)


def fill(full, count, halos, plan, left):
    _, cols, cells = full.shape
    for n, halo in enumerate(halos):
        width = halo.shape[0]
        values = jnp.where(plan[len(halos) + n] != 0, halo[...], 0.0)
        if left is not None:
            values = apply_scaler(left, values.reshape(width * cols, cells))
            values = values.reshape(width, cols, cells)
        full[pl.ds(count + plan[n] * width, width)] = values


def gather(high, low, full, columns, weights, rows, count):
    _, cols, cells = full.shape
    for r, b in enumerate(rows):
        for k in range(high.shape[1] // cells):
            at = k * count + b
            upper, lower = split(full[columns[at]] * weights[at])
            place = slice(r * cols, (r + 1) * cols), slice(k * cells, (k + 1) * cells)
            high[place] = upper
            low[place] = lower


def multiply(high, low, tiles):
    cells = tiles.shape[1] // 2
    both = jnp.dot(high[...], tiles[...], preferred_element_type=F32)
    rest = jnp.dot(low[...], tiles[:, :cells], preferred_element_type=F32)
    return both[:, :cells] + (both[:, cells:] + rest)


def operator_kernel(plan, columns, weights, sends_hbm, block, h0, h1, h2, h3, tiles, *rest):
    image, sent, scratch = rest[0], rest[1:5], rest[5:]
    full, high0, low0, high1, low1, sends, sem = scratch
    copy = pltpu.make_async_copy(sends_hbm, sends, sem)
    copy.start()
    count, cols, cells = block.shape
    step = high0.shape[0] // cols

    def load(high, low, first):
        gather(high, low, full, columns, weights, [first + r for r in range(step)], count)

    def put(first, high, low):
        image[pl.ds(first, step)] = multiply(high, low, tiles).reshape(step, cols, cells)

    full[:count] = block[...]
    fill(full, count, (h0, h1, h2, h3), plan, None)
    load(high0, low0, 0)

    @pl.loop(0, count // (2 * step))
    def _(i):
        first = pl.multiple_of(i * 2 * step, 2 * step)
        load(high1, low1, first + step)
        put(first, high0, low0)
        load(high0, low0, jnp.minimum(first + 2 * step, count - step))
        put(first + step, high1, low1)

    copy.wait()
    for n, out in enumerate(sent):
        for h in range(out.shape[0]):
            out[h] = image[sends[plan[n], h]]


def last_first_kernel(plan, columns, weights, order, own, h0, h1, h2, h3, tiles, inv, meta, *rest):
    chunk, full, high, low = rest
    _, cols, cells = full.shape
    count = full.shape[0] - 4 * h0.shape[0]
    step = high.shape[0] // cols
    fill(full, count, (h0, h1, h2, h3), plan, scaler(inv[...]))
    gather(high, low, full, columns, weights, [order[r] for r in range(step)], count)
    chunk[:step] = multiply(high, low, tiles).reshape(step, cols, cells)
    chunk[step] = meta[...]


def last_rest_kernel(columns, weights, order, full, tiles, *rest):
    chunks, slots = rest[:-4], (rest[-4:-2], rest[-2:])
    _, cols, cells = full.shape
    step = slots[0][0].shape[0] // cols
    parts = len(chunks)
    count = (parts + 1) * step

    def load(part):
        rows = [order[part * step + r] for r in range(step)]
        gather(*slots[part % 2], full, columns, weights, rows, count)

    load(1)
    for part in range(1, parts + 1):
        if part < parts:
            load(part + 1)
        value = multiply(*slots[part % 2], tiles)
        chunks[part - 1][...] = value.reshape(step, cols, cells)


def row_sum(sums):
    total = sums[0]
    for d in range(1, sums.shape[0]):
        total = total + sums[d]
    return total


def put_rows(packed, row):
    for d in range(packed.shape[0]):
        packed[d] = row


def groups_of(ref):
    count, cols, _ = ref.shape
    per = 128 // cols
    return [ref[g * per : (g + 1) * per].reshape(128, 128) for g in range(count // per)]


def gram_kernel(image, packed):
    cols = image.shape[1]
    both = stacked(groups_of(image))
    put_rows(packed, pack(inner(both, both, cols), cols))


def scale_kernel(sums, image, out, inverse, packed):
    _, cols, cells = image.shape
    per = 128 // cols
    inv = eliminate(unpack(row_sum(sums), cols), identity(cols))
    inverse[...] = inv
    left = scaler(inv)
    groups = [apply_scaler(left, g) for g in groups_of(image)]
    for g, value in enumerate(groups):
        out[g * per : (g + 1) * per] = value.reshape(per, cols, cells)
    both = stacked(groups)
    put_rows(packed, pack(inner(both, both, cols), cols))


def sums_kernel(order, sums, full, first, *rest):
    later, (packed, inverse) = rest[:-2], rest[-2:]
    _, cols, cells = full.shape
    per = 128 // cols
    inv = eliminate(unpack(row_sum(sums), cols), identity(cols))
    inverse[...] = inv
    left = scaler(inv)
    count = (first.shape[0] - 1) * (len(later) + 1)
    own = groups_of(first.at[: first.shape[0] - 1])
    for chunk in later:
        own = own + groups_of(chunk)
    previous = [
        jnp.concatenate([full[order[g * per + r]] for r in range(per)], 0)
        for g in range(count // per)
    ]
    now = stacked([apply_scaler(left, g) for g in own])
    before = stacked([apply_scaler(left, g) for g in previous])
    gram = pack(inner(now, now, cols), cols)
    cross = pack(inner(before, now, cols), cols)
    put_rows(packed, jnp.concatenate([gram, cross], 1))


def final_kernel(order, sums, inverse, *rest):
    chunks, (out, rayleigh, weights, columns, rows, ready, sems) = rest[:-7], rest[-7:]
    mine, theirs = chunks[: len(chunks) // 2], chunks[len(chunks) // 2 :]
    slots, count = weights.shape
    cols, cells = out.shape[1:]
    size, per = count // len(mine), 128 // cols
    wide = cols * cols
    for i in range(len(mine)):
        rows[i * size : (i + 1) * size] = mine[i][:size]
        rows[count + i * size : count + (i + 1) * size] = theirs[i][:size]
    total = row_sum(sums)
    left = scaler(eliminate(unpack(total[:, :wide], cols), inverse[...]))
    copies = []
    for i in range(len(mine)):
        for g in range(i * size, (i + 1) * size, per):
            value = rows[pl.ds(order[count] + g, per)].reshape(128, cells)
            ready[g : g + per] = apply_scaler(left, value).reshape(per, cols, cells)
        part = pl.ds(i * size, size)
        copies.append(pltpu.make_async_copy(ready.at[part], out.at[part], sems.at[i]))
        copies[i].start()
    rayleigh[...] = unpack(total[:, wide:], cols)[:, :cols]
    both = jnp.concatenate([mine[0][size], theirs[0][size]], 1)
    moved = pltpu.roll(both, 2 * count - order[count], 1)[:, :count]
    weights[...] = moved[:slots]
    columns[...] = moved[slots:].astype(jnp.int32)
    for copy in copies:
        copy.wait()


def call(kernel, out_shape, in_specs, out_specs, scratch=(), limit=24, cost=(0, 0), **more):
    return pl.pallas_call(
        kernel,
        out_shape=out_shape,
        in_specs=in_specs,
        out_specs=out_specs,
        scratch_shapes=list(scratch),
        compiler_params=pltpu.CompilerParams(vmem_limit_bytes=limit << 20),
        cost_estimate=pl.CostEstimate(flops=cost[0], transcendentals=0, bytes_accessed=cost[1]),
        **more,
    )


def pairs(x, axis, odd):
    sizes = [lax.axis_size(name) for name in AXES]
    along = AXES.index(axis)
    swap = []
    for here in range(sizes[0] * sizes[1]):
        place = list(divmod(here, sizes[1]))
        if not odd:
            place[along] ^= 1
        elif place[along] in (0, sizes[along] - 1):
            place[1 - along] ^= 1
        else:
            place[along] += 1 if place[along] % 2 else -1
        swap.append((here, place[0] * sizes[1] + place[1]))
    return lax.ppermute(x, AXES, swap)


def in_hbm(x):
    return pltpu.with_memory_space_constraint(x, pltpu.HBM)


def halo(sent):
    near = [None] * 4
    for n, axis, odd in ((3, "gy", 1), (0, "gx", 0), (1, "gx", 1), (2, "gy", 0)):
        near[n] = pairs(sent[n], axis, odd)
    return near


def everywhere(rows):
    return lax.all_to_all(rows, AXES, 0, 0, tiled=True)


def shape(*dims, dtype=F32):
    return jax.ShapeDtypeStruct(dims, dtype)


def exchange_plan(size_x, size_y):
    numbers, counts = [], []
    for base, axis, size in ((0, "gx", size_x), (2, "gy", size_y)):
        place = lax.axis_index(axis)
        odd = place % 2
        edge = jnp.where(odd == 1, place < size - 1, place > 0).astype(jnp.int32)
        numbers += [base + 1 - odd, base + odd]
        counts += [jnp.int32(1), edge]
    return jnp.stack(numbers + counts).astype(jnp.int32)


def per_device(start_block, slot_tiles, edge_weights, block_columns, halo_sends, split_side):
    block = start_block[0, 0]
    sends = halo_sends[0, 0]
    weights, columns = edge_weights[0, 0].T, block_columns[0, 0].T
    count, cols, cells = block.shape
    slots, width = slot_tiles.shape[0], sends.shape[1]
    size_x, size_y = lax.axis_size("gx"), lax.axis_size("gy")
    devices = size_x * size_y
    plan = exchange_plan(size_x, size_y)
    flat_weights = weights.reshape(slots * count)
    flat_columns = columns.reshape(slots * count)

    piece = shape(width, cols, cells)
    whole = shape(count, cols, cells)
    square = shape(cols, cells)
    block, slot_tiles, *sent = call(
        first_sends_kernel,
        [whole, shape(*slot_tiles.shape)] + [piece] * 4,
        [SMEM] + [HBM] * 3,
        [VMEM] * 6,
        [pltpu.SMEM(sends.shape, jnp.int32), pltpu.SemaphoreType.DMA((3,))],
    )(plan, in_hbm(sends), in_hbm(block), in_hbm(slot_tiles))
    near = halo(sent)

    wide = 2 * cells
    tiles = call(tiles_kernel, shape(slots * cells, wide, dtype=BF16), [VMEM], VMEM)(slot_tiles)
    my_side = (lax.axis_index("gy") >= size_y // 2).astype(jnp.int32)
    order, meta = call(
        order_kernel,
        [shape(8, count, dtype=jnp.int32), shape(2 * slots, count)],
        [SMEM] + [VMEM] * 3,
        [VMEM] * 2,
    )(my_side.reshape(1), split_side[0], weights, columns)
    order = order.reshape(8 * count)
    near, order, meta = lax.optimization_barrier((near, order, meta))

    size = count // CHUNKS
    blocks = shape(count + 4 * width, cols, cells)
    half = pltpu.VMEM((size * cols, slots * cells), BF16)
    work = 6 * count * cols * cells * cells * slots, 0
    small = 8 * count * cells * cells * cols, 0

    def operator(block, near):
        image, *sent = call(
            operator_kernel,
            [whole] + [piece] * 4,
            [SMEM] * 3 + [HBM] + [VMEM] * 6,
            [VMEM] * 5,
            [
                pltpu.VMEM(blocks.shape, F32),
                half,
                half,
                half,
                half,
                pltpu.SMEM(sends.shape, jnp.int32),
                pltpu.SemaphoreType.DMA,
            ],
            cost=work,
            input_output_aliases={4: 0},
        )(plan, flat_columns, flat_weights, in_hbm(sends), block, *near, tiles)
        return image, sent

    gram_rows = shape(devices, 1, cols * cols)
    image, sent = operator(block, near)
    near = halo(sent)
    packed = call(gram_kernel, gram_rows, [VMEM], VMEM, cost=small)(image)
    image, packed = lax.optimization_barrier((image, packed))
    sums = everywhere(packed)
    image, sent = operator(image, near)
    near = halo(sent)
    full, inverse, packed = call(
        scale_kernel, [blocks, square, gram_rows], [VMEM] * 2, [VMEM] * 3, cost=small
    )(sums, image)
    packed, *near = lax.optimization_barrier((packed, *near))
    sums = everywhere(packed)

    first, full = call(
        last_first_kernel,
        [shape(size + 1, cols, cells), blocks],
        [SMEM] * 4 + [VMEM] * 8,
        [VMEM] * 2,
        [half] * 2,
        cost=(work[0] // CHUNKS, 0),
        input_output_aliases={4: 1},
    )(plan, flat_columns, flat_weights, order, full, *near, tiles, inverse, meta)
    swap = [(j, j ^ (size_y // 2)) for j in range(size_y)]
    their_first = lax.ppermute(first, "gy", swap)
    later = call(
        last_rest_kernel,
        [shape(size, cols, cells)] * (CHUNKS - 1),
        [SMEM] * 3 + [VMEM] * 2,
        [VMEM] * (CHUNKS - 1),
        [half] * 4,
        cost=(work[0] // CHUNKS * (CHUNKS - 1), 0),
    )(flat_columns, flat_weights, order, full, tiles)
    later, sums = lax.optimization_barrier((later, sums))
    their_later = [lax.ppermute(x, "gy", swap) for x in later]

    packed, inverse = call(
        sums_kernel,
        [shape(devices, 1, 2 * cols * cols), square],
        [SMEM] + [VMEM] * (2 + CHUNKS),
        [VMEM] * 2,
    )(order, sums, full, first, *later)
    sums = everywhere(packed)
    moved_basis, rayleigh, moved_weights, moved_columns = call(
        final_kernel,
        [
            whole,
            shape(cols, cols),
            shape(slots, count),
            shape(slots, count, dtype=jnp.int32),
        ],
        [SMEM] + [VMEM] * (2 + 2 * CHUNKS),
        [ANY] + [VMEM] * 3,
        [
            pltpu.VMEM((2 * count, cols, cells), F32),
            pltpu.VMEM((count, cols, cells), F32),
            pltpu.SemaphoreType.DMA((CHUNKS,)),
        ],
    )(order, sums, inverse, first, *later, their_first, *their_later)
    return (
        moved_basis[None, None],
        moved_weights.T[None, None],
        moved_columns.T[None, None],
        rayleigh,
    )


def solution(mesh):
    return jax.shard_map(
        per_device,
        mesh=mesh,
        in_specs=(
            P("gx", "gy", None, None, None),
            P(),
            P("gx", "gy", None, None),
            P("gx", "gy", None, None),
            P("gx", "gy", None, None),
            P("gx", "gy", None),
        ),
        out_specs=(
            P("gx", "gy", None, None, None),
            P("gx", "gy", None, None),
            P("gx", "gy", None, None),
            P(),
        ),
        check_vma=False,
    )
```

```python
import functools

import jax
import jax.numpy as jnp
from jax import lax
from jax.experimental import pallas as pl
from jax.experimental.pallas import tpu as pltpu
from jax.sharding import PartitionSpec as P

F32 = jnp.float32
BF16 = jnp.bfloat16
AXES = ("gx", "gy")
EXCHANGES = (("gy", 1), ("gx", 0), ("gx", 1), ("gy", 0))
CHUNKS = 4
VMEM = pl.BlockSpec(memory_space=pltpu.VMEM)
SMEM = pl.BlockSpec(memory_space=pltpu.SMEM)
ANY = pl.BlockSpec(memory_space=pl.ANY)
HBM = pl.BlockSpec(memory_space=pltpu.HBM)


def split(x):
    high = x.astype(BF16)
    return high, (x - high.astype(F32)).astype(BF16)


def lane_group(rows, cols):
    return lax.broadcasted_iota(jnp.int32, (rows, 128), 1) // cols


def spread(x, cols):
    width = 64
    while width >= cols:
        x = x + pltpu.roll(x, width, 1)
        width //= 2
    return x


def unpack(packed, cols):
    half = 128 // cols
    sub = lax.broadcasted_iota(jnp.int32, (half, 128), 0)
    own = lane_group(half, cols) == sub
    parts = []
    for start in range(0, cols, half):
        row = packed[:, start * cols : start * cols + 128]
        parts.append(spread(jnp.where(own, jnp.broadcast_to(row, (half, 128)), 0.0), cols))
    return jnp.concatenate(parts, 0)


def pack(tiled, cols):
    half = 128 // cols
    sub = lax.broadcasted_iota(jnp.int32, (half, 128), 0)
    own = lane_group(half, cols) == sub
    rows = []
    for start in range(0, cols, half):
        part = jnp.where(own, tiled[start : start + half], 0.0)
        rows.append(jnp.sum(part, 0, keepdims=True))
    return jnp.concatenate(rows, 1)


def identity(cols):
    lane = lax.broadcasted_iota(jnp.int32, (cols, 128), 1) % cols
    return (lane == lax.broadcasted_iota(jnp.int32, (cols, 128), 0)).astype(F32)


def eliminate(gram, right):
    size = gram.shape[0]
    row = lax.broadcasted_iota(jnp.int32, (size, 128), 0)
    columns = [jnp.broadcast_to(gram[:, j : j + 1], (size, 128)) for j in range(size)]
    pivots = []
    for j in range(size):
        pivots.append(columns[j][j : j + 1])
        factor = jnp.where(row > j, columns[j], 0.0) * (1.0 / pivots[j])
        for k in range(j + 1, size):
            columns[k] = columns[k] - factor * columns[k][j : j + 1]
        right = right - factor * right[j : j + 1]
    return right * lax.rsqrt(jnp.concatenate(pivots, 0))


def scaler(small):
    cols = small.shape[0]
    group = lane_group(cols, cols)
    diag = jnp.concatenate(
        [jnp.where(group == g, small, 0.0) for g in range(128 // cols)], 0
    )
    high, low = split(diag)
    return jnp.concatenate(
        [jnp.concatenate([high, high], 1), jnp.concatenate([low, low], 1)], 0
    )


def apply_scaler(left, x):
    high, low = split(x)
    both = jnp.dot(left, jnp.concatenate([high, low], 0), preferred_element_type=F32)
    return both[:128] + both[128:]


def stacked(groups):
    pairs = [split(x) for x in groups]
    return jnp.concatenate(
        [
            jnp.concatenate([p[0] for p in pairs], 1),
            jnp.concatenate([p[1] for p in pairs], 1),
        ],
        0,
    )


def inner(a, b, cols):
    full = lax.dot_general(a, b, (((1,), (1,)), ((), ())), preferred_element_type=F32)
    half = full[:128] + full[128:]
    square = half[:, :128] + half[:, 128:]
    group = lane_group(cols, cols)
    total = jnp.zeros((cols, 128), F32)
    for g in range(128 // cols):
        total = total + jnp.where(group == g, square[g * cols : (g + 1) * cols], 0.0)
    return spread(total, cols)


def read_group(ref, g, per):
    x = ref[g * per : (g + 1) * per]
    return x.reshape(128, 128)


def first_sends_kernel(plan, sends_hbm, block_hbm, tiles_hbm, block, tiles, *rest):
    outs, (sends, sends_sem, block_sems, tiles_sem) = rest[:-4], rest[-4:]
    parts = block_sems.shape[0]
    size = block.shape[0] // parts
    first = pltpu.make_async_copy(sends_hbm, sends, sends_sem)
    first.start()
    copies = []
    for i in range(parts):
        part = pl.ds(i * size, size)
        copies.append(pltpu.make_async_copy(block_hbm.at[part], block.at[part], block_sems.at[i]))
        copies[i].start()
    last = pltpu.make_async_copy(tiles_hbm, tiles, tiles_sem)
    last.start()
    first.wait()
    for copy in copies:
        copy.wait()
    for n, out in enumerate(outs):
        for h in range(out.shape[0]):
            out[h] = block[sends[plan[n], h]]
    last.wait()


def tiles_kernel(tiles, both_out):
    cells = tiles.shape[1]
    for k in range(tiles.shape[0]):
        high, low = split(tiles[k])
        both_out[k * cells : (k + 1) * cells, :cells] = high
        both_out[k * cells : (k + 1) * cells, cells:] = low


def lanes_product(a, b):
    return lax.dot_general(
        a.astype(BF16), b.astype(BF16), (((1,), (1,)), ((), ())), preferred_element_type=F32
    )


def order_kernel(side, sides, weights, columns, order, meta):
    count, slots = sides.shape[1], weights.shape[0]
    row = lax.broadcasted_iota(jnp.int32, (count, count), 0)
    col = lax.broadcasted_iota(jnp.int32, (count, count), 1)
    keep = jnp.broadcast_to((sides[...] == side[0]).astype(F32), (8, count))
    kept = lanes_product(keep, (col <= row).astype(F32))
    given = count - jnp.sum(keep, 1, keepdims=True)
    lane = lax.broadcasted_iota(jnp.int32, (8, count), 1).astype(F32)
    place = jnp.where(keep > 0.5, given + kept - 1.0, lane - kept)
    pick = (place[:1].astype(jnp.int32) == row).astype(F32)
    moved = lanes_product(lane, pick)
    order[...] = jnp.where(
        lax.broadcasted_iota(jnp.int32, (8, count), 0) == 0, moved, given
    ).astype(jnp.int32)
    values = weights[...]
    total = jnp.zeros((slots, count), F32)
    for _ in range(3):
        part = values.astype(BF16)
        total = total + lanes_product(part, pick)
        values = values - part.astype(F32)
    meta[:slots] = total
    meta[slots:] = lanes_product(columns[...].astype(F32), pick)


def fill(full, count, halos, plan, left):
    _, cols, cells = full.shape
    for n, halo in enumerate(halos):
        width = halo.shape[0]
        values = jnp.where(plan[len(halos) + n] != 0, halo[...], 0.0)
        if left is not None:
            values = apply_scaler(left, values.reshape(width * cols, cells))
            values = values.reshape(width, cols, cells)
        full[pl.ds(count + plan[n] * width, width)] = values


def gather(high, low, full, columns, weights, rows, count):
    _, cols, cells = full.shape
    for r, b in enumerate(rows):
        for k in range(high.shape[1] // cells):
            at = k * count + b
            upper, lower = split(full[columns[at]] * weights[at])
            place = slice(r * cols, (r + 1) * cols), slice(k * cells, (k + 1) * cells)
            high[place] = upper
            low[place] = lower


def multiply(high, low, tiles):
    cells = tiles.shape[1] // 2
    both = jnp.dot(high[...], tiles[...], preferred_element_type=F32)
    rest = jnp.dot(low[...], tiles[:, :cells], preferred_element_type=F32)
    return both[:, :cells] + (both[:, cells:] + rest)


def operator_kernel(plan, columns, weights, sends_hbm, block, h0, h1, h2, h3, tiles, *rest):
    image, sent, scratch = rest[0], rest[1:5], rest[5:]
    full, high0, low0, high1, low1, sends, sem = scratch
    copy = pltpu.make_async_copy(sends_hbm, sends, sem)
    copy.start()
    count, cols, cells = block.shape
    step = high0.shape[0] // cols

    def load(high, low, first):
        gather(high, low, full, columns, weights, [first + r for r in range(step)], count)

    def put(first, high, low):
        image[pl.ds(first, step)] = multiply(high, low, tiles).reshape(step, cols, cells)

    full[:count] = block[...]
    fill(full, count, (h0, h1, h2, h3), plan, None)
    load(high0, low0, 0)

    @pl.loop(0, count // (2 * step))
    def _(i):
        first = pl.multiple_of(i * 2 * step, 2 * step)
        load(high1, low1, first + step)
        put(first, high0, low0)
        load(high0, low0, jnp.minimum(first + 2 * step, count - step))
        put(first + step, high1, low1)

    copy.wait()
    for n, out in enumerate(sent):
        for h in range(out.shape[0]):
            out[h] = image[sends[plan[n], h]]


def last_first_kernel(plan, columns, weights, order, own, h0, h1, h2, h3, tiles, inv, meta, *rest):
    chunk, full, high, low = rest
    _, cols, cells = full.shape
    count = full.shape[0] - 4 * h0.shape[0]
    step = high.shape[0] // cols
    fill(full, count, (h0, h1, h2, h3), plan, scaler(inv[...]))
    gather(high, low, full, columns, weights, [order[r] for r in range(step)], count)
    chunk[:step] = multiply(high, low, tiles).reshape(step, cols, cells)
    chunk[step] = meta[...]


def last_rest_kernel(columns, weights, order, full, tiles, *rest):
    chunks, slots = rest[:-4], (rest[-4:-2], rest[-2:])
    _, cols, cells = full.shape
    step = slots[0][0].shape[0] // cols
    parts = len(chunks)
    count = (parts + 1) * step

    def load(part):
        rows = [order[part * step + r] for r in range(step)]
        gather(*slots[part % 2], full, columns, weights, rows, count)

    load(1)
    for part in range(1, parts + 1):
        if part < parts:
            load(part + 1)
        value = multiply(*slots[part % 2], tiles)
        chunks[part - 1][...] = value.reshape(step, cols, cells)


def row_sum(sums):
    total = sums[0]
    for d in range(1, sums.shape[0]):
        total = total + sums[d]
    return total


def put_rows(packed, row):
    for d in range(packed.shape[0]):
        packed[d] = row


def groups_of(ref):
    count, cols, _ = ref.shape
    per = 128 // cols
    return [ref[g * per : (g + 1) * per].reshape(128, 128) for g in range(count // per)]


def gram_kernel(image, packed):
    cols = image.shape[1]
    both = stacked(groups_of(image))
    put_rows(packed, pack(inner(both, both, cols), cols))


def scale_kernel(sums, image, out, inverse, packed):
    _, cols, cells = image.shape
    per = 128 // cols
    inv = eliminate(unpack(row_sum(sums), cols), identity(cols))
    inverse[...] = inv
    left = scaler(inv)
    groups = [apply_scaler(left, g) for g in groups_of(image)]
    for g, value in enumerate(groups):
        out[g * per : (g + 1) * per] = value.reshape(per, cols, cells)
    both = stacked(groups)
    put_rows(packed, pack(inner(both, both, cols), cols))


def sums_kernel(order, sums, full, first, *rest):
    later, (packed, inverse) = rest[:-2], rest[-2:]
    _, cols, cells = full.shape
    per = 128 // cols
    inv = eliminate(unpack(row_sum(sums), cols), identity(cols))
    inverse[...] = inv
    left = scaler(inv)
    count = (first.shape[0] - 1) * (len(later) + 1)
    own = groups_of(first.at[: first.shape[0] - 1])
    for chunk in later:
        own = own + groups_of(chunk)
    previous = [
        jnp.concatenate([full[order[g * per + r]] for r in range(per)], 0)
        for g in range(count // per)
    ]
    now = stacked([apply_scaler(left, g) for g in own])
    before = stacked([apply_scaler(left, g) for g in previous])
    gram = pack(inner(now, now, cols), cols)
    cross = pack(inner(before, now, cols), cols)
    put_rows(packed, jnp.concatenate([gram, cross], 1))


def final_kernel(order, sums, inverse, *rest):
    chunks, (out, rayleigh, weights, columns, rows, ready, sems) = rest[:-7], rest[-7:]
    mine, theirs = chunks[: len(chunks) // 2], chunks[len(chunks) // 2 :]
    slots, count = weights.shape
    cols, cells = out.shape[1:]
    size, per = count // len(mine), 128 // cols
    wide = cols * cols
    for i in range(len(mine)):
        rows[i * size : (i + 1) * size] = mine[i][:size]
        rows[count + i * size : count + (i + 1) * size] = theirs[i][:size]
    total = row_sum(sums)
    left = scaler(eliminate(unpack(total[:, :wide], cols), inverse[...]))
    copies = []
    part_size = count // sems.shape[0]
    for i in range(sems.shape[0]):
        for g in range(i * part_size, (i + 1) * part_size, per):
            value = rows[pl.ds(order[count] + g, per)].reshape(128, cells)
            ready[g : g + per] = apply_scaler(left, value).reshape(per, cols, cells)
        part = pl.ds(i * part_size, part_size)
        copies.append(pltpu.make_async_copy(ready.at[part], out.at[part], sems.at[i]))
        copies[i].start()
    rayleigh[...] = unpack(total[:, wide:], cols)[:, :cols]
    both = jnp.concatenate([mine[0][size], theirs[0][size]], 1)
    moved = pltpu.roll(both, 2 * count - order[count], 1)[:, :count]
    weights[...] = moved[:slots]
    columns[...] = moved[slots:].astype(jnp.int32)
    for copy in copies:
        copy.wait()


def call(kernel, out_shape, in_specs, out_specs, scratch=(), limit=24, cost=(0, 0), **more):
    return pl.pallas_call(
        kernel,
        out_shape=out_shape,
        in_specs=in_specs,
        out_specs=out_specs,
        scratch_shapes=list(scratch),
        compiler_params=pltpu.CompilerParams(vmem_limit_bytes=limit << 20),
        cost_estimate=pl.CostEstimate(flops=cost[0], transcendentals=0, bytes_accessed=cost[1]),
        **more,
    )


def pairs(x, axis, odd):
    sizes = [lax.axis_size(name) for name in AXES]
    along = AXES.index(axis)
    swap = []
    for here in range(sizes[0] * sizes[1]):
        place = list(divmod(here, sizes[1]))
        if not odd:
            place[along] ^= 1
        elif place[along] in (0, sizes[along] - 1):
            place[1 - along] ^= 1
        else:
            place[along] += 1 if place[along] % 2 else -1
        swap.append((here, place[0] * sizes[1] + place[1]))
    return lax.ppermute(x, AXES, swap)


def in_hbm(x):
    return pltpu.with_memory_space_constraint(x, pltpu.HBM)


def halo(sent):
    return [pairs(x, axis, odd) for x, (axis, odd) in zip(sent, EXCHANGES)]


def everywhere(rows):
    return lax.all_to_all(rows, AXES, 0, 0, tiled=True)


def shape(*dims, dtype=F32):
    return jax.ShapeDtypeStruct(dims, dtype)


def exchange_plan():
    numbers, counts = [], []
    for axis, odd in EXCHANGES:
        place = lax.axis_index(axis)
        upper = place % 2 if odd else 1 - place % 2
        inside = jnp.where(upper == 1, place < lax.axis_size(axis) - 1, place > 0)
        numbers.append(2 * AXES.index(axis) + upper)
        counts.append(inside.astype(jnp.int32))
    return jnp.stack(numbers + counts).astype(jnp.int32)


def per_device(start_block, slot_tiles, edge_weights, block_columns, halo_sends, split_side):
    block = start_block[0, 0]
    sends = halo_sends[0, 0]
    weights, columns = edge_weights[0, 0].T, block_columns[0, 0].T
    count, cols, cells = block.shape
    slots, width = slot_tiles.shape[0], sends.shape[1]
    size_x, size_y = lax.axis_size("gx"), lax.axis_size("gy")
    devices = size_x * size_y
    plan = exchange_plan()
    flat_weights = weights.reshape(slots * count)
    flat_columns = columns.reshape(slots * count)

    piece = shape(width, cols, cells)
    whole = shape(count, cols, cells)
    square = shape(cols, cells)
    block, slot_tiles, *sent = call(
        first_sends_kernel,
        [whole, shape(*slot_tiles.shape)] + [piece] * 4,
        [SMEM] + [HBM] * 3,
        [VMEM] * 6,
        [
            pltpu.SMEM(sends.shape, jnp.int32),
            pltpu.SemaphoreType.DMA,
            pltpu.SemaphoreType.DMA((8,)),
            pltpu.SemaphoreType.DMA,
        ],
    )(plan, in_hbm(sends), in_hbm(block), in_hbm(slot_tiles))
    near = halo(sent)

    wide = 2 * cells
    tiles = call(tiles_kernel, shape(slots * cells, wide, dtype=BF16), [VMEM], VMEM)(slot_tiles)
    my_side = (lax.axis_index("gy") >= size_y // 2).astype(jnp.int32)
    order, meta = call(
        order_kernel,
        [shape(8, count, dtype=jnp.int32), shape(2 * slots, count)],
        [SMEM] + [VMEM] * 3,
        [VMEM] * 2,
    )(my_side.reshape(1), split_side[0], weights, columns)
    order = order.reshape(8 * count)
    near, order, meta = lax.optimization_barrier((near, order, meta))

    size = count // CHUNKS
    blocks = shape(count + 4 * width, cols, cells)
    half = pltpu.VMEM((size * cols, slots * cells), BF16)
    work = 6 * count * cols * cells * cells * slots, 0
    small = 8 * count * cells * cells * cols, 0

    def operator(block, near):
        image, *sent = call(
            operator_kernel,
            [whole] + [piece] * 4,
            [SMEM] * 3 + [HBM] + [VMEM] * 6,
            [VMEM] * 5,
            [
                pltpu.VMEM(blocks.shape, F32),
                half,
                half,
                half,
                half,
                pltpu.SMEM(sends.shape, jnp.int32),
                pltpu.SemaphoreType.DMA,
            ],
            cost=work,
            input_output_aliases={4: 0},
        )(plan, flat_columns, flat_weights, in_hbm(sends), block, *near, tiles)
        return image, sent

    gram_rows = shape(devices, 1, cols * cols)
    image, sent = operator(block, near)
    near = halo(sent)
    packed = call(gram_kernel, gram_rows, [VMEM], VMEM, cost=small)(image)
    image, packed = lax.optimization_barrier((image, packed))
    sums = everywhere(packed)
    image, sent = operator(image, near)
    near = halo(sent)
    full, inverse, packed = call(
        scale_kernel, [blocks, square, gram_rows], [VMEM] * 2, [VMEM] * 3, cost=small
    )(sums, image)
    packed, *near = lax.optimization_barrier((packed, *near))
    sums = everywhere(packed)

    first, full = call(
        last_first_kernel,
        [shape(size + 1, cols, cells), blocks],
        [SMEM] * 4 + [VMEM] * 8,
        [VMEM] * 2,
        [half] * 2,
        cost=(work[0] // CHUNKS, 0),
        input_output_aliases={4: 1},
    )(plan, flat_columns, flat_weights, order, full, *near, tiles, inverse, meta)
    swap = [(j, j ^ (size_y // 2)) for j in range(size_y)]
    their_first = lax.ppermute(first, "gy", swap)
    later = call(
        last_rest_kernel,
        [shape(size, cols, cells)] * (CHUNKS - 1),
        [SMEM] * 3 + [VMEM] * 2,
        [VMEM] * (CHUNKS - 1),
        [half] * 4,
        cost=(work[0] // CHUNKS * (CHUNKS - 1), 0),
    )(flat_columns, flat_weights, order, full, tiles)
    later, sums = lax.optimization_barrier((later, sums))
    their_later = [lax.ppermute(x, "gy", swap) for x in later]

    packed, inverse = call(
        sums_kernel,
        [shape(devices, 1, 2 * cols * cols), square],
        [SMEM] + [VMEM] * (2 + CHUNKS),
        [VMEM] * 2,
    )(order, sums, full, first, *later)
    sums = everywhere(packed)
    moved_basis, rayleigh, moved_weights, moved_columns = call(
        final_kernel,
        [
            whole,
            shape(cols, cols),
            shape(slots, count),
            shape(slots, count, dtype=jnp.int32),
        ],
        [SMEM] + [VMEM] * (2 + 2 * CHUNKS),
        [ANY] + [VMEM] * 3,
        [
            pltpu.VMEM((2 * count, cols, cells), F32),
            pltpu.VMEM((count, cols, cells), F32),
            pltpu.SemaphoreType.DMA((8,)),
        ],
    )(order, sums, inverse, first, *later, their_first, *their_later)
    return (
        moved_basis[None, None],
        moved_weights.T[None, None],
        moved_columns.T[None, None],
        rayleigh,
    )


def solution(mesh):
    return jax.shard_map(
        per_device,
        mesh=mesh,
        in_specs=(
            P("gx", "gy", None, None, None),
            P(),
            P("gx", "gy", None, None),
            P("gx", "gy", None, None),
            P("gx", "gy", None, None),
            P("gx", "gy", None),
        ),
        out_specs=(
            P("gx", "gy", None, None, None),
            P("gx", "gy", None, None),
            P("gx", "gy", None, None),
            P(),
        ),
        check_vma=False,
    )
```

```python
import functools

import jax
import jax.numpy as jnp
from jax import lax
from jax.experimental import pallas as pl
from jax.experimental.pallas import tpu as pltpu
from jax.sharding import PartitionSpec as P

F32 = jnp.float32
BF16 = jnp.bfloat16
AXES = ("gx", "gy")
EXCHANGES = (("gy", 1), ("gx", 0), ("gx", 1), ("gy", 0))
CHUNKS = 4
PIECES = 4
VMEM = pl.BlockSpec(memory_space=pltpu.VMEM)
SMEM = pl.BlockSpec(memory_space=pltpu.SMEM)
ANY = pl.BlockSpec(memory_space=pl.ANY)
HBM = pl.BlockSpec(memory_space=pltpu.HBM)


def split(x):
    high = x.astype(BF16)
    return high, (x - high.astype(F32)).astype(BF16)


def lane_group(rows, cols):
    return lax.broadcasted_iota(jnp.int32, (rows, 128), 1) // cols


def spread(x, cols):
    width = 64
    while width >= cols:
        x = x + pltpu.roll(x, width, 1)
        width //= 2
    return x


def unpack(packed, cols):
    half = 128 // cols
    sub = lax.broadcasted_iota(jnp.int32, (half, 128), 0)
    own = lane_group(half, cols) == sub
    parts = []
    for start in range(0, cols, half):
        row = packed[:, start * cols : start * cols + 128]
        parts.append(spread(jnp.where(own, jnp.broadcast_to(row, (half, 128)), 0.0), cols))
    return jnp.concatenate(parts, 0)


def pack(tiled, cols):
    half = 128 // cols
    sub = lax.broadcasted_iota(jnp.int32, (half, 128), 0)
    own = lane_group(half, cols) == sub
    rows = []
    for start in range(0, cols, half):
        part = jnp.where(own, tiled[start : start + half], 0.0)
        rows.append(jnp.sum(part, 0, keepdims=True))
    return jnp.concatenate(rows, 1)


def identity(cols):
    lane = lax.broadcasted_iota(jnp.int32, (cols, 128), 1) % cols
    return (lane == lax.broadcasted_iota(jnp.int32, (cols, 128), 0)).astype(F32)


def eliminate(gram, right):
    size = gram.shape[0]
    row = lax.broadcasted_iota(jnp.int32, (size, 128), 0)
    columns = [jnp.broadcast_to(gram[:, j : j + 1], (size, 128)) for j in range(size)]
    pivots = []
    for j in range(size):
        pivots.append(columns[j][j : j + 1])
        factor = jnp.where(row > j, columns[j], 0.0) * (1.0 / pivots[j])
        for k in range(j + 1, size):
            columns[k] = columns[k] - factor * columns[k][j : j + 1]
        right = right - factor * right[j : j + 1]
    return right * lax.rsqrt(jnp.concatenate(pivots, 0))


def scaler(small):
    cols = small.shape[0]
    group = lane_group(cols, cols)
    diag = jnp.concatenate(
        [jnp.where(group == g, small, 0.0) for g in range(128 // cols)], 0
    )
    high, low = split(diag)
    return jnp.concatenate(
        [jnp.concatenate([high, high], 1), jnp.concatenate([low, low], 1)], 0
    )


def apply_scaler(left, x):
    high, low = split(x)
    both = jnp.dot(left, jnp.concatenate([high, low], 0), preferred_element_type=F32)
    return both[:128] + both[128:]


def stacked(groups):
    pairs = [split(x) for x in groups]
    return jnp.concatenate(
        [
            jnp.concatenate([p[0] for p in pairs], 1),
            jnp.concatenate([p[1] for p in pairs], 1),
        ],
        0,
    )


def inner(a, b, cols):
    full = lax.dot_general(a, b, (((1,), (1,)), ((), ())), preferred_element_type=F32)
    half = full[:128] + full[128:]
    square = half[:, :128] + half[:, 128:]
    group = lane_group(cols, cols)
    total = jnp.zeros((cols, 128), F32)
    for g in range(128 // cols):
        total = total + jnp.where(group == g, square[g * cols : (g + 1) * cols], 0.0)
    return spread(total, cols)


def read_group(ref, g, per):
    x = ref[g * per : (g + 1) * per]
    return x.reshape(128, 128)


def first_sends_kernel(plan, sends_hbm, block_hbm, tiles_hbm, block, tiles, *rest):
    outs, (sends, sends_sem, block_sems, tiles_sem) = rest[:-4], rest[-4:]
    parts = block_sems.shape[0]
    size = block.shape[0] // parts
    first = pltpu.make_async_copy(sends_hbm, sends, sends_sem)
    first.start()
    copies = []
    for i in range(parts):
        part = pl.ds(i * size, size)
        copies.append(pltpu.make_async_copy(block_hbm.at[part], block.at[part], block_sems.at[i]))
        copies[i].start()
    last = pltpu.make_async_copy(tiles_hbm, tiles, tiles_sem)
    last.start()
    first.wait()
    for copy in copies:
        copy.wait()
    for n, out in enumerate(outs):
        for h in range(out.shape[0]):
            out[h] = block[sends[plan[n], h]]
    last.wait()


def tiles_kernel(tiles, both_out):
    cells = tiles.shape[1]
    for k in range(tiles.shape[0]):
        high, low = split(tiles[k])
        both_out[k * cells : (k + 1) * cells, :cells] = high
        both_out[k * cells : (k + 1) * cells, cells:] = low


def lanes_product(a, b):
    return lax.dot_general(
        a.astype(BF16), b.astype(BF16), (((1,), (1,)), ((), ())), preferred_element_type=F32
    )


def order_kernel(side, sides, weights, columns, order, meta):
    count, slots = sides.shape[1], weights.shape[0]
    row = lax.broadcasted_iota(jnp.int32, (count, count), 0)
    col = lax.broadcasted_iota(jnp.int32, (count, count), 1)
    keep = jnp.broadcast_to((sides[...] == side[0]).astype(F32), (8, count))
    kept = lanes_product(keep, (col <= row).astype(F32))
    given = count - jnp.sum(keep, 1, keepdims=True)
    lane = lax.broadcasted_iota(jnp.int32, (8, count), 1).astype(F32)
    place = jnp.where(keep > 0.5, given + kept - 1.0, lane - kept)
    pick = (place[:1].astype(jnp.int32) == row).astype(F32)
    moved = lanes_product(lane, pick)
    order[...] = jnp.where(
        lax.broadcasted_iota(jnp.int32, (8, count), 0) == 0, moved, given
    ).astype(jnp.int32)
    values = weights[...]
    total = jnp.zeros((slots, count), F32)
    for _ in range(3):
        part = values.astype(BF16)
        total = total + lanes_product(part, pick)
        values = values - part.astype(F32)
    meta[:slots] = total
    meta[slots:] = lanes_product(columns[...].astype(F32), pick)


def fill(full, count, halos, plan, left):
    _, cols, cells = full.shape
    for n, halo in enumerate(halos):
        width = halo.shape[0]
        values = jnp.where(plan[len(halos) + n] != 0, halo[...], 0.0)
        if left is not None:
            values = apply_scaler(left, values.reshape(width * cols, cells))
            values = values.reshape(width, cols, cells)
        full[pl.ds(count + plan[n] * width, width)] = values


def gather(high, low, full, columns, weights, rows, count):
    _, cols, cells = full.shape
    for r, b in enumerate(rows):
        for k in range(high.shape[1] // cells):
            at = k * count + b
            upper, lower = split(full[columns[at]] * weights[at])
            place = slice(r * cols, (r + 1) * cols), slice(k * cells, (k + 1) * cells)
            high[place] = upper
            low[place] = lower


def multiply(high, low, tiles):
    cells = tiles.shape[1] // 2
    both = jnp.dot(high[...], tiles[...], preferred_element_type=F32)
    rest = jnp.dot(low[...], tiles[:, :cells], preferred_element_type=F32)
    return both[:, :cells] + (both[:, cells:] + rest)


def operator_kernel(plan, columns, weights, sends_hbm, block, h0, h1, h2, h3, tiles, *rest):
    image, sent, scratch = rest[0], rest[1:5], rest[5:]
    full, high0, low0, high1, low1, sends, sem = scratch
    copy = pltpu.make_async_copy(sends_hbm, sends, sem)
    copy.start()
    count, cols, cells = block.shape
    step = high0.shape[0] // cols

    def load(high, low, first):
        gather(high, low, full, columns, weights, [first + r for r in range(step)], count)

    def put(first, high, low):
        image[pl.ds(first, step)] = multiply(high, low, tiles).reshape(step, cols, cells)

    full[:count] = block[...]
    fill(full, count, (h0, h1, h2, h3), plan, None)
    load(high0, low0, 0)

    @pl.loop(0, count // (2 * step))
    def _(i):
        first = pl.multiple_of(i * 2 * step, 2 * step)
        load(high1, low1, first + step)
        put(first, high0, low0)
        load(high0, low0, jnp.minimum(first + 2 * step, count - step))
        put(first + step, high1, low1)

    copy.wait()
    for n, out in enumerate(sent):
        for h in range(out.shape[0]):
            out[h] = image[sends[plan[n], h]]


def last_first_kernel(plan, columns, weights, order, own, h0, h1, h2, h3, tiles, inv, meta, *rest):
    chunk, full, high, low = rest
    _, cols, cells = full.shape
    count = full.shape[0] - 4 * h0.shape[0]
    step = high.shape[0] // cols
    fill(full, count, (h0, h1, h2, h3), plan, scaler(inv[...]))
    gather(high, low, full, columns, weights, [order[r] for r in range(step)], count)
    chunk[:step] = multiply(high, low, tiles).reshape(step, cols, cells)
    chunk[step] = meta[...]


def last_rest_kernel(columns, weights, order, full, tiles, *rest):
    chunks, slots = rest[:-4], (rest[-4:-2], rest[-2:])
    _, cols, cells = full.shape
    step = slots[0][0].shape[0] // cols
    count = step + sum(chunk.shape[0] for chunk in chunks)
    parts = count // step - 1
    chunks = iter(chunks)

    def load(part):
        rows = [order[part * step + r] for r in range(step)]
        gather(*slots[part % 2], full, columns, weights, rows, count)

    load(1)
    for part in range(1, parts + 1):
        if part < parts:
            load(part + 1)
        value = multiply(*slots[part % 2], tiles).reshape(step, cols, cells)
        done = 0
        while done < step:
            chunk = next(chunks)
            chunk[...] = value[done : done + chunk.shape[0]]
            done += chunk.shape[0]


def row_sum(sums):
    total = sums[0]
    for d in range(1, sums.shape[0]):
        total = total + sums[d]
    return total


def put_rows(packed, row):
    for d in range(packed.shape[0]):
        packed[d] = row


def groups_of(ref):
    count, cols, _ = ref.shape
    per = 128 // cols
    return [ref[g * per : (g + 1) * per].reshape(128, 128) for g in range(count // per)]


def gram_kernel(image, packed):
    cols = image.shape[1]
    both = stacked(groups_of(image))
    put_rows(packed, pack(inner(both, both, cols), cols))


def scale_kernel(sums, image, out, inverse, packed):
    _, cols, cells = image.shape
    per = 128 // cols
    inv = eliminate(unpack(row_sum(sums), cols), identity(cols))
    inverse[...] = inv
    left = scaler(inv)
    groups = [apply_scaler(left, g) for g in groups_of(image)]
    for g, value in enumerate(groups):
        out[g * per : (g + 1) * per] = value.reshape(per, cols, cells)
    both = stacked(groups)
    put_rows(packed, pack(inner(both, both, cols), cols))


def sums_kernel(order, sums, full, first, *rest):
    later, (packed, inverse) = rest[:-2], rest[-2:]
    _, cols, cells = full.shape
    per = 128 // cols
    inv = eliminate(unpack(row_sum(sums), cols), identity(cols))
    inverse[...] = inv
    left = scaler(inv)
    count = first.shape[0] - 1 + sum(chunk.shape[0] for chunk in later)
    own = groups_of(first.at[: first.shape[0] - 1])
    for chunk in later:
        own = own + groups_of(chunk)
    previous = [
        jnp.concatenate([full[order[g * per + r]] for r in range(per)], 0)
        for g in range(count // per)
    ]
    now = stacked([apply_scaler(left, g) for g in own])
    before = stacked([apply_scaler(left, g) for g in previous])
    gram = pack(inner(now, now, cols), cols)
    cross = pack(inner(before, now, cols), cols)
    put_rows(packed, jnp.concatenate([gram, cross], 1))


def factor_kernel(order, sums, inverse, mine, theirs, total_inverse, rayleigh, weights, columns):
    cols = inverse.shape[0]
    slots, count = weights.shape
    wide = cols * cols
    total = row_sum(sums)
    total_inverse[...] = eliminate(unpack(total[:, :wide], cols), inverse[...])
    rayleigh[...] = unpack(total[:, wide:], cols)[:, :cols]
    last = mine.shape[0] - 1
    both = jnp.concatenate([mine[last], theirs[last]], 1)
    moved = pltpu.roll(both, 2 * count - order[count], 1)[:, :count]
    weights[...] = moved[:slots]
    columns[...] = moved[slots:].astype(jnp.int32)


def final_kernel(order, inverse, *rest):
    chunks, (out, rows, ready, sems) = rest[:-4], rest[-4:]
    mine, theirs = chunks[: len(chunks) // 2], chunks[len(chunks) // 2 :]
    count, cols, cells = out.shape
    size, per = mine[0].shape[0] - 1, 128 // cols
    for start, chunks in ((0, mine), (count, theirs)):
        for i, chunk in enumerate(chunks):
            stop = start + (chunk.shape[0] if i else size)
            rows[start:stop] = chunk[: stop - start]
            start = stop
    left = scaler(inverse[...])
    copies = []
    part_size = count // sems.shape[0]
    for i in range(sems.shape[0]):
        for g in range(i * part_size, (i + 1) * part_size, per):
            value = rows[pl.ds(order[count] + g, per)].reshape(128, cells)
            ready[g : g + per] = apply_scaler(left, value).reshape(per, cols, cells)
        part = pl.ds(i * part_size, part_size)
        copies.append(pltpu.make_async_copy(ready.at[part], out.at[part], sems.at[i]))
        copies[i].start()
    for copy in copies:
        copy.wait()


def call(kernel, out_shape, in_specs, out_specs, scratch=(), limit=24, cost=(0, 0), **more):
    return pl.pallas_call(
        kernel,
        out_shape=out_shape,
        in_specs=in_specs,
        out_specs=out_specs,
        scratch_shapes=list(scratch),
        compiler_params=pltpu.CompilerParams(vmem_limit_bytes=limit << 20),
        cost_estimate=pl.CostEstimate(flops=cost[0], transcendentals=0, bytes_accessed=cost[1]),
        **more,
    )


def pairs(x, axis, odd):
    sizes = [lax.axis_size(name) for name in AXES]
    along = AXES.index(axis)
    swap = []
    for here in range(sizes[0] * sizes[1]):
        place = list(divmod(here, sizes[1]))
        if not odd:
            place[along] ^= 1
        elif place[along] in (0, sizes[along] - 1):
            place[1 - along] ^= 1
        else:
            place[along] += 1 if place[along] % 2 else -1
        swap.append((here, place[0] * sizes[1] + place[1]))
    return lax.ppermute(x, AXES, swap)


def in_hbm(x):
    return pltpu.with_memory_space_constraint(x, pltpu.HBM)


def halo(sent):
    return [pairs(x, axis, odd) for x, (axis, odd) in zip(sent, EXCHANGES)]


def everywhere(rows):
    return lax.all_to_all(rows, AXES, 0, 0, tiled=True)


def shape(*dims, dtype=F32):
    return jax.ShapeDtypeStruct(dims, dtype)


def exchange_plan():
    numbers, counts = [], []
    for axis, odd in EXCHANGES:
        place = lax.axis_index(axis)
        upper = place % 2 if odd else 1 - place % 2
        inside = jnp.where(upper == 1, place < lax.axis_size(axis) - 1, place > 0)
        numbers.append(2 * AXES.index(axis) + upper)
        counts.append(inside.astype(jnp.int32))
    return jnp.stack(numbers + counts).astype(jnp.int32)


def per_device(start_block, slot_tiles, edge_weights, block_columns, halo_sends, split_side):
    block = start_block[0, 0]
    sends = halo_sends[0, 0]
    weights, columns = edge_weights[0, 0].T, block_columns[0, 0].T
    count, cols, cells = block.shape
    slots, width = slot_tiles.shape[0], sends.shape[1]
    size_x, size_y = lax.axis_size("gx"), lax.axis_size("gy")
    devices = size_x * size_y
    plan = exchange_plan()
    flat_weights = weights.reshape(slots * count)
    flat_columns = columns.reshape(slots * count)

    piece = shape(width, cols, cells)
    whole = shape(count, cols, cells)
    square = shape(cols, cells)
    block, slot_tiles, *sent = call(
        first_sends_kernel,
        [whole, shape(*slot_tiles.shape)] + [piece] * 4,
        [SMEM] + [HBM] * 3,
        [VMEM] * 6,
        [
            pltpu.SMEM(sends.shape, jnp.int32),
            pltpu.SemaphoreType.DMA,
            pltpu.SemaphoreType.DMA((1,)),
            pltpu.SemaphoreType.DMA,
        ],
    )(plan, in_hbm(sends), in_hbm(block), in_hbm(slot_tiles))
    near = halo(sent)

    wide = 2 * cells
    tiles = call(tiles_kernel, shape(slots * cells, wide, dtype=BF16), [VMEM], VMEM)(slot_tiles)
    my_side = (lax.axis_index("gy") >= size_y // 2).astype(jnp.int32)
    order, meta = call(
        order_kernel,
        [shape(8, count, dtype=jnp.int32), shape(2 * slots, count)],
        [SMEM] + [VMEM] * 3,
        [VMEM] * 2,
    )(my_side.reshape(1), split_side[0], weights, columns)
    order = order.reshape(8 * count)
    near, order, meta = lax.optimization_barrier((near, order, meta))

    size = count // CHUNKS
    blocks = shape(count + 4 * width, cols, cells)
    half = pltpu.VMEM((size * cols, slots * cells), BF16)
    work = 6 * count * cols * cells * cells * slots, 0
    small = 8 * count * cells * cells * cols, 0

    def operator(block, near):
        image, *sent = call(
            operator_kernel,
            [whole] + [piece] * 4,
            [SMEM] * 3 + [HBM] + [VMEM] * 6,
            [VMEM] * 5,
            [
                pltpu.VMEM(blocks.shape, F32),
                half,
                half,
                half,
                half,
                pltpu.SMEM(sends.shape, jnp.int32),
                pltpu.SemaphoreType.DMA,
            ],
            cost=work,
            input_output_aliases={4: 0},
        )(plan, flat_columns, flat_weights, in_hbm(sends), block, *near, tiles)
        return image, sent

    gram_rows = shape(devices, 1, cols * cols)
    image, sent = operator(block, near)
    near = halo(sent)
    packed = call(gram_kernel, gram_rows, [VMEM], VMEM, cost=small)(image)
    image, packed = lax.optimization_barrier((image, packed))
    sums = everywhere(packed)
    image, sent = operator(image, near)
    near = halo(sent)
    full, inverse, packed = call(
        scale_kernel, [blocks, square, gram_rows], [VMEM] * 2, [VMEM] * 3, cost=small
    )(sums, image)
    packed, *near = lax.optimization_barrier((packed, *near))
    sums = everywhere(packed)

    first, full = call(
        last_first_kernel,
        [shape(size + 1, cols, cells), blocks],
        [SMEM] * 4 + [VMEM] * 8,
        [VMEM] * 2,
        [half] * 2,
        cost=(work[0] // CHUNKS, 0),
        input_output_aliases={4: 1},
    )(plan, flat_columns, flat_weights, order, full, *near, tiles, inverse, meta)
    swap = [(j, j ^ (size_y // 2)) for j in range(size_y)]
    their_first = lax.ppermute(first, "gy", swap)
    later_sizes = [size] + [size // PIECES] * (PIECES * (CHUNKS - 2))
    later = call(
        last_rest_kernel,
        [shape(n, cols, cells) for n in later_sizes],
        [SMEM] * 3 + [VMEM] * 2,
        [VMEM] * len(later_sizes),
        [half] * 4,
        cost=(work[0] // CHUNKS * (CHUNKS - 1), 0),
    )(flat_columns, flat_weights, order, full, tiles)
    second, sums = lax.optimization_barrier((later[0], sums))
    their_second = lax.ppermute(second, "gy", swap)

    packed, inverse = call(
        sums_kernel,
        [shape(devices, 1, 2 * cols * cols), square],
        [SMEM] + [VMEM] * (3 + len(later)),
        [VMEM] * 2,
    )(order, sums, full, first, *later)
    packed, *last = lax.optimization_barrier((packed, *later[1:]))
    sums = everywhere(packed)
    their_later = [their_second] + [lax.ppermute(x, "gy", swap) for x in last]
    inverse, rayleigh, moved_weights, moved_columns = call(
        factor_kernel,
        [
            square,
            shape(cols, cols),
            shape(slots, count),
            shape(slots, count, dtype=jnp.int32),
        ],
        [SMEM] + [VMEM] * 4,
        [VMEM] * 4,
        cost=small,
    )(order, sums, inverse, first, their_first)
    moved_basis = call(
        final_kernel,
        whole,
        [SMEM] + [VMEM] * (3 + 2 * len(later)),
        ANY,
        [
            pltpu.VMEM((2 * count, cols, cells), F32),
            pltpu.VMEM((count, cols, cells), F32),
            pltpu.SemaphoreType.DMA((8,)),
        ],
    )(order, inverse, first, *later, their_first, *their_later)
    return (
        moved_basis[None, None],
        moved_weights.T[None, None],
        moved_columns.T[None, None],
        rayleigh,
    )


def solution(mesh):
    return jax.shard_map(
        per_device,
        mesh=mesh,
        in_specs=(
            P("gx", "gy", None, None, None),
            P(),
            P("gx", "gy", None, None),
            P("gx", "gy", None, None),
            P("gx", "gy", None, None),
            P("gx", "gy", None),
        ),
        out_specs=(
            P("gx", "gy", None, None, None),
            P("gx", "gy", None, None),
            P("gx", "gy", None, None),
            P(),
        ),
        check_vma=False,
    )
```

```python
import functools

import jax
import jax.numpy as jnp
from jax import lax
from jax.experimental import pallas as pl
from jax.experimental.pallas import tpu as pltpu
from jax.sharding import PartitionSpec as P

F32 = jnp.float32
BF16 = jnp.bfloat16
AXES = ("gx", "gy")
EXCHANGES = (("gy", 1), ("gx", 0), ("gx", 1), ("gy", 0))
CHUNKS = 4
SHARES = (2, 2, 1, 1)
AHEAD = 2
VMEM = pl.BlockSpec(memory_space=pltpu.VMEM)
SMEM = pl.BlockSpec(memory_space=pltpu.SMEM)
ANY = pl.BlockSpec(memory_space=pl.ANY)
HBM = pl.BlockSpec(memory_space=pltpu.HBM)


def split(x):
    high = x.astype(BF16)
    return high, (x - high.astype(F32)).astype(BF16)


def lane_group(rows, cols):
    return lax.broadcasted_iota(jnp.int32, (rows, 128), 1) // cols


def spread(x, cols):
    width = 64
    while width >= cols:
        x = x + pltpu.roll(x, width, 1)
        width //= 2
    return x


def unpack(packed, cols):
    half = 128 // cols
    sub = lax.broadcasted_iota(jnp.int32, (half, 128), 0)
    own = lane_group(half, cols) == sub
    parts = []
    for start in range(0, cols, half):
        row = packed[:, start * cols : start * cols + 128]
        parts.append(spread(jnp.where(own, jnp.broadcast_to(row, (half, 128)), 0.0), cols))
    return jnp.concatenate(parts, 0)


def pack(tiled, cols):
    half = 128 // cols
    sub = lax.broadcasted_iota(jnp.int32, (half, 128), 0)
    own = lane_group(half, cols) == sub
    rows = []
    for start in range(0, cols, half):
        part = jnp.where(own, tiled[start : start + half], 0.0)
        rows.append(jnp.sum(part, 0, keepdims=True))
    return jnp.concatenate(rows, 1)


def identity(cols):
    lane = lax.broadcasted_iota(jnp.int32, (cols, 128), 1) % cols
    return (lane == lax.broadcasted_iota(jnp.int32, (cols, 128), 0)).astype(F32)


def eliminate(gram, right):
    size = gram.shape[0]
    row = lax.broadcasted_iota(jnp.int32, (size, 128), 0)
    columns = [jnp.broadcast_to(gram[:, j : j + 1], (size, 128)) for j in range(size)]
    pivots = []
    for j in range(size):
        pivots.append(columns[j][j : j + 1])
        factor = jnp.where(row > j, columns[j], 0.0) * (1.0 / pivots[j])
        for k in range(j + 1, size):
            columns[k] = columns[k] - factor * columns[k][j : j + 1]
        right = right - factor * right[j : j + 1]
    return right * lax.rsqrt(jnp.concatenate(pivots, 0))


def scaler(small):
    cols = small.shape[0]
    group = lane_group(cols, cols)
    diag = jnp.concatenate(
        [jnp.where(group == g, small, 0.0) for g in range(128 // cols)], 0
    )
    high, low = split(diag)
    return jnp.concatenate(
        [jnp.concatenate([high, high], 1), jnp.concatenate([low, low], 1)], 0
    )


def apply_scaler(left, x):
    high, low = split(x)
    both = jnp.dot(left, jnp.concatenate([high, low], 0), preferred_element_type=F32)
    return both[:128] + both[128:]


def stacked(groups):
    pairs = [split(x) for x in groups]
    return jnp.concatenate(
        [
            jnp.concatenate([p[0] for p in pairs], 1),
            jnp.concatenate([p[1] for p in pairs], 1),
        ],
        0,
    )


def inner(a, b, cols):
    full = lax.dot_general(a, b, (((1,), (1,)), ((), ())), preferred_element_type=F32)
    half = full[:128] + full[128:]
    square = half[:, :128] + half[:, 128:]
    group = lane_group(cols, cols)
    total = jnp.zeros((cols, 128), F32)
    for g in range(128 // cols):
        total = total + jnp.where(group == g, square[g * cols : (g + 1) * cols], 0.0)
    return spread(total, cols)


def read_group(ref, g, per):
    x = ref[g * per : (g + 1) * per]
    return x.reshape(128, 128)


def first_sends_kernel(plan, sends_hbm, block_hbm, tiles_hbm, block, tiles, *rest):
    outs, (sends, sends_sem, block_sems, tiles_sem) = rest[:-4], rest[-4:]
    parts = block_sems.shape[0]
    size = block.shape[0] // parts
    first = pltpu.make_async_copy(sends_hbm, sends, sends_sem)
    first.start()
    copies = []
    for i in range(parts):
        part = pl.ds(i * size, size)
        copies.append(pltpu.make_async_copy(block_hbm.at[part], block.at[part], block_sems.at[i]))
        copies[i].start()
    last = pltpu.make_async_copy(tiles_hbm, tiles, tiles_sem)
    last.start()
    first.wait()
    for copy in copies:
        copy.wait()
    for n, out in enumerate(outs):
        for h in range(out.shape[0]):
            out[h] = block[sends[plan[n], h]]
    last.wait()


def tiles_kernel(tiles, both_out):
    cells = tiles.shape[1]
    for k in range(tiles.shape[0]):
        high, low = split(tiles[k])
        both_out[k * cells : (k + 1) * cells, :cells] = high
        both_out[k * cells : (k + 1) * cells, cells:] = low


def lanes_product(a, b):
    return lax.dot_general(
        a.astype(BF16), b.astype(BF16), (((1,), (1,)), ((), ())), preferred_element_type=F32
    )


def order_kernel(side, sides, weights, columns, order, meta):
    count, slots = sides.shape[1], weights.shape[0]
    row = lax.broadcasted_iota(jnp.int32, (count, count), 0)
    col = lax.broadcasted_iota(jnp.int32, (count, count), 1)
    keep = jnp.broadcast_to((sides[...] == side[0]).astype(F32), (8, count))
    kept = lanes_product(keep, (col <= row).astype(F32))
    given = count - jnp.sum(keep, 1, keepdims=True)
    lane = lax.broadcasted_iota(jnp.int32, (8, count), 1).astype(F32)
    place = jnp.where(keep > 0.5, given + kept - 1.0, lane - kept)
    pick = (place[:1].astype(jnp.int32) == row).astype(F32)
    moved = lanes_product(lane, pick)
    order[...] = jnp.where(
        lax.broadcasted_iota(jnp.int32, (8, count), 0) == 0, moved, given
    ).astype(jnp.int32)
    values = weights[...]
    total = jnp.zeros((slots, count), F32)
    for _ in range(3):
        part = values.astype(BF16)
        total = total + lanes_product(part, pick)
        values = values - part.astype(F32)
    meta[:slots] = total
    meta[slots:] = lanes_product(columns[...].astype(F32), pick)


def fill(full, count, halos, plan, left):
    _, cols, cells = full.shape
    for n, halo in enumerate(halos):
        width = halo.shape[0]
        values = jnp.where(plan[len(halos) + n] != 0, halo[...], 0.0)
        if left is not None:
            values = apply_scaler(left, values.reshape(width * cols, cells))
            values = values.reshape(width, cols, cells)
        full[pl.ds(count + plan[n] * width, width)] = values


def gather(high, low, full, columns, weights, rows, count):
    _, cols, cells = full.shape
    for r, b in enumerate(rows):
        for k in range(high.shape[1] // cells):
            at = k * count + b
            upper, lower = split(full[columns[at]] * weights[at])
            place = slice(r * cols, (r + 1) * cols), slice(k * cells, (k + 1) * cells)
            high[place] = upper
            low[place] = lower


def multiply(high, low, tiles):
    cells = tiles.shape[1] // 2
    both = jnp.dot(high[...], tiles[...], preferred_element_type=F32)
    rest = jnp.dot(low[...], tiles[:, :cells], preferred_element_type=F32)
    return both[:, :cells] + (both[:, cells:] + rest)


def operator_kernel(plan, columns, weights, sends_hbm, block, h0, h1, h2, h3, tiles, *rest):
    image, sent, scratch = rest[0], rest[1:5], rest[5:]
    full, high0, low0, high1, low1, sends, sem = scratch
    copy = pltpu.make_async_copy(sends_hbm, sends, sem)
    copy.start()
    count, cols, cells = block.shape
    step = high0.shape[0] // cols

    def load(high, low, first):
        gather(high, low, full, columns, weights, [first + r for r in range(step)], count)

    def put(first, high, low):
        image[pl.ds(first, step)] = multiply(high, low, tiles).reshape(step, cols, cells)

    full[:count] = block[...]
    fill(full, count, (h0, h1, h2, h3), plan, None)
    load(high0, low0, 0)

    @pl.loop(0, count // (2 * step))
    def _(i):
        first = pl.multiple_of(i * 2 * step, 2 * step)
        load(high1, low1, first + step)
        put(first, high0, low0)
        load(high0, low0, jnp.minimum(first + 2 * step, count - step))
        put(first + step, high1, low1)

    copy.wait()
    for n, out in enumerate(sent):
        for h in range(out.shape[0]):
            out[h] = image[sends[plan[n], h]]


def last_first_kernel(plan, columns, weights, order, own, h0, h1, h2, h3, tiles, inv, meta, *rest):
    chunk, full, high, low = rest
    _, cols, cells = full.shape
    count = full.shape[0] - 4 * h0.shape[0]
    step = high.shape[0] // cols
    fill(full, count, (h0, h1, h2, h3), plan, scaler(inv[...]))
    gather(high, low, full, columns, weights, [order[r] for r in range(step)], count)
    chunk[:step] = multiply(high, low, tiles).reshape(step, cols, cells)
    chunk[step] = meta[...]


def last_rest_kernel(columns, weights, order, full, tiles, *rest):
    chunks, slots = rest[:-4], (rest[-4:-2], rest[-2:])
    _, cols, cells = full.shape
    step = slots[0][0].shape[0] // cols
    count = step + sum(chunk.shape[0] for chunk in chunks)
    parts = count // step - 1

    def load(part):
        rows = [order[part * step + r] for r in range(step)]
        gather(*slots[part % 2], full, columns, weights, rows, count)

    load(1)
    for part in range(1, parts + 1):
        if part < parts:
            load(part + 1)
        value = multiply(*slots[part % 2], tiles).reshape(step, cols, cells)
        low, start = (part - 1) * step, 0
        for chunk in chunks:
            stop = start + chunk.shape[0]
            a, b = max(start, low), min(stop, low + step)
            if a < b:
                chunk[a - start : b - start] = value[a - low : b - low]
            start = stop


def row_sum(sums):
    total = sums[0]
    for d in range(1, sums.shape[0]):
        total = total + sums[d]
    return total


def put_rows(packed, row):
    for d in range(packed.shape[0]):
        packed[d] = row


def groups_of(ref):
    count, cols, _ = ref.shape
    per = 128 // cols
    return [ref[g * per : (g + 1) * per].reshape(128, 128) for g in range(count // per)]


def gram_kernel(image, packed):
    cols = image.shape[1]
    both = stacked(groups_of(image))
    put_rows(packed, pack(inner(both, both, cols), cols))


def scale_kernel(sums, image, out, inverse, packed):
    _, cols, cells = image.shape
    per = 128 // cols
    inv = eliminate(unpack(row_sum(sums), cols), identity(cols))
    inverse[...] = inv
    left = scaler(inv)
    groups = [apply_scaler(left, g) for g in groups_of(image)]
    for g, value in enumerate(groups):
        out[g * per : (g + 1) * per] = value.reshape(per, cols, cells)
    both = stacked(groups)
    put_rows(packed, pack(inner(both, both, cols), cols))


def sums_kernel(order, sums, full, first, *rest):
    later, (packed, inverse) = rest[:-2], rest[-2:]
    _, cols, cells = full.shape
    per = 128 // cols
    inv = eliminate(unpack(row_sum(sums), cols), identity(cols))
    inverse[...] = inv
    left = scaler(inv)
    count = first.shape[0] - 1 + sum(chunk.shape[0] for chunk in later)
    own = groups_of(first.at[: first.shape[0] - 1])
    for chunk in later:
        own = own + groups_of(chunk)
    previous = [
        jnp.concatenate([full[order[g * per + r]] for r in range(per)], 0)
        for g in range(count // per)
    ]
    now = stacked([apply_scaler(left, g) for g in own])
    before = stacked([apply_scaler(left, g) for g in previous])
    gram = pack(inner(now, now, cols), cols)
    cross = pack(inner(before, now, cols), cols)
    put_rows(packed, jnp.concatenate([gram, cross], 1))


def factor_kernel(order, sums, inverse, mine, theirs, total_inverse, rayleigh, weights, columns):
    cols = inverse.shape[0]
    slots, count = weights.shape
    wide = cols * cols
    total = row_sum(sums)
    total_inverse[...] = eliminate(unpack(total[:, :wide], cols), inverse[...])
    rayleigh[...] = unpack(total[:, wide:], cols)[:, :cols]
    last = mine.shape[0] - 1
    both = jnp.concatenate([mine[last], theirs[last]], 1)
    moved = pltpu.roll(both, 2 * count - order[count], 1)[:, :count]
    weights[...] = moved[:slots]
    columns[...] = moved[slots:].astype(jnp.int32)


def final_kernel(order, inverse, *rest):
    chunks, (out, rows, ready, sems) = rest[:-4], rest[-4:]
    mine, theirs = chunks[: len(chunks) // 2], chunks[len(chunks) // 2 :]
    count, cols, cells = out.shape
    size, per = mine[0].shape[0] - 1, 128 // cols
    for start, chunks in ((0, mine), (count, theirs)):
        for i, chunk in enumerate(chunks):
            stop = start + (chunk.shape[0] if i else size)
            rows[start:stop] = chunk[: stop - start]
            start = stop
    left = scaler(inverse[...])
    copies = []
    part_size = count // sems.shape[0]
    for i in range(sems.shape[0]):
        for g in range(i * part_size, (i + 1) * part_size, per):
            value = rows[pl.ds(order[count] + g, per)].reshape(128, cells)
            ready[g : g + per] = apply_scaler(left, value).reshape(per, cols, cells)
        part = pl.ds(i * part_size, part_size)
        copies.append(pltpu.make_async_copy(ready.at[part], out.at[part], sems.at[i]))
        copies[i].start()
    for copy in copies:
        copy.wait()


def call(kernel, out_shape, in_specs, out_specs, scratch=(), limit=24, cost=(0, 0), **more):
    return pl.pallas_call(
        kernel,
        out_shape=out_shape,
        in_specs=in_specs,
        out_specs=out_specs,
        scratch_shapes=list(scratch),
        compiler_params=pltpu.CompilerParams(vmem_limit_bytes=limit << 20),
        cost_estimate=pl.CostEstimate(flops=cost[0], transcendentals=0, bytes_accessed=cost[1]),
        **more,
    )


def pairs(x, axis, odd):
    sizes = [lax.axis_size(name) for name in AXES]
    along = AXES.index(axis)
    swap = []
    for here in range(sizes[0] * sizes[1]):
        place = list(divmod(here, sizes[1]))
        if not odd:
            place[along] ^= 1
        elif place[along] in (0, sizes[along] - 1):
            place[1 - along] ^= 1
        else:
            place[along] += 1 if place[along] % 2 else -1
        swap.append((here, place[0] * sizes[1] + place[1]))
    return lax.ppermute(x, AXES, swap)


def in_hbm(x):
    return pltpu.with_memory_space_constraint(x, pltpu.HBM)


def halo(sent):
    return [pairs(x, axis, odd) for x, (axis, odd) in zip(sent, EXCHANGES)]


def everywhere(rows):
    return lax.all_to_all(rows, AXES, 0, 0, tiled=True)


def shape(*dims, dtype=F32):
    return jax.ShapeDtypeStruct(dims, dtype)


def exchange_plan():
    numbers, counts = [], []
    for axis, odd in EXCHANGES:
        place = lax.axis_index(axis)
        upper = place % 2 if odd else 1 - place % 2
        inside = jnp.where(upper == 1, place < lax.axis_size(axis) - 1, place > 0)
        numbers.append(2 * AXES.index(axis) + upper)
        counts.append(inside.astype(jnp.int32))
    return jnp.stack(numbers + counts).astype(jnp.int32)


def per_device(start_block, slot_tiles, edge_weights, block_columns, halo_sends, split_side):
    block = start_block[0, 0]
    sends = halo_sends[0, 0]
    weights, columns = edge_weights[0, 0].T, block_columns[0, 0].T
    count, cols, cells = block.shape
    slots, width = slot_tiles.shape[0], sends.shape[1]
    size_x, size_y = lax.axis_size("gx"), lax.axis_size("gy")
    devices = size_x * size_y
    plan = exchange_plan()
    flat_weights = weights.reshape(slots * count)
    flat_columns = columns.reshape(slots * count)

    piece = shape(width, cols, cells)
    whole = shape(count, cols, cells)
    square = shape(cols, cells)
    block, slot_tiles, *sent = call(
        first_sends_kernel,
        [whole, shape(*slot_tiles.shape)] + [piece] * 4,
        [SMEM] + [HBM] * 3,
        [VMEM] * 6,
        [
            pltpu.SMEM(sends.shape, jnp.int32),
            pltpu.SemaphoreType.DMA,
            pltpu.SemaphoreType.DMA((1,)),
            pltpu.SemaphoreType.DMA,
        ],
    )(plan, in_hbm(sends), in_hbm(block), in_hbm(slot_tiles))
    near = halo(sent)

    wide = 2 * cells
    tiles = call(tiles_kernel, shape(slots * cells, wide, dtype=BF16), [VMEM], VMEM)(slot_tiles)
    my_side = (lax.axis_index("gy") >= size_y // 2).astype(jnp.int32)
    order, meta = call(
        order_kernel,
        [shape(8, count, dtype=jnp.int32), shape(2 * slots, count)],
        [SMEM] + [VMEM] * 3,
        [VMEM] * 2,
    )(my_side.reshape(1), split_side[0], weights, columns)
    order = order.reshape(8 * count)
    near, order, meta = lax.optimization_barrier((near, order, meta))

    size = count // CHUNKS
    blocks = shape(count + 4 * width, cols, cells)
    half = pltpu.VMEM((size * cols, slots * cells), BF16)
    work = 6 * count * cols * cells * cells * slots, 0
    small = 8 * count * cells * cells * cols, 0

    def operator(block, near):
        image, *sent = call(
            operator_kernel,
            [whole] + [piece] * 4,
            [SMEM] * 3 + [HBM] + [VMEM] * 6,
            [VMEM] * 5,
            [
                pltpu.VMEM(blocks.shape, F32),
                half,
                half,
                half,
                half,
                pltpu.SMEM(sends.shape, jnp.int32),
                pltpu.SemaphoreType.DMA,
            ],
            cost=work,
            input_output_aliases={4: 0},
        )(plan, flat_columns, flat_weights, in_hbm(sends), block, *near, tiles)
        return image, sent

    gram_rows = shape(devices, 1, cols * cols)
    image, sent = operator(block, near)
    near = halo(sent)
    packed = call(gram_kernel, gram_rows, [VMEM], VMEM, cost=small)(image)
    image, packed = lax.optimization_barrier((image, packed))
    sums = everywhere(packed)
    image, sent = operator(image, near)
    near = halo(sent)
    full, inverse, packed = call(
        scale_kernel, [blocks, square, gram_rows], [VMEM] * 2, [VMEM] * 3, cost=small
    )(sums, image)
    packed, *near = lax.optimization_barrier((packed, *near))
    sums = everywhere(packed)

    first, full = call(
        last_first_kernel,
        [shape(size + 1, cols, cells), blocks],
        [SMEM] * 4 + [VMEM] * 8,
        [VMEM] * 2,
        [half] * 2,
        cost=(work[0] // CHUNKS, 0),
        input_output_aliases={4: 1},
    )(plan, flat_columns, flat_weights, order, full, *near, tiles, inverse, meta)
    swap = [(j, j ^ (size_y // 2)) for j in range(size_y)]
    their_first = lax.ppermute(first, "gy", swap)
    later_sizes = [(count - size) * n // sum(SHARES) for n in SHARES]
    later = call(
        last_rest_kernel,
        [shape(n, cols, cells) for n in later_sizes],
        [SMEM] * 3 + [VMEM] * 2,
        [VMEM] * len(later_sizes),
        [half] * 4,
        cost=(work[0] // CHUNKS * (CHUNKS - 1), 0),
    )(flat_columns, flat_weights, order, full, tiles)
    *ahead, sums = lax.optimization_barrier((*later[:AHEAD], sums))
    their_later = [lax.ppermute(x, "gy", swap) for x in ahead]

    packed, inverse = call(
        sums_kernel,
        [shape(devices, 1, 2 * cols * cols), square],
        [SMEM] + [VMEM] * (3 + len(later)),
        [VMEM] * 2,
    )(order, sums, full, first, *later)
    packed, *last = lax.optimization_barrier((packed, *later[AHEAD:]))
    sums = everywhere(packed)
    their_later += [lax.ppermute(x, "gy", swap) for x in last]
    inverse, rayleigh, moved_weights, moved_columns = call(
        factor_kernel,
        [
            square,
            shape(cols, cols),
            shape(slots, count),
            shape(slots, count, dtype=jnp.int32),
        ],
        [SMEM] + [VMEM] * 4,
        [VMEM] * 4,
        cost=small,
    )(order, sums, inverse, first, their_first)
    moved_basis = call(
        final_kernel,
        whole,
        [SMEM] + [VMEM] * (3 + 2 * len(later)),
        ANY,
        [
            pltpu.VMEM((2 * count, cols, cells), F32),
            pltpu.VMEM((count, cols, cells), F32),
            pltpu.SemaphoreType.DMA((8,)),
        ],
    )(order, inverse, first, *later, their_first, *their_later)
    return (
        moved_basis[None, None],
        moved_weights.T[None, None],
        moved_columns.T[None, None],
        rayleigh,
    )


def solution(mesh):
    return jax.shard_map(
        per_device,
        mesh=mesh,
        in_specs=(
            P("gx", "gy", None, None, None),
            P(),
            P("gx", "gy", None, None),
            P("gx", "gy", None, None),
            P("gx", "gy", None, None),
            P("gx", "gy", None),
        ),
        out_specs=(
            P("gx", "gy", None, None, None),
            P("gx", "gy", None, None),
            P("gx", "gy", None, None),
            P(),
        ),
        check_vma=False,
    )
```

```python
import functools

import jax
import jax.numpy as jnp
from jax import lax
from jax.experimental import pallas as pl
from jax.experimental.pallas import tpu as pltpu
from jax.sharding import PartitionSpec as P

F32 = jnp.float32
BF16 = jnp.bfloat16
AXES = ("gx", "gy")
EXCHANGES = (("gy", 1), ("gx", 0), ("gx", 1), ("gy", 0))
CHUNKS = 4
FIRST = 2
SHARES = (3, 3, 2)
AHEAD = 2
VMEM = pl.BlockSpec(memory_space=pltpu.VMEM)
SMEM = pl.BlockSpec(memory_space=pltpu.SMEM)
ANY = pl.BlockSpec(memory_space=pl.ANY)
HBM = pl.BlockSpec(memory_space=pltpu.HBM)


def split(x):
    high = x.astype(BF16)
    return high, (x - high.astype(F32)).astype(BF16)


def lane_group(rows, cols):
    return lax.broadcasted_iota(jnp.int32, (rows, 128), 1) // cols


def spread(x, cols):
    width = 64
    while width >= cols:
        x = x + pltpu.roll(x, width, 1)
        width //= 2
    return x


def unpack(packed, cols):
    half = 128 // cols
    sub = lax.broadcasted_iota(jnp.int32, (half, 128), 0)
    own = lane_group(half, cols) == sub
    parts = []
    for start in range(0, cols, half):
        row = packed[:, start * cols : start * cols + 128]
        parts.append(spread(jnp.where(own, jnp.broadcast_to(row, (half, 128)), 0.0), cols))
    return jnp.concatenate(parts, 0)


def pack(tiled, cols):
    half = 128 // cols
    sub = lax.broadcasted_iota(jnp.int32, (half, 128), 0)
    own = lane_group(half, cols) == sub
    rows = []
    for start in range(0, cols, half):
        part = jnp.where(own, tiled[start : start + half], 0.0)
        rows.append(jnp.sum(part, 0, keepdims=True))
    return jnp.concatenate(rows, 1)


def identity(cols):
    lane = lax.broadcasted_iota(jnp.int32, (cols, 128), 1) % cols
    return (lane == lax.broadcasted_iota(jnp.int32, (cols, 128), 0)).astype(F32)


def eliminate(gram, right):
    size = gram.shape[0]
    row = lax.broadcasted_iota(jnp.int32, (size, 128), 0)
    columns = [jnp.broadcast_to(gram[:, j : j + 1], (size, 128)) for j in range(size)]
    pivots = []
    for j in range(size):
        pivots.append(columns[j][j : j + 1])
        factor = jnp.where(row > j, columns[j], 0.0) * (1.0 / pivots[j])
        for k in range(j + 1, size):
            columns[k] = columns[k] - factor * columns[k][j : j + 1]
        right = right - factor * right[j : j + 1]
    return right * lax.rsqrt(jnp.concatenate(pivots, 0))


def scaler(small):
    cols = small.shape[0]
    group = lane_group(cols, cols)
    diag = jnp.concatenate(
        [jnp.where(group == g, small, 0.0) for g in range(128 // cols)], 0
    )
    high, low = split(diag)
    return jnp.concatenate(
        [jnp.concatenate([high, high], 1), jnp.concatenate([low, low], 1)], 0
    )


def apply_scaler(left, x):
    high, low = split(x)
    both = jnp.dot(left, jnp.concatenate([high, low], 0), preferred_element_type=F32)
    return both[:128] + both[128:]


def stacked(groups):
    pairs = [split(x) for x in groups]
    return jnp.concatenate(
        [
            jnp.concatenate([p[0] for p in pairs], 1),
            jnp.concatenate([p[1] for p in pairs], 1),
        ],
        0,
    )


def inner(a, b, cols):
    full = lax.dot_general(a, b, (((1,), (1,)), ((), ())), preferred_element_type=F32)
    half = full[:128] + full[128:]
    square = half[:, :128] + half[:, 128:]
    group = lane_group(cols, cols)
    total = jnp.zeros((cols, 128), F32)
    for g in range(128 // cols):
        total = total + jnp.where(group == g, square[g * cols : (g + 1) * cols], 0.0)
    return spread(total, cols)


def read_group(ref, g, per):
    x = ref[g * per : (g + 1) * per]
    return x.reshape(128, 128)


def first_sends_kernel(plan, sends_hbm, block_hbm, tiles_hbm, block, tiles, *rest):
    outs, (sends, sends_sem, block_sems, tiles_sem) = rest[:-4], rest[-4:]
    parts = block_sems.shape[0]
    size = block.shape[0] // parts
    first = pltpu.make_async_copy(sends_hbm, sends, sends_sem)
    first.start()
    copies = []
    for i in range(parts):
        part = pl.ds(i * size, size)
        copies.append(pltpu.make_async_copy(block_hbm.at[part], block.at[part], block_sems.at[i]))
        copies[i].start()
    last = pltpu.make_async_copy(tiles_hbm, tiles, tiles_sem)
    last.start()
    first.wait()
    for copy in copies:
        copy.wait()
    for n, out in enumerate(outs):
        for h in range(out.shape[0]):
            out[h] = block[sends[plan[n], h]]
    last.wait()


def tiles_kernel(tiles, both_out):
    cells = tiles.shape[1]
    for k in range(tiles.shape[0]):
        high, low = split(tiles[k])
        both_out[k * cells : (k + 1) * cells, :cells] = high
        both_out[k * cells : (k + 1) * cells, cells:] = low


def lanes_product(a, b):
    return lax.dot_general(
        a.astype(BF16), b.astype(BF16), (((1,), (1,)), ((), ())), preferred_element_type=F32
    )


def order_kernel(side, sides, weights, columns, order, meta):
    count, slots = sides.shape[1], weights.shape[0]
    row = lax.broadcasted_iota(jnp.int32, (count, count), 0)
    col = lax.broadcasted_iota(jnp.int32, (count, count), 1)
    keep = jnp.broadcast_to((sides[...] == side[0]).astype(F32), (8, count))
    kept = lanes_product(keep, (col <= row).astype(F32))
    given = count - jnp.sum(keep, 1, keepdims=True)
    lane = lax.broadcasted_iota(jnp.int32, (8, count), 1).astype(F32)
    place = jnp.where(keep > 0.5, given + kept - 1.0, lane - kept)
    pick = (place[:1].astype(jnp.int32) == row).astype(F32)
    moved = lanes_product(lane, pick)
    order[...] = jnp.where(
        lax.broadcasted_iota(jnp.int32, (8, count), 0) == 0, moved, given
    ).astype(jnp.int32)
    values = weights[...]
    total = jnp.zeros((slots, count), F32)
    for _ in range(3):
        part = values.astype(BF16)
        total = total + lanes_product(part, pick)
        values = values - part.astype(F32)
    meta[:slots] = total
    meta[slots:] = lanes_product(columns[...].astype(F32), pick)


def fill(full, count, halos, plan, left):
    _, cols, cells = full.shape
    for n, halo in enumerate(halos):
        width = halo.shape[0]
        values = jnp.where(plan[len(halos) + n] != 0, halo[...], 0.0)
        if left is not None:
            values = apply_scaler(left, values.reshape(width * cols, cells))
            values = values.reshape(width, cols, cells)
        full[pl.ds(count + plan[n] * width, width)] = values


def gather(high, low, full, columns, weights, rows, count):
    _, cols, cells = full.shape
    for r, b in enumerate(rows):
        for k in range(high.shape[1] // cells):
            at = k * count + b
            upper, lower = split(full[columns[at]] * weights[at])
            place = slice(r * cols, (r + 1) * cols), slice(k * cells, (k + 1) * cells)
            high[place] = upper
            low[place] = lower


def multiply(high, low, tiles):
    cells = tiles.shape[1] // 2
    both = jnp.dot(high[...], tiles[...], preferred_element_type=F32)
    rest = jnp.dot(low[...], tiles[:, :cells], preferred_element_type=F32)
    return both[:, :cells] + (both[:, cells:] + rest)


def operator_kernel(plan, columns, weights, sends_hbm, block, h0, h1, h2, h3, tiles, *rest):
    image, sent, scratch = rest[0], rest[1:5], rest[5:]
    full, high0, low0, high1, low1, sends, sem = scratch
    copy = pltpu.make_async_copy(sends_hbm, sends, sem)
    copy.start()
    count, cols, cells = block.shape
    step = high0.shape[0] // cols

    def load(high, low, first):
        gather(high, low, full, columns, weights, [first + r for r in range(step)], count)

    def put(first, high, low):
        image[pl.ds(first, step)] = multiply(high, low, tiles).reshape(step, cols, cells)

    full[:count] = block[...]
    fill(full, count, (h0, h1, h2, h3), plan, None)
    load(high0, low0, 0)

    @pl.loop(0, count // (2 * step))
    def _(i):
        first = pl.multiple_of(i * 2 * step, 2 * step)
        load(high1, low1, first + step)
        put(first, high0, low0)
        load(high0, low0, jnp.minimum(first + 2 * step, count - step))
        put(first + step, high1, low1)

    copy.wait()
    for n, out in enumerate(sent):
        for h in range(out.shape[0]):
            out[h] = image[sends[plan[n], h]]


def last_first_kernel(plan, columns, weights, order, own, h0, h1, h2, h3, tiles, inv, meta, *rest):
    chunk, full, slots = rest[0], rest[1], (rest[2:4], rest[4:6])
    _, cols, cells = full.shape
    count = full.shape[0] - 4 * h0.shape[0]
    step = slots[0][0].shape[0] // cols
    parts = chunk.shape[0] // step

    def load(part):
        rows = [order[part * step + r] for r in range(step)]
        gather(*slots[part % 2], full, columns, weights, rows, count)

    fill(full, count, (h0, h1, h2, h3), plan, scaler(inv[...]))
    load(0)
    for part in range(parts):
        if part + 1 < parts:
            load(part + 1)
        value = multiply(*slots[part % 2], tiles).reshape(step, cols, cells)
        chunk[part * step : (part + 1) * step] = value
    chunk[parts * step] = meta[...]


def last_rest_kernel(columns, weights, order, full, tiles, *rest):
    chunks, slots = rest[:-4], (rest[-4:-2], rest[-2:])
    _, cols, cells = full.shape
    step = slots[0][0].shape[0] // cols
    count = columns.shape[0] * cells // tiles.shape[0]
    begin = (count - sum(chunk.shape[0] for chunk in chunks)) // step
    parts = count // step

    def load(part):
        rows = [order[part * step + r] for r in range(step)]
        gather(*slots[part % 2], full, columns, weights, rows, count)

    load(begin)
    for part in range(begin, parts):
        if part + 1 < parts:
            load(part + 1)
        value = multiply(*slots[part % 2], tiles).reshape(step, cols, cells)
        low, start = (part - begin) * step, 0
        for chunk in chunks:
            stop = start + chunk.shape[0]
            a, b = max(start, low), min(stop, low + step)
            if a < b:
                chunk[a - start : b - start] = value[a - low : b - low]
            start = stop


def row_sum(sums):
    total = sums[0]
    for d in range(1, sums.shape[0]):
        total = total + sums[d]
    return total


def put_rows(packed, row):
    for d in range(packed.shape[0]):
        packed[d] = row


def groups_of(ref):
    count, cols, _ = ref.shape
    per = 128 // cols
    return [ref[g * per : (g + 1) * per].reshape(128, 128) for g in range(count // per)]


def gram_kernel(image, packed):
    cols = image.shape[1]
    both = stacked(groups_of(image))
    put_rows(packed, pack(inner(both, both, cols), cols))


def scale_kernel(sums, image, out, inverse, packed):
    _, cols, cells = image.shape
    per = 128 // cols
    inv = eliminate(unpack(row_sum(sums), cols), identity(cols))
    inverse[...] = inv
    left = scaler(inv)
    groups = [apply_scaler(left, g) for g in groups_of(image)]
    for g, value in enumerate(groups):
        out[g * per : (g + 1) * per] = value.reshape(per, cols, cells)
    both = stacked(groups)
    put_rows(packed, pack(inner(both, both, cols), cols))


def sums_kernel(order, sums, full, first, *rest):
    later, (packed, inverse) = rest[:-2], rest[-2:]
    _, cols, cells = full.shape
    per = 128 // cols
    inv = eliminate(unpack(row_sum(sums), cols), identity(cols))
    inverse[...] = inv
    left = scaler(inv)
    count = first.shape[0] - 1 + sum(chunk.shape[0] for chunk in later)
    own = groups_of(first.at[: first.shape[0] - 1])
    for chunk in later:
        own = own + groups_of(chunk)
    previous = [
        jnp.concatenate([full[order[g * per + r]] for r in range(per)], 0)
        for g in range(count // per)
    ]
    now = stacked([apply_scaler(left, g) for g in own])
    before = stacked([apply_scaler(left, g) for g in previous])
    gram = pack(inner(now, now, cols), cols)
    cross = pack(inner(before, now, cols), cols)
    put_rows(packed, jnp.concatenate([gram, cross], 1))


def factor_kernel(order, sums, inverse, mine, theirs, total_inverse, rayleigh, weights, columns):
    cols = inverse.shape[0]
    slots, count = weights.shape
    wide = cols * cols
    total = row_sum(sums)
    total_inverse[...] = eliminate(unpack(total[:, :wide], cols), inverse[...])
    rayleigh[...] = unpack(total[:, wide:], cols)[:, :cols]
    last = mine.shape[0] - 1
    both = jnp.concatenate([mine[last], theirs[last]], 1)
    moved = pltpu.roll(both, 2 * count - order[count], 1)[:, :count]
    weights[...] = moved[:slots]
    columns[...] = moved[slots:].astype(jnp.int32)


def final_kernel(order, inverse, *rest):
    chunks, (out, rows, ready, sems) = rest[:-4], rest[-4:]
    mine, theirs = chunks[: len(chunks) // 2], chunks[len(chunks) // 2 :]
    count, cols, cells = out.shape
    size, per = mine[0].shape[0] - 1, 128 // cols
    for start, chunks in ((0, mine), (count, theirs)):
        for i, chunk in enumerate(chunks):
            stop = start + (chunk.shape[0] if i else size)
            rows[start:stop] = chunk[: stop - start]
            start = stop
    left = scaler(inverse[...])
    copies = []
    part_size = count // sems.shape[0]
    for i in range(sems.shape[0]):
        for g in range(i * part_size, (i + 1) * part_size, per):
            value = rows[pl.ds(order[count] + g, per)].reshape(128, cells)
            ready[g : g + per] = apply_scaler(left, value).reshape(per, cols, cells)
        part = pl.ds(i * part_size, part_size)
        copies.append(pltpu.make_async_copy(ready.at[part], out.at[part], sems.at[i]))
        copies[i].start()
    for copy in copies:
        copy.wait()


def call(kernel, out_shape, in_specs, out_specs, scratch=(), limit=24, cost=(0, 0), **more):
    return pl.pallas_call(
        kernel,
        out_shape=out_shape,
        in_specs=in_specs,
        out_specs=out_specs,
        scratch_shapes=list(scratch),
        compiler_params=pltpu.CompilerParams(vmem_limit_bytes=limit << 20),
        cost_estimate=pl.CostEstimate(flops=cost[0], transcendentals=0, bytes_accessed=cost[1]),
        **more,
    )


def pairs(x, axis, odd):
    sizes = [lax.axis_size(name) for name in AXES]
    along = AXES.index(axis)
    swap = []
    for here in range(sizes[0] * sizes[1]):
        place = list(divmod(here, sizes[1]))
        if not odd:
            place[along] ^= 1
        elif place[along] in (0, sizes[along] - 1):
            place[1 - along] ^= 1
        else:
            place[along] += 1 if place[along] % 2 else -1
        swap.append((here, place[0] * sizes[1] + place[1]))
    return lax.ppermute(x, AXES, swap)


def in_hbm(x):
    return pltpu.with_memory_space_constraint(x, pltpu.HBM)


def halo(sent):
    return [pairs(x, axis, odd) for x, (axis, odd) in zip(sent, EXCHANGES)]


def everywhere(rows):
    return lax.all_to_all(rows, AXES, 0, 0, tiled=True)


def shape(*dims, dtype=F32):
    return jax.ShapeDtypeStruct(dims, dtype)


def exchange_plan():
    numbers, counts = [], []
    for axis, odd in EXCHANGES:
        place = lax.axis_index(axis)
        upper = place % 2 if odd else 1 - place % 2
        inside = jnp.where(upper == 1, place < lax.axis_size(axis) - 1, place > 0)
        numbers.append(2 * AXES.index(axis) + upper)
        counts.append(inside.astype(jnp.int32))
    return jnp.stack(numbers + counts).astype(jnp.int32)


def per_device(start_block, slot_tiles, edge_weights, block_columns, halo_sends, split_side):
    block = start_block[0, 0]
    sends = halo_sends[0, 0]
    weights, columns = edge_weights[0, 0].T, block_columns[0, 0].T
    count, cols, cells = block.shape
    slots, width = slot_tiles.shape[0], sends.shape[1]
    size_x, size_y = lax.axis_size("gx"), lax.axis_size("gy")
    devices = size_x * size_y
    plan = exchange_plan()
    flat_weights = weights.reshape(slots * count)
    flat_columns = columns.reshape(slots * count)

    piece = shape(width, cols, cells)
    whole = shape(count, cols, cells)
    square = shape(cols, cells)
    block, slot_tiles, *sent = call(
        first_sends_kernel,
        [whole, shape(*slot_tiles.shape)] + [piece] * 4,
        [SMEM] + [HBM] * 3,
        [VMEM] * 6,
        [
            pltpu.SMEM(sends.shape, jnp.int32),
            pltpu.SemaphoreType.DMA,
            pltpu.SemaphoreType.DMA((1,)),
            pltpu.SemaphoreType.DMA,
        ],
    )(plan, in_hbm(sends), in_hbm(block), in_hbm(slot_tiles))
    near = halo(sent)

    wide = 2 * cells
    tiles = call(tiles_kernel, shape(slots * cells, wide, dtype=BF16), [VMEM], VMEM)(slot_tiles)
    my_side = (lax.axis_index("gy") >= size_y // 2).astype(jnp.int32)
    order, meta = call(
        order_kernel,
        [shape(8, count, dtype=jnp.int32), shape(2 * slots, count)],
        [SMEM] + [VMEM] * 3,
        [VMEM] * 2,
    )(my_side.reshape(1), split_side[0], weights, columns)
    order = order.reshape(8 * count)
    near, order, meta = lax.optimization_barrier((near, order, meta))

    size = count // CHUNKS
    blocks = shape(count + 4 * width, cols, cells)
    half = pltpu.VMEM((size * cols, slots * cells), BF16)
    work = 6 * count * cols * cells * cells * slots, 0
    small = 8 * count * cells * cells * cols, 0

    def operator(block, near):
        image, *sent = call(
            operator_kernel,
            [whole] + [piece] * 4,
            [SMEM] * 3 + [HBM] + [VMEM] * 6,
            [VMEM] * 5,
            [
                pltpu.VMEM(blocks.shape, F32),
                half,
                half,
                half,
                half,
                pltpu.SMEM(sends.shape, jnp.int32),
                pltpu.SemaphoreType.DMA,
            ],
            cost=work,
            input_output_aliases={4: 0},
        )(plan, flat_columns, flat_weights, in_hbm(sends), block, *near, tiles)
        return image, sent

    gram_rows = shape(devices, 1, cols * cols)
    image, sent = operator(block, near)
    near = halo(sent)
    packed = call(gram_kernel, gram_rows, [VMEM], VMEM, cost=small)(image)
    image, packed = lax.optimization_barrier((image, packed))
    sums = everywhere(packed)
    image, sent = operator(image, near)
    near = halo(sent)
    full, inverse, packed = call(
        scale_kernel, [blocks, square, gram_rows], [VMEM] * 2, [VMEM] * 3, cost=small
    )(sums, image)
    packed, *near = lax.optimization_barrier((packed, *near))
    sums = everywhere(packed)

    first, full = call(
        last_first_kernel,
        [shape(FIRST * size + 1, cols, cells), blocks],
        [SMEM] * 4 + [VMEM] * 8,
        [VMEM] * 2,
        [half] * 4,
        cost=(work[0] // CHUNKS * FIRST, 0),
        input_output_aliases={4: 1},
    )(plan, flat_columns, flat_weights, order, full, *near, tiles, inverse, meta)
    swap = [(j, j ^ (size_y // 2)) for j in range(size_y)]
    their_first = lax.ppermute(first, "gy", swap)
    later_sizes = [(count - FIRST * size) * n // sum(SHARES) for n in SHARES]
    later = call(
        last_rest_kernel,
        [shape(n, cols, cells) for n in later_sizes],
        [SMEM] * 3 + [VMEM] * 2,
        [VMEM] * len(later_sizes),
        [half] * 4,
        cost=(work[0] // CHUNKS * (CHUNKS - FIRST), 0),
    )(flat_columns, flat_weights, order, full, tiles)
    their_later = [lax.ppermute(x, "gy", swap) for x in later[:AHEAD]]

    packed, inverse = call(
        sums_kernel,
        [shape(devices, 1, 2 * cols * cols), square],
        [SMEM] + [VMEM] * (3 + len(later)),
        [VMEM] * 2,
    )(order, sums, full, first, *later)
    packed, *last = lax.optimization_barrier((packed, *later[AHEAD:]))
    sums = everywhere(packed)
    their_later += [lax.ppermute(x, "gy", swap) for x in last]
    inverse, rayleigh, moved_weights, moved_columns = call(
        factor_kernel,
        [
            square,
            shape(cols, cols),
            shape(slots, count),
            shape(slots, count, dtype=jnp.int32),
        ],
        [SMEM] + [VMEM] * 4,
        [VMEM] * 4,
        cost=small,
    )(order, sums, inverse, first, their_first)
    moved_basis = call(
        final_kernel,
        whole,
        [SMEM] + [VMEM] * (3 + 2 * len(later)),
        ANY,
        [
            pltpu.VMEM((2 * count, cols, cells), F32),
            pltpu.VMEM((count, cols, cells), F32),
            pltpu.SemaphoreType.DMA((8,)),
        ],
    )(order, inverse, first, *later, their_first, *their_later)
    return (
        moved_basis[None, None],
        moved_weights.T[None, None],
        moved_columns.T[None, None],
        rayleigh,
    )


def solution(mesh):
    return jax.shard_map(
        per_device,
        mesh=mesh,
        in_specs=(
            P("gx", "gy", None, None, None),
            P(),
            P("gx", "gy", None, None),
            P("gx", "gy", None, None),
            P("gx", "gy", None, None),
            P("gx", "gy", None),
        ),
        out_specs=(
            P("gx", "gy", None, None, None),
            P("gx", "gy", None, None),
            P("gx", "gy", None, None),
            P(),
        ),
        check_vma=False,
    )
```

```python
import functools

import jax
import jax.numpy as jnp
from jax import lax
from jax.experimental import pallas as pl
from jax.experimental.pallas import tpu as pltpu
from jax.sharding import PartitionSpec as P

F32 = jnp.float32
BF16 = jnp.bfloat16
AXES = ("gx", "gy")
EXCHANGES = (("gy", 1), ("gx", 0), ("gx", 1), ("gy", 0))
CHUNKS = 4
SHARES = (2, 2, 1, 1)
AHEAD = 2
VMEM = pl.BlockSpec(memory_space=pltpu.VMEM)
SMEM = pl.BlockSpec(memory_space=pltpu.SMEM)
ANY = pl.BlockSpec(memory_space=pl.ANY)
HBM = pl.BlockSpec(memory_space=pltpu.HBM)


def split(x):
    high = x.astype(BF16)
    return high, (x - high.astype(F32)).astype(BF16)


def lane_group(rows, cols):
    return lax.broadcasted_iota(jnp.int32, (rows, 128), 1) // cols


def spread(x, cols):
    width = 64
    while width >= cols:
        x = x + pltpu.roll(x, width, 1)
        width //= 2
    return x


def unpack(packed, cols):
    half = 128 // cols
    sub = lax.broadcasted_iota(jnp.int32, (half, 128), 0)
    own = lane_group(half, cols) == sub
    parts = []
    for start in range(0, cols, half):
        row = packed[:, start * cols : start * cols + 128]
        parts.append(spread(jnp.where(own, jnp.broadcast_to(row, (half, 128)), 0.0), cols))
    return jnp.concatenate(parts, 0)


def pack(tiled, cols):
    half = 128 // cols
    sub = lax.broadcasted_iota(jnp.int32, (half, 128), 0)
    own = lane_group(half, cols) == sub
    rows = []
    for start in range(0, cols, half):
        part = jnp.where(own, tiled[start : start + half], 0.0)
        rows.append(jnp.sum(part, 0, keepdims=True))
    return jnp.concatenate(rows, 1)


def identity(cols):
    lane = lax.broadcasted_iota(jnp.int32, (cols, 128), 1) % cols
    return (lane == lax.broadcasted_iota(jnp.int32, (cols, 128), 0)).astype(F32)


def eliminate(gram, right):
    size = gram.shape[0]
    row = lax.broadcasted_iota(jnp.int32, (size, 128), 0)
    columns = [jnp.broadcast_to(gram[:, j : j + 1], (size, 128)) for j in range(size)]
    pivots = []
    for j in range(size):
        pivots.append(columns[j][j : j + 1])
        factor = jnp.where(row > j, columns[j], 0.0) * (1.0 / pivots[j])
        for k in range(j + 1, size):
            columns[k] = columns[k] - factor * columns[k][j : j + 1]
        right = right - factor * right[j : j + 1]
    return right * lax.rsqrt(jnp.concatenate(pivots, 0))


def scaler(small):
    cols = small.shape[0]
    group = lane_group(cols, cols)
    diag = jnp.concatenate(
        [jnp.where(group == g, small, 0.0) for g in range(128 // cols)], 0
    )
    high, low = split(diag)
    return jnp.concatenate(
        [jnp.concatenate([high, high], 1), jnp.concatenate([low, low], 1)], 0
    )


def apply_scaler(left, x):
    high, low = split(x)
    both = jnp.dot(left, jnp.concatenate([high, low], 0), preferred_element_type=F32)
    return both[:128] + both[128:]


def stacked(groups):
    pairs = [split(x) for x in groups]
    return jnp.concatenate(
        [
            jnp.concatenate([p[0] for p in pairs], 1),
            jnp.concatenate([p[1] for p in pairs], 1),
        ],
        0,
    )


def inner(a, b, cols):
    full = lax.dot_general(a, b, (((1,), (1,)), ((), ())), preferred_element_type=F32)
    half = full[:128] + full[128:]
    square = half[:, :128] + half[:, 128:]
    group = lane_group(cols, cols)
    total = jnp.zeros((cols, 128), F32)
    for g in range(128 // cols):
        total = total + jnp.where(group == g, square[g * cols : (g + 1) * cols], 0.0)
    return spread(total, cols)


def read_group(ref, g, per):
    x = ref[g * per : (g + 1) * per]
    return x.reshape(128, 128)


def first_sends_kernel(plan, sends_hbm, block_hbm, tiles_hbm, block, tiles, *rest):
    outs, (sends, sends_sem, block_sems, tiles_sem) = rest[:-4], rest[-4:]
    parts = block_sems.shape[0]
    size = block.shape[0] // parts
    first = pltpu.make_async_copy(sends_hbm, sends, sends_sem)
    first.start()
    copies = []
    for i in range(parts):
        part = pl.ds(i * size, size)
        copies.append(pltpu.make_async_copy(block_hbm.at[part], block.at[part], block_sems.at[i]))
        copies[i].start()
    last = pltpu.make_async_copy(tiles_hbm, tiles, tiles_sem)
    last.start()
    first.wait()
    for copy in copies:
        copy.wait()
    for n, out in enumerate(outs):
        for h in range(out.shape[0]):
            out[h] = block[sends[plan[n], h]]
    last.wait()


def tiles_kernel(tiles, both_out):
    cells = tiles.shape[1]
    for k in range(tiles.shape[0]):
        high, low = split(tiles[k])
        both_out[k * cells : (k + 1) * cells, :cells] = high
        both_out[k * cells : (k + 1) * cells, cells:] = low


def lanes_product(a, b):
    return lax.dot_general(
        a.astype(BF16), b.astype(BF16), (((1,), (1,)), ((), ())), preferred_element_type=F32
    )


def order_kernel(side, sides, weights, columns, order, meta):
    count, slots = sides.shape[1], weights.shape[0]
    row = lax.broadcasted_iota(jnp.int32, (count, count), 0)
    col = lax.broadcasted_iota(jnp.int32, (count, count), 1)
    keep = jnp.broadcast_to((sides[...] == side[0]).astype(F32), (8, count))
    kept = lanes_product(keep, (col <= row).astype(F32))
    given = count - jnp.sum(keep, 1, keepdims=True)
    lane = lax.broadcasted_iota(jnp.int32, (8, count), 1).astype(F32)
    place = jnp.where(keep > 0.5, given + kept - 1.0, lane - kept)
    pick = (place[:1].astype(jnp.int32) == row).astype(F32)
    moved = lanes_product(lane, pick)
    order[...] = jnp.where(
        lax.broadcasted_iota(jnp.int32, (8, count), 0) == 0, moved, given
    ).astype(jnp.int32)
    values = weights[...]
    total = jnp.zeros((slots, count), F32)
    for _ in range(3):
        part = values.astype(BF16)
        total = total + lanes_product(part, pick)
        values = values - part.astype(F32)
    meta[:slots] = total
    meta[slots:] = lanes_product(columns[...].astype(F32), pick)


def fill(full, count, halos, plan, left):
    _, cols, cells = full.shape
    for n, halo in enumerate(halos):
        width = halo.shape[0]
        values = jnp.where(plan[len(halos) + n] != 0, halo[...], 0.0)
        if left is not None:
            values = apply_scaler(left, values.reshape(width * cols, cells))
            values = values.reshape(width, cols, cells)
        full[pl.ds(count + plan[n] * width, width)] = values


def gather(high, low, full, columns, weights, rows, count):
    _, cols, cells = full.shape
    for r, b in enumerate(rows):
        for k in range(high.shape[1] // cells):
            at = k * count + b
            upper, lower = split(full[columns[at]] * weights[at])
            place = slice(r * cols, (r + 1) * cols), slice(k * cells, (k + 1) * cells)
            high[place] = upper
            low[place] = lower


def multiply(high, low, tiles):
    cells = tiles.shape[1] // 2
    both = jnp.dot(high[...], tiles[...], preferred_element_type=F32)
    rest = jnp.dot(low[...], tiles[:, :cells], preferred_element_type=F32)
    return both[:, :cells] + (both[:, cells:] + rest)


def operator_kernel(plan, columns, weights, sends_hbm, block, h0, h1, h2, h3, tiles, *rest):
    image, sent, scratch = rest[0], rest[1:5], rest[5:]
    full, high0, low0, high1, low1, sends, sem = scratch
    copy = pltpu.make_async_copy(sends_hbm, sends, sem)
    copy.start()
    count, cols, cells = block.shape
    step = high0.shape[0] // cols

    def load(high, low, first):
        gather(high, low, full, columns, weights, [first + r for r in range(step)], count)

    def put(first, high, low):
        image[pl.ds(first, step)] = multiply(high, low, tiles).reshape(step, cols, cells)

    full[:count] = block[...]
    fill(full, count, (h0, h1, h2, h3), plan, None)
    load(high0, low0, 0)

    @pl.loop(0, count // (2 * step))
    def _(i):
        first = pl.multiple_of(i * 2 * step, 2 * step)
        load(high1, low1, first + step)
        put(first, high0, low0)
        load(high0, low0, jnp.minimum(first + 2 * step, count - step))
        put(first + step, high1, low1)

    copy.wait()
    for n, out in enumerate(sent):
        for h in range(out.shape[0]):
            out[h] = image[sends[plan[n], h]]


def last_first_kernel(plan, columns, weights, order, own, h0, h1, h2, h3, tiles, inv, meta, *rest):
    chunk, full, high, low = rest
    _, cols, cells = full.shape
    count = full.shape[0] - 4 * h0.shape[0]
    step = high.shape[0] // cols
    fill(full, count, (h0, h1, h2, h3), plan, scaler(inv[...]))
    gather(high, low, full, columns, weights, [order[r] for r in range(step)], count)
    chunk[:step] = multiply(high, low, tiles).reshape(step, cols, cells)
    chunk[step] = meta[...]


def last_rest_kernel(columns, weights, order, full, tiles, *rest):
    chunks, slots = rest[:-4], (rest[-4:-2], rest[-2:])
    _, cols, cells = full.shape
    step = slots[0][0].shape[0] // cols
    count = step + sum(chunk.shape[0] for chunk in chunks)
    parts = count // step - 1

    def load(part):
        rows = [order[part * step + r] for r in range(step)]
        gather(*slots[part % 2], full, columns, weights, rows, count)

    load(1)
    for part in range(1, parts + 1):
        if part < parts:
            load(part + 1)
        value = multiply(*slots[part % 2], tiles).reshape(step, cols, cells)
        low, start = (part - 1) * step, 0
        for chunk in chunks:
            stop = start + chunk.shape[0]
            a, b = max(start, low), min(stop, low + step)
            if a < b:
                chunk[a - start : b - start] = value[a - low : b - low]
            start = stop


def row_sum(sums):
    total = sums[0]
    for d in range(1, sums.shape[0]):
        total = total + sums[d]
    return total


def put_rows(packed, row):
    for d in range(packed.shape[0]):
        packed[d] = row


def groups_of(ref):
    count, cols, _ = ref.shape
    per = 128 // cols
    return [ref[g * per : (g + 1) * per].reshape(128, 128) for g in range(count // per)]


def gram_kernel(image, packed):
    cols = image.shape[1]
    both = stacked(groups_of(image))
    put_rows(packed, pack(inner(both, both, cols), cols))


def scale_kernel(sums, image, out, inverse, packed):
    _, cols, cells = image.shape
    per = 128 // cols
    inv = eliminate(unpack(row_sum(sums), cols), identity(cols))
    inverse[...] = inv
    left = scaler(inv)
    groups = [apply_scaler(left, g) for g in groups_of(image)]
    for g, value in enumerate(groups):
        out[g * per : (g + 1) * per] = value.reshape(per, cols, cells)
    both = stacked(groups)
    put_rows(packed, pack(inner(both, both, cols), cols))


def sums_kernel(order, sums, full, first, *rest):
    later, (packed, inverse) = rest[:-2], rest[-2:]
    _, cols, cells = full.shape
    per = 128 // cols
    inv = eliminate(unpack(row_sum(sums), cols), identity(cols))
    inverse[...] = inv
    left = scaler(inv)
    count = first.shape[0] - 1 + sum(chunk.shape[0] for chunk in later)
    own = groups_of(first.at[: first.shape[0] - 1])
    for chunk in later:
        own = own + groups_of(chunk)
    previous = [
        jnp.concatenate([full[order[g * per + r]] for r in range(per)], 0)
        for g in range(count // per)
    ]
    now = stacked([apply_scaler(left, g) for g in own])
    before = stacked([apply_scaler(left, g) for g in previous])
    gram = pack(inner(now, now, cols), cols)
    cross = pack(inner(before, now, cols), cols)
    put_rows(packed, jnp.concatenate([gram, cross], 1))


def factor_kernel(order, sums, inverse, mine, theirs, total_inverse, rayleigh, weights, columns):
    cols = inverse.shape[0]
    slots, count = weights.shape
    wide = cols * cols
    total = row_sum(sums)
    total_inverse[...] = eliminate(unpack(total[:, :wide], cols), inverse[...])
    rayleigh[...] = unpack(total[:, wide:], cols)[:, :cols]
    last = mine.shape[0] - 1
    both = jnp.concatenate([mine[last], theirs[last]], 1)
    moved = pltpu.roll(both, lax.rem(2 * count - order[count], 2 * count), 1)[:, :count]
    weights[...] = moved[:slots]
    columns[...] = moved[slots:].astype(jnp.int32)


def final_kernel(order, inverse, *rest):
    chunks, (out, rows, ready, sems) = rest[:-4], rest[-4:]
    mine, theirs = chunks[: len(chunks) // 2], chunks[len(chunks) // 2 :]
    count, cols, cells = out.shape
    size, per = mine[0].shape[0] - 1, 128 // cols
    for start, chunks in ((0, mine), (count, theirs)):
        for i, chunk in enumerate(chunks):
            stop = start + (chunk.shape[0] if i else size)
            rows[start:stop] = chunk[: stop - start]
            start = stop
    left = scaler(inverse[...])
    copies = []
    part_size = count // sems.shape[0]
    for i in range(sems.shape[0]):
        for g in range(i * part_size, (i + 1) * part_size, per):
            value = rows[pl.ds(order[count] + g, per)].reshape(128, cells)
            ready[g : g + per] = apply_scaler(left, value).reshape(per, cols, cells)
        part = pl.ds(i * part_size, part_size)
        copies.append(pltpu.make_async_copy(ready.at[part], out.at[part], sems.at[i]))
        copies[i].start()
    for copy in copies:
        copy.wait()


def call(kernel, out_shape, in_specs, out_specs, scratch=(), limit=24, cost=(0, 0), **more):
    return pl.pallas_call(
        kernel,
        out_shape=out_shape,
        in_specs=in_specs,
        out_specs=out_specs,
        scratch_shapes=list(scratch),
        compiler_params=pltpu.CompilerParams(vmem_limit_bytes=limit << 20),
        cost_estimate=pl.CostEstimate(flops=cost[0], transcendentals=0, bytes_accessed=cost[1]),
        **more,
    )


def pairs(x, axis, odd):
    sizes = [lax.axis_size(name) for name in AXES]
    along = AXES.index(axis)
    swap = []
    for here in range(sizes[0] * sizes[1]):
        place = list(divmod(here, sizes[1]))
        if not odd:
            place[along] ^= 1
        elif place[along] in (0, sizes[along] - 1):
            place[1 - along] ^= 1
        else:
            place[along] += 1 if place[along] % 2 else -1
        swap.append((here, place[0] * sizes[1] + place[1]))
    return lax.ppermute(x, AXES, swap)


def in_hbm(x):
    return pltpu.with_memory_space_constraint(x, pltpu.HBM)


def halo(sent):
    return [pairs(x, axis, odd) for x, (axis, odd) in zip(sent, EXCHANGES)]


def everywhere(rows):
    return lax.all_to_all(rows, AXES, 0, 0, tiled=True)


def shape(*dims, dtype=F32):
    return jax.ShapeDtypeStruct(dims, dtype)


def exchange_plan():
    numbers, counts = [], []
    for axis, odd in EXCHANGES:
        place = lax.axis_index(axis)
        upper = place % 2 if odd else 1 - place % 2
        inside = jnp.where(upper == 1, place < lax.axis_size(axis) - 1, place > 0)
        numbers.append(2 * AXES.index(axis) + upper)
        counts.append(inside.astype(jnp.int32))
    return jnp.stack(numbers + counts).astype(jnp.int32)


def per_device(start_block, slot_tiles, edge_weights, block_columns, halo_sends, split_side):
    block = start_block[0, 0]
    sends = halo_sends[0, 0]
    weights, columns = edge_weights[0, 0].T, block_columns[0, 0].T
    count, cols, cells = block.shape
    slots, width = slot_tiles.shape[0], sends.shape[1]
    size_x, size_y = lax.axis_size("gx"), lax.axis_size("gy")
    devices = size_x * size_y
    plan = exchange_plan()
    flat_weights = weights.reshape(slots * count)
    flat_columns = columns.reshape(slots * count)

    piece = shape(width, cols, cells)
    whole = shape(count, cols, cells)
    square = shape(cols, cells)
    block, slot_tiles, *sent = call(
        first_sends_kernel,
        [whole, shape(*slot_tiles.shape)] + [piece] * 4,
        [SMEM] + [HBM] * 3,
        [VMEM] * 6,
        [
            pltpu.SMEM(sends.shape, jnp.int32),
            pltpu.SemaphoreType.DMA,
            pltpu.SemaphoreType.DMA((1,)),
            pltpu.SemaphoreType.DMA,
        ],
    )(plan, in_hbm(sends), in_hbm(block), in_hbm(slot_tiles))
    near = halo(sent)

    wide = 2 * cells
    tiles = call(tiles_kernel, shape(slots * cells, wide, dtype=BF16), [VMEM], VMEM)(slot_tiles)
    my_side = (lax.axis_index("gy") >= size_y // 2).astype(jnp.int32)
    order, meta = call(
        order_kernel,
        [shape(8, count, dtype=jnp.int32), shape(2 * slots, count)],
        [SMEM] + [VMEM] * 3,
        [VMEM] * 2,
    )(my_side.reshape(1), split_side[0], weights, columns)
    order = order.reshape(8 * count)
    near, order, meta = lax.optimization_barrier((near, order, meta))

    size = count // CHUNKS
    blocks = shape(count + 4 * width, cols, cells)
    half = pltpu.VMEM((size * cols, slots * cells), BF16)
    work = 6 * count * cols * cells * cells * slots, 0
    small = 8 * count * cells * cells * cols, 0

    def operator(block, near):
        image, *sent = call(
            operator_kernel,
            [whole] + [piece] * 4,
            [SMEM] * 3 + [HBM] + [VMEM] * 6,
            [VMEM] * 5,
            [
                pltpu.VMEM(blocks.shape, F32),
                half,
                half,
                half,
                half,
                pltpu.SMEM(sends.shape, jnp.int32),
                pltpu.SemaphoreType.DMA,
            ],
            cost=work,
            input_output_aliases={4: 0},
        )(plan, flat_columns, flat_weights, in_hbm(sends), block, *near, tiles)
        return image, sent

    gram_rows = shape(devices, 1, cols * cols)
    image, sent = operator(block, near)
    near = halo(sent)
    packed = call(gram_kernel, gram_rows, [VMEM], VMEM, cost=small)(image)
    image, packed = lax.optimization_barrier((image, packed))
    sums = everywhere(packed)
    image, sent = operator(image, near)
    near = halo(sent)
    full, inverse, packed = call(
        scale_kernel, [blocks, square, gram_rows], [VMEM] * 2, [VMEM] * 3, cost=small
    )(sums, image)
    packed, *near = lax.optimization_barrier((packed, *near))
    sums = everywhere(packed)

    first, full = call(
        last_first_kernel,
        [shape(size + 1, cols, cells), blocks],
        [SMEM] * 4 + [VMEM] * 8,
        [VMEM] * 2,
        [half] * 2,
        cost=(work[0] // CHUNKS, 0),
        input_output_aliases={4: 1},
    )(plan, flat_columns, flat_weights, order, full, *near, tiles, inverse, meta)
    swap = [(j, j ^ (size_y // 2)) for j in range(size_y)]
    their_first = lax.ppermute(first, "gy", swap)
    later_sizes = [(count - size) * n // sum(SHARES) for n in SHARES]
    later = call(
        last_rest_kernel,
        [shape(n, cols, cells) for n in later_sizes],
        [SMEM] * 3 + [VMEM] * 2,
        [VMEM] * len(later_sizes),
        [half] * 4,
        cost=(work[0] // CHUNKS * (CHUNKS - 1), 0),
    )(flat_columns, flat_weights, order, full, tiles)
    *ahead, sums = lax.optimization_barrier((*later[:AHEAD], sums))
    their_later = [lax.ppermute(x, "gy", swap) for x in ahead]

    packed, inverse = call(
        sums_kernel,
        [shape(devices, 1, 2 * cols * cols), square],
        [SMEM] + [VMEM] * (3 + len(later)),
        [VMEM] * 2,
    )(order, sums, full, first, *later)
    packed, *last = lax.optimization_barrier((packed, *later[AHEAD:]))
    sums = everywhere(packed)
    their_later += [lax.ppermute(x, "gy", swap) for x in last]
    inverse, rayleigh, moved_weights, moved_columns = call(
        factor_kernel,
        [
            square,
            shape(cols, cols),
            shape(slots, count),
            shape(slots, count, dtype=jnp.int32),
        ],
        [SMEM] + [VMEM] * 4,
        [VMEM] * 4,
        cost=small,
    )(order, sums, inverse, first, their_first)
    moved_basis = call(
        final_kernel,
        whole,
        [SMEM] + [VMEM] * (3 + 2 * len(later)),
        ANY,
        [
            pltpu.VMEM((2 * count, cols, cells), F32),
            pltpu.VMEM((count, cols, cells), F32),
            pltpu.SemaphoreType.DMA((8,)),
        ],
    )(order, inverse, first, *later, their_first, *their_later)
    return (
        moved_basis[None, None],
        moved_weights.T[None, None],
        moved_columns.T[None, None],
        rayleigh,
    )


def solution(mesh):
    return jax.shard_map(
        per_device,
        mesh=mesh,
        in_specs=(
            P("gx", "gy", None, None, None),
            P(),
            P("gx", "gy", None, None),
            P("gx", "gy", None, None),
            P("gx", "gy", None, None),
            P("gx", "gy", None),
        ),
        out_specs=(
            P("gx", "gy", None, None, None),
            P("gx", "gy", None, None),
            P("gx", "gy", None, None),
            P(),
        ),
        check_vma=False,
    )
```
